128 devices in a mesh: ctx: 32 (over x, y, core), head: 4 (over z).
Axes of the slice: x: 4, y: 4, z: 4, core: 2. Of those that a mesh axis runs over, the one named last changes fastest.
Arguments:
- query: bfloat16 [16384, 2048], P('ctx', 'head'), may hold values from -6 to 6
- key: bfloat16 [16384, 2048], P('ctx', 'head'), may hold values from -6 to 6
- value: bfloat16 [16384, 2048], P('ctx', 'head'), may hold values from -6 to 6
- out_grad: bfloat16 [16384, 2048], P('ctx', 'head'), may hold values from -6 to 6
- links: int32 [128, 6], replicated, may hold values from -1 to 125, as said below
Outputs:
- query_grad: bfloat16 [16384, 2048], P('ctx', 'head')
- key_grad: bfloat16 [16384, 2048], P('ctx', 'head')
- value_grad: bfloat16 [16384, 2048], P('ctx', 'head')
The draws below stay inside these ranges and needn't reach their ends.
Inputs may be any that keep to these rules, and one draw needn't show every extreme that they name: `links`: entry (b, s) is -1 or the index of a block at most b - 2. Over the 6 entries of all query blocks held by one index of ctx, at most 2 name blocks held by any one index of ctx (itself included), and on every index of ctx some index is named exactly 2 times.
All inputs are finite; a program needn't handle non-finite values.
Results may differ from the reference program's by a relative error of at most 0.01.
Values may be sent and summed in bfloat16 or wider, within the bound.
A program may use at most 192 MiB of HBM per device.

```python
import jax
import jax.numpy as jnp
from jax import lax

HEADS = 16
HEAD_DIM = 128
BLK = 128
WIN = 2
LINKS = 6
TOK_DEV = 512
SHARDS = 32
SEQ = 16384
NBLK = 128
STRETCH_BLOCKS = 2
WIDTH = 2048
LINK_CAP = 2
N_CTX = 32


def storage_order(natural):
    half_rows = TOK_DEV // 2
    width = natural.shape[-1]
    first = natural[:SHARDS * half_rows].reshape(SHARDS, half_rows, width)
    second = natural[SHARDS * half_rows:].reshape(SHARDS, half_rows, width)[::-1]
    return jnp.stack((first, second), 1).reshape(-1, width)


def drawn_pair(key, part):
    base_query = jnp.clip(jax.random.normal(jax.random.fold_in(key, 11), (SEQ, WIDTH), jnp.float32), -6.0, 6.0)
    base_key = jnp.clip(jax.random.normal(jax.random.fold_in(key, 12), (SEQ, WIDTH), jnp.float32), -6.0, 6.0)
    return (storage_order(base_query).astype(jnp.bfloat16), storage_order(base_key).astype(jnp.bfloat16))


def draw_query(key, part):
    return drawn_pair(key, part)[0]


def draw_key(key, part):
    return drawn_pair(key, part)[1]


def draw_links(key, part):
    shards = SHARDS
    stretch_blocks = STRETCH_BLOCKS
    capacity = LINK_CAP
    entries = 2 * stretch_blocks * LINKS
    devices = jnp.arange(shards, dtype=jnp.int32)
    local_ids = jnp.arange(2 * stretch_blocks, dtype=jnp.int32)
    query_stretch = jnp.where(local_ids[None, :] < stretch_blocks, devices[:, None], 2 * shards - 1 - devices[:, None])
    query_block = query_stretch * stretch_blocks + local_ids[None, :] % stretch_blocks
    entry_block = jnp.repeat(query_block, LINKS, axis=1)
    entry_local = jnp.repeat(local_ids, LINKS)
    ordinal = jnp.arange(entries, dtype=jnp.int32)
    order_score = jax.random.randint(jax.random.fold_in(key, 21), (shards, entries), 0, 1 << 16) * entries + ordinal[None, :]
    order_score = order_score + jnp.where(entry_local[None, :] < stretch_blocks, entries << 16, 0)
    ordering = jnp.argsort(order_score, axis=1)
    position = jnp.argsort(ordering, axis=1).astype(jnp.int32)
    owner_score = jax.random.randint(jax.random.fold_in(key, 22), (shards, shards), 0, 1 << 16) * shards + devices[None, :]
    owner_perm = jnp.argsort(owner_score, axis=1).astype(jnp.int32)
    owner_dev = jnp.take_along_axis(owner_perm, position // capacity, axis=1)
    cand_stretch = jnp.where(local_ids[None, None, :] < stretch_blocks, owner_dev[:, :, None], 2 * shards - 1 - owner_dev[:, :, None])
    candidate = cand_stretch * stretch_blocks + local_ids[None, None, :] % stretch_blocks
    allowed = candidate <= entry_block[:, :, None] - WIN
    pick_score = jax.random.randint(jax.random.fold_in(key, 23), (shards, entries, 2 * stretch_blocks), 0, 1 << 16) * (2 * stretch_blocks) + local_ids[None, None, :]
    pick_score = jnp.where(allowed, pick_score, 1 << 30)
    picked = jnp.argmin(pick_score, axis=2).astype(jnp.int32)
    chosen = jnp.take_along_axis(candidate, picked[:, :, None], axis=2)[:, :, 0]
    named_block = jnp.where(jnp.any(allowed, axis=2), chosen, -1).astype(jnp.int32)
    table = named_block.reshape(shards, 2 * stretch_blocks, LINKS)
    first = table[:, :stretch_blocks].reshape(shards * stretch_blocks, LINKS)
    second = table[::-1, stretch_blocks:].reshape(shards * stretch_blocks, LINKS)
    return jnp.concatenate((first, second), 0).astype(jnp.int32)


def block_levels(key, shape, cuts, least, top_value):
    def one(dim, blocks):
        steps = jax.random.uniform(jax.random.fold_in(jax.random.fold_in(key, 6), dim), (blocks,), jnp.float32, least / len(cuts), top_value / len(cuts))
        return jnp.repeat(jnp.exp(steps), shape[dim] // blocks).reshape((-1,) + (1,) * (len(shape) - dim - 1))

    factor_of = one(*cuts[0])
    for cut in cuts[1:]:
        factor_of = factor_of * one(*cut)
    return factor_of


def centred(stream_key, extent, spread, bound, cuts=(), kind=jnp.bfloat16):
    values = jax.random.normal(stream_key, extent, jnp.float32) * spread
    if len(cuts) > 0:
        values = block_levels(stream_key, extent, cuts, -0.22, 0.18) * values
    return jnp.clip(values, min=-bound, max=bound).astype(kind)


def setup_inputs(seed: int = 0) -> dict:
    streams_of = jax.random.split(jax.random.key(seed), 6)
    query = draw_query(jax.random.fold_in(streams_of[5], 71), 0)
    key = draw_key(jax.random.fold_in(streams_of[5], 71), 0)
    value = centred(streams_of[2], (SEQ, WIDTH), 1.0, 6.0, ((0, 32), (1, 4)))
    out_grad = centred(streams_of[3], (SEQ, WIDTH), 1.0, 6.0, ((0, 32), (1, 4)))
    links = draw_links(jax.random.fold_in(streams_of[5], 71), 0)
    return dict(query=query, key=key, value=value, out_grad=out_grad, links=links)


NEG_FILL = -1.0e30


def to_natural(stored):
    half_rows = TOK_DEV // 2
    width = stored.shape[-1]
    parts = stored.reshape(N_CTX, 2, half_rows, width)
    return jnp.concatenate((parts[:, 0].reshape(-1, width), parts[::-1, 1].reshape(-1, width)), 0)


def to_storage(natural):
    half_rows = TOK_DEV // 2
    width = natural.shape[-1]
    first = natural[: N_CTX * half_rows].reshape(N_CTX, half_rows, width)
    second = natural[N_CTX * half_rows:].reshape(N_CTX, half_rows, width)[::-1]
    return jnp.stack((first, second), 1).reshape(-1, width)


def rounded(values):
    return lax.optimization_barrier(values.astype(jnp.bfloat16)).astype(jnp.float32)


def reference(query, key, value, out_grad, links):
    scaling = HEAD_DIM ** -0.5
    span = WIN + LINKS

    def blocked(stored):
        return to_natural(stored).reshape(NBLK, BLK, HEADS, HEAD_DIM)

    q_all = blocked(query)
    k_all = blocked(key)
    v_all = blocked(value)
    o_all = blocked(out_grad)
    offsets = jnp.arange(WIN, dtype=jnp.int32)
    positions = jnp.arange(BLK, dtype=jnp.int32)
    causal = positions[:, None] >= positions[None, :]
    first_only = (jnp.arange(span, dtype=jnp.int32) == 0)[:, None, None]
    inner = jnp.where(first_only, causal[None], True)
    is_link = (jnp.arange(span, dtype=jnp.int32) >= WIN)[:, None, None, None]

    def step(carry, block):
        key_acc, value_acc = carry
        listed = jnp.concatenate((block - offsets, links[block].astype(jnp.int32))).astype(jnp.int32)
        usable = listed >= 0
        safe = jnp.maximum(listed, 0).astype(jnp.int32)
        keys = k_all[safe].astype(jnp.float32)
        values = v_all[safe].astype(jnp.float32)
        q_blk = q_all[block].astype(jnp.float32)
        o_blk = o_all[block].astype(jnp.float32)
        live = (usable[:, None, None] & inner).transpose(1, 0, 2)[None]
        score = jnp.einsum("qhd,skhd->hqsk", q_blk, keys) * scaling
        score = jnp.where(live, score, NEG_FILL)
        top = jnp.max(score, axis=(2, 3), keepdims=True)
        prob = jnp.where(live, jnp.exp(score - top), 0.0)
        prob = prob / jnp.sum(prob, axis=(2, 3), keepdims=True)
        dprob = jnp.einsum("qhd,skhd->hqsk", o_blk, values)
        delta = jnp.sum(prob * dprob, axis=(2, 3), keepdims=True)
        dscore = prob * (dprob - delta)
        prob_b = rounded(prob)
        dscore_b = rounded(dscore)
        dq_window = jnp.einsum("hqsk,skhd->qhd", dscore_b[:, :, :WIN], keys[:WIN]) * scaling
        dq_link = rounded(jnp.einsum("hqsk,skhd->sqhd", dscore_b[:, :, WIN:], keys[WIN:]) * scaling)
        dq_block = dq_window + jnp.sum(dq_link, axis=0)
        dk_terms = jnp.einsum("hqsk,qhd->skhd", dscore_b, q_blk) * scaling
        dv_terms = jnp.einsum("hqsk,qhd->skhd", prob_b, o_blk)
        dk_terms = jnp.where(is_link, rounded(dk_terms), dk_terms)
        dv_terms = jnp.where(is_link, rounded(dv_terms), dv_terms)
        return (key_acc.at[safe].add(dk_terms), value_acc.at[safe].add(dv_terms)), dq_block.astype(jnp.bfloat16)

    zeros_acc = jnp.zeros((NBLK, BLK, HEADS, HEAD_DIM), jnp.float32)
    (key_acc, value_acc), dq_all = lax.scan(step, (zeros_acc, zeros_acc), jnp.arange(NBLK, dtype=jnp.int32))
    rows_all = NBLK * BLK
    query_grad = to_storage(dq_all.reshape(rows_all, HEADS * HEAD_DIM))
    key_grad = to_storage(key_acc.reshape(rows_all, HEADS * HEAD_DIM)).astype(jnp.bfloat16)
    value_grad = to_storage(value_acc.reshape(rows_all, HEADS * HEAD_DIM)).astype(jnp.bfloat16)
    return query_grad, key_grad, value_grad
```

```python
import functools

import jax
import jax.numpy as jnp
from jax import lax
from jax.experimental import pallas as pl
from jax.experimental.pallas import tpu as pltpu
from jax.sharding import PartitionSpec as P

HEAD_DIM = 128
BLK = 128
LINKS = 6
SPAN = 8
HEADS_HERE = 4
NX = 4
NY = 4
NG = 8
LOCAL = 4
ROWS = 512
COLS = 512
LAST = 63
NEG = -1e30
SCALE = HEAD_DIM**-0.5
MESH = pl.DeviceIdType.MESH
BF16 = jnp.bfloat16
F32 = jnp.float32
VMEM = pltpu.VMEM
MIB = 1 << 20


def whole(space):
    return pl.BlockSpec(memory_space=space)


def place():
    me = lax.axis_index("ctx")
    return me // 8, (me // 2) % 4, me % 2, lax.axis_index("head")


def barrier_with(partners):
    sem = pltpu.get_barrier_semaphore()
    for partner in partners:
        pl.semaphore_signal(sem, inc=1, device_id=partner, device_id_type=MESH)
    pl.semaphore_wait(sem, len(partners))


class Copies:
    def __init__(self, send_sem, recv_sem):
        self.send_sem, self.recv_sem, self.made = send_sem, recv_sem, []

    def start(self, src, dst, device):
        n = len(self.made)
        copy = pltpu.make_async_remote_copy(
            src_ref=src,
            dst_ref=dst,
            send_sem=self.send_sem.at[n],
            recv_sem=self.recv_sem.at[n],
            device_id=device,
            device_id_type=MESH,
        )
        copy.start()
        self.made.append(copy)
        return copy

    def finish_sends(self):
        for copy in self.made:
            copy.wait_send()


N_GATHER = 20


def gather_kernel(q_ref, o_ref, k_ref, v_ref, qg_ref, kg_ref, send_sem, recv_sem, own_sem):
    x, y, c, h = place()
    g = y * 2 + c
    own = [
        pltpu.make_async_copy(q_ref, qg_ref.at[g, 0], own_sem.at[0]),
        pltpu.make_async_copy(o_ref, qg_ref.at[g, 1], own_sem.at[1]),
        pltpu.make_async_copy(k_ref, kg_ref.at[x, 0], own_sem.at[2]),
        pltpu.make_async_copy(v_ref, kg_ref.at[x, 1], own_sem.at[3]),
    ]
    for copy in own:
        copy.start()

    def dev(xx, yy, cc):
        return ((xx * NY + yy) * 2 + cc, h)

    x_up, x_down, x_far = (x + 1) % NX, (x + NX - 1) % NX, (x + 2) % NX
    y_up, y_down, y_far = (y + 1) % NY, (y + NY - 1) % NY, (y + 2) % NY
    right, left = dev(x_up, y, c), dev(x_down, y, c)
    upper, lower = dev(x, y_up, c), dev(x, y_down, c)
    twin = dev(x, y, 1 - c)
    barrier_with([right, left, upper, lower, twin])
    copies = Copies(send_sem, recv_sem)
    go = copies.start
    kr0 = go(k_ref, kg_ref.at[x, 0], right)
    kl1 = go(v_ref, kg_ref.at[x, 1], left)
    qu0 = go(q_ref, qg_ref.at[g, 0], upper)
    ql1 = go(o_ref, qg_ref.at[g, 1], lower)
    kr1 = go(v_ref, kg_ref.at[x, 1], right)
    kl0 = go(k_ref, kg_ref.at[x, 0], left)
    qu1 = go(o_ref, qg_ref.at[g, 1], upper)
    ql0 = go(q_ref, qg_ref.at[g, 0], lower)
    twins = [go(q_ref, qg_ref.at[g, 0], twin), go(o_ref, qg_ref.at[g, 1], twin)]

    def on(yy, a, device):
        slot = qg_ref.at[yy * 2 + c, a]
        return go(slot, slot, device)

    kr0.wait_recv()
    kr2 = go(kg_ref.at[x_down, 0], kg_ref.at[x_down, 0], right)
    kl1.wait_recv()
    kl2 = go(kg_ref.at[x_up, 1], kg_ref.at[x_up, 1], left)
    qu0.wait_recv()
    qu2 = on(y_down, 0, upper)
    twins.append(on(y_down, 0, twin))
    ql1.wait_recv()
    ql2 = on(y_up, 1, lower)
    twins.append(on(y_up, 1, twin))
    qu1.wait_recv()
    twins.append(on(y_down, 1, twin))
    ql0.wait_recv()
    twins.append(on(y_up, 0, twin))
    qu2.wait_recv()
    twins.append(on(y_far, 0, twin))
    ql2.wait_recv()
    twins.append(on(y_far, 1, twin))
    for copy in (kr1, kl0, kr2, kl2, *twins):
        copy.wait_recv()
    copies.finish_sends()
    for copy in own:
        copy.wait()


def gathered(query, out_grad, key, value):
    return pl.pallas_call(
        gather_kernel,
        out_shape=(
            jax.ShapeDtypeStruct((NG, 2, ROWS, COLS), BF16),
            jax.ShapeDtypeStruct((NX, 2, ROWS, COLS), BF16),
        ),
        in_specs=[whole(pl.ANY)] * 4,
        out_specs=(whole(pl.ANY), whole(pl.ANY)),
        scratch_shapes=[
            pltpu.SemaphoreType.DMA((N_GATHER,)),
            pltpu.SemaphoreType.DMA((N_GATHER,)),
            pltpu.SemaphoreType.DMA((4,)),
        ],
        compiler_params=pltpu.CompilerParams(
            collective_id=0, has_side_effects=True, vmem_limit_bytes=4 * MIB
        ),
        name="gather",
    )(query, out_grad, key, value)


def entry_at(links_ref, r, t):
    me = lax.axis_index("ctx")
    mine = lax.rem(me, NG)
    g = lax.div(r, LOCAL)
    lb = lax.rem(r, LOCAL)
    qd = lax.div(me, NG) * NG + g
    block = jnp.where(lb < 2, 2 * qd + lb, 2 * (LAST - qd) + lb - 2)
    j = jnp.where(t < 2, block - t, links_ref[block, jnp.maximum(t - 2, 0)])
    safe = jnp.maximum(j, 0)
    stretch = lax.div(safe, 2)
    late = stretch > LAST // 2
    kd = jnp.where(late, LAST - stretch, stretch)
    klb = lax.rem(safe, 2) + jnp.where(late, 2, 0)
    here = jnp.logical_and(j >= 0, lax.rem(kd, NG) == mine)
    return here, lax.div(kd, NG), klb


def nt(a, b):
    return lax.dot_general(a, b, (((1,), (1,)), ((), ())), preferred_element_type=F32)


def nn(a, b):
    return lax.dot_general(a, b, (((1,), (0,)), ((), ())), preferred_element_type=F32)


def tn(a, b):
    return lax.dot_general(a, b, (((0,), (0,)), ((), ())), preferred_element_type=F32)


def live_mask(t):
    keys = lax.broadcasted_iota(jnp.int32, (BLK, BLK), 0)
    queries = lax.broadcasted_iota(jnp.int32, (BLK, BLK), 1)
    return keys <= queries + jnp.where(t == 0, 0, BLK)


def head(ref, slot, a, lb, i):
    return ref[slot, a, pl.ds(pl.multiple_of(lb * BLK, BLK), BLK), i * HEAD_DIM : (i + 1) * HEAD_DIM]


def stats_kernel(links_ref, qg_ref, kg_ref, part_ref):
    def slot_body(r, _):
        g, lb = lax.div(r, LOCAL), lax.rem(r, LOCAL)
        part_ref[r, 0:4, :] = jnp.full((4, BLK), NEG, F32)
        part_ref[r, 4:16, :] = jnp.zeros((12, BLK), F32)

        def entry_body(t, _):
            here, kx, klb = entry_at(links_ref, r, t)

            @pl.when(here)
            def _():
                live = live_mask(t)
                for i in range(HEADS_HERE):
                    score = nt(head(kg_ref, kx, 0, klb, i), head(qg_ref, g, 0, lb, i)) * SCALE
                    dprob = nt(head(kg_ref, kx, 1, klb, i), head(qg_ref, g, 1, lb, i))
                    score = jnp.where(live, score, NEG)
                    old = part_ref[r, i : i + 1, :]
                    top = jnp.maximum(old, jnp.max(score, axis=0, keepdims=True))
                    shrink = jnp.exp(old - top)
                    e = jnp.exp(score - top)
                    part_ref[r, i : i + 1, :] = top
                    part_ref[r, 4 + i : 5 + i, :] = part_ref[
                        r, 4 + i : 5 + i, :
                    ] * shrink + jnp.sum(e, axis=0, keepdims=True)
                    part_ref[r, 8 + i : 9 + i, :] = part_ref[
                        r, 8 + i : 9 + i, :
                    ] * shrink + jnp.sum(e * dprob, axis=0, keepdims=True)

            return 0

        lax.fori_loop(0, SPAN, entry_body, 0)
        return 0

    lax.fori_loop(0, NG * LOCAL, slot_body, 0)


def partial_stats(links, qg, kg):
    return pl.pallas_call(
        stats_kernel,
        out_shape=jax.ShapeDtypeStruct((NG * LOCAL, 16, BLK), F32),
        in_specs=[whole(pltpu.SMEM), whole(VMEM), whole(VMEM)],
        out_specs=whole(VMEM),
        compiler_params=pltpu.CompilerParams(vmem_limit_bytes=40 * MIB),
        name="partial_stats",
    )(links, qg, kg)


def join_kernel(part_ref, full_ref, got_ref, mine_ref, send_sem, recv_sem):
    x, y, c, h = place()
    g = y * 2 + c
    group = [(x * NG + (g + p) % NG, h) for p in range(1, NG)]
    barrier_with(group)
    copies = Copies(send_sem, recv_sem)
    for p in range(1, NG):
        peer = (g + p) % NG
        copies.start(part_ref.at[pl.ds(peer * LOCAL, LOCAL)], got_ref.at[p - 1], group[p - 1])
    mine_ref[...] = part_ref[pl.ds(g * LOCAL, LOCAL)]
    for copy in list(copies.made):
        copy.wait_recv()
    tops = [mine_ref[:, 0:4, :]] + [got_ref[p, :, 0:4, :] for p in range(NG - 1)]
    top = functools.reduce(jnp.maximum, tops)
    weights = [jnp.exp(t - top) for t in tops]
    total = mine_ref[:, 4:8, :] * weights[0]
    dot = mine_ref[:, 8:12, :] * weights[0]
    for p in range(NG - 1):
        total = total + got_ref[p, :, 4:8, :] * weights[p + 1]
        dot = dot + got_ref[p, :, 8:12, :] * weights[p + 1]
    own = pl.ds(g * LOCAL, LOCAL)
    full_ref[own, 0:4, :] = top + jnp.log(total)
    full_ref[own, 4:8, :] = dot / total
    later = [copies.start(full_ref.at[own], full_ref.at[own], device) for device in group]
    for copy in later:
        copy.wait_recv()
    copies.finish_sends()


def joined_stats(part):
    return pl.pallas_call(
        join_kernel,
        out_shape=jax.ShapeDtypeStruct((NG * LOCAL, 8, BLK), F32),
        in_specs=[whole(VMEM)],
        out_specs=whole(VMEM),
        scratch_shapes=[
            VMEM((NG - 1, LOCAL, 16, BLK), F32),
            VMEM((LOCAL, 16, BLK), F32),
            pltpu.SemaphoreType.DMA((14,)),
            pltpu.SemaphoreType.DMA((14,)),
        ],
        compiler_params=pltpu.CompilerParams(
            collective_id=1, has_side_effects=True, vmem_limit_bytes=8 * MIB
        ),
        name="join_stats",
    )(part)


def grads_kernel(links_ref, qg_ref, kg_ref, full_ref, dq_ref, dkv_ref, kv_acc, q_acc):
    def clear(n, _):
        kv_acc[n] = jnp.zeros((ROWS, COLS), F32)
        return 0

    lax.fori_loop(0, 2 * NX, clear, 0)

    def slot_body(r, _):
        g, lb = lax.div(r, LOCAL), lax.rem(r, LOCAL)
        q_acc[...] = jnp.zeros_like(q_acc)

        def entry_body(t, _):
            here, kx, klb = entry_at(links_ref, r, t)

            @pl.when(here)
            def _():
                live = live_mask(t)
                rows = pl.ds(pl.multiple_of(klb * BLK, BLK), BLK)
                for i in range(HEADS_HERE):
                    cols = slice(i * HEAD_DIM, (i + 1) * HEAD_DIM)
                    q, o = head(qg_ref, g, 0, lb, i), head(qg_ref, g, 1, lb, i)
                    k = head(kg_ref, kx, 0, klb, i)
                    score = nt(k, q) * SCALE
                    dprob = nt(head(kg_ref, kx, 1, klb, i), o)
                    prob = jnp.exp(jnp.where(live, score - full_ref[r, i : i + 1, :], NEG))
                    dscore = (prob * (dprob - full_ref[r, 4 + i : 5 + i, :])).astype(BF16)
                    kv_acc[2 * kx, rows, cols] += nn(dscore, q)
                    kv_acc[2 * kx + 1, rows, cols] += nn(prob.astype(BF16), o)
                    q_acc[:, cols] += tn(dscore, k)

            return 0

        lax.fori_loop(0, SPAN, entry_body, 0)
        dq_ref[g, pl.ds(pl.multiple_of(lb * BLK, BLK), BLK), :] = (q_acc[...] * SCALE).astype(BF16)
        return 0

    lax.fori_loop(0, NG * LOCAL, slot_body, 0)

    def leave(n, _):
        dkv_ref[n, 0] = (kv_acc[2 * n] * SCALE).astype(BF16)
        dkv_ref[n, 1] = kv_acc[2 * n + 1].astype(BF16)
        return 0

    lax.fori_loop(0, NX, leave, 0)


def partial_grads(links, qg, kg, full):
    return pl.pallas_call(
        grads_kernel,
        out_shape=(
            jax.ShapeDtypeStruct((NG, ROWS, COLS), BF16),
            jax.ShapeDtypeStruct((NX, 2, ROWS, COLS), BF16),
        ),
        in_specs=[whole(pltpu.SMEM), whole(VMEM), whole(VMEM), whole(VMEM)],
        out_specs=(whole(VMEM), whole(VMEM)),
        scratch_shapes=[VMEM((2 * NX, ROWS, COLS), F32), VMEM((BLK, COLS), F32)],
        compiler_params=pltpu.CompilerParams(vmem_limit_bytes=56 * MIB),
        name="partial_grads",
    )(links, qg, kg, full)


N_SUM = 16
CHUNK = 64


def add_rows(dst, start, stop, *terms):
    def body(n, _):
        rows = pl.ds(pl.multiple_of(start + n * CHUNK, CHUNK), CHUNK)
        total = terms[0][rows, :].astype(F32)
        for term in terms[1:]:
            total = total + term[rows, :].astype(F32)
        dst[rows, :] = total.astype(BF16)
        return 0

    lax.fori_loop(0, (stop - start) // CHUNK, body, 0)


def sum_kernel(
    dq_ref, dkv_ref, gq_ref, gk_ref, gv_ref, twin_buf, q_acc, k_in, q_in, k_mid, q_mid, send_sem, recv_sem
):
    x, y, c, h = place()

    def dev(xx, yy, cc):
        return ((xx * NY + yy) * 2 + cc, h)

    x_up, x_down, x_far = (x + 1) % NX, (x + NX - 1) % NX, (x + 2) % NX
    y_up, y_down, y_far = (y + 1) % NY, (y + NY - 1) % NY, (y + 2) % NY
    right, left = dev(x_up, y, c), dev(x_down, y, c)
    upper, lower = dev(x, y_up, c), dev(x, y_down, c)
    twin = dev(x, y, 1 - c)
    barrier_with([right, left, upper, lower, twin])
    copies = Copies(send_sem, recv_sem)
    go = copies.start
    half = ROWS // 2
    top, bottom = pl.ds(0, half), pl.ds(half, half)
    kr0 = go(dkv_ref.at[x_far, 0], k_mid.at[0], right)
    kl0 = go(dkv_ref.at[x_far, 1], k_mid.at[1], left)
    order = (y_far, y_up, y_down, y)
    pairs = [
        go(dq_ref.at[yy * 2 + 1 - c], twin_buf.at[n], twin) for n, yy in enumerate(order)
    ]
    kr1 = go(dkv_ref.at[x_up, 1], k_in.at[0, 1], right)
    kl1 = go(dkv_ref.at[x_down, 0], k_in.at[1, 0], left)

    def take(n):
        pairs[n].wait_recv()
        add_rows(q_acc.at[n], 0, ROWS, dq_ref.at[order[n] * 2 + c], twin_buf.at[n])

    take(0)
    qu0 = go(q_acc.at[0, top], q_mid.at[0, top], upper)
    ql0 = go(q_acc.at[0, bottom], q_mid.at[0, bottom], lower)
    take(1)
    qu1 = go(q_acc.at[1, bottom], q_in.at[0, bottom], upper)
    take(2)
    ql1 = go(q_acc.at[2, top], q_in.at[1, top], lower)
    take(3)
    qu0.wait_recv()
    add_rows(q_mid.at[1], 0, half, q_acc.at[1], q_mid.at[0])
    qu2 = go(q_mid.at[1, top], q_in.at[0, top], upper)
    ql0.wait_recv()
    add_rows(q_mid.at[1], half, ROWS, q_acc.at[2], q_mid.at[0])
    ql2 = go(q_mid.at[1, bottom], q_in.at[1, bottom], lower)
    kr0.wait_recv()
    add_rows(k_mid.at[2], 0, ROWS, dkv_ref.at[x_up, 0], k_mid.at[0])
    kr2 = go(k_mid.at[2], k_in.at[0, 0], right)
    kl0.wait_recv()
    add_rows(k_mid.at[3], 0, ROWS, dkv_ref.at[x_down, 1], k_mid.at[1])
    kl2 = go(k_mid.at[3], k_in.at[1, 1], left)
    for copy in (qu1, ql1, qu2, ql2):
        copy.wait_recv()
    add_rows(gq_ref, 0, ROWS, q_acc.at[3], q_in.at[0], q_in.at[1])
    kr1.wait_recv()
    kl2.wait_recv()
    add_rows(gv_ref, 0, ROWS, dkv_ref.at[x, 1], k_in.at[0, 1], k_in.at[1, 1])
    kl1.wait_recv()
    kr2.wait_recv()
    add_rows(gk_ref, 0, ROWS, dkv_ref.at[x, 0], k_in.at[0, 0], k_in.at[1, 0])
    copies.finish_sends()


def summed(dq, dkv):
    grad = jax.ShapeDtypeStruct((ROWS, COLS), BF16)
    return pl.pallas_call(
        sum_kernel,
        out_shape=(grad, grad, grad),
        in_specs=[whole(VMEM), whole(VMEM)],
        out_specs=(whole(VMEM), whole(VMEM), whole(VMEM)),
        scratch_shapes=[
            VMEM((NY, ROWS, COLS), BF16),
            VMEM((NY, ROWS, COLS), BF16),
            VMEM((2, 2, ROWS, COLS), BF16),
            VMEM((2, ROWS, COLS), BF16),
            VMEM((4, ROWS, COLS), BF16),
            VMEM((2, ROWS, COLS), BF16),
            pltpu.SemaphoreType.DMA((N_SUM,)),
            pltpu.SemaphoreType.DMA((N_SUM,)),
        ],
        compiler_params=pltpu.CompilerParams(
            collective_id=2, has_side_effects=True, vmem_limit_bytes=40 * MIB
        ),
        name="sum_grads",
    )(dq, dkv)


def per_device(query, key, value, out_grad, links):
    qg, kg = gathered(query, out_grad, key, value)
    full = joined_stats(partial_stats(links, qg, kg))
    dq, dkv = partial_grads(links, qg, kg, full)
    return summed(dq, dkv)


def solution(mesh):
    spec = P("ctx", "head")
    return jax.shard_map(
        per_device,
        mesh=mesh,
        in_specs=(spec, spec, spec, spec, P()),
        out_specs=(spec, spec, spec),
        check_vma=False,
    )
```

```python
import functools

import jax
import jax.numpy as jnp
from jax import lax
from jax.experimental import pallas as pl
from jax.experimental.pallas import tpu as pltpu
from jax.sharding import PartitionSpec as P

HEAD_DIM = 128
BLK = 128
LINKS = 6
HEADS = 2
SIDE = 4
NG = 8
LOCAL = 4
ROWS = 512
COLS = 512
WIDE = HEADS * HEAD_DIM
NQ = 2 * NG * LOCAL
NK = 2 * SIDE * LOCAL
LAST = 63
UNROLL = 4
LIST = 256
NEG = -1e30
SCALE = HEAD_DIM**-0.5
LOG2E = 1.4426950408889634
MESH = pl.DeviceIdType.MESH
BF16 = jnp.bfloat16
F32 = jnp.float32
VMEM = pltpu.VMEM
MIB = 1 << 20


def whole(space):
    return pl.BlockSpec(memory_space=space)


def place():
    me = lax.axis_index("ctx")
    return me // 8, (me // 2) % 4, me % 2


class Half:
    def __init__(self, s):
        x, y, c = place()
        self.s, self.c = s, c
        self.a, self.b = (x, y) if s == 0 else (y, x)
        self.g = self.b * 2 + c
        self.a_up, self.a_down, self.a_far = [(self.a + n) % SIDE for n in (1, 3, 2)]
        self.b_up, self.b_down, self.b_far = [(self.b + n) % SIDE for n in (1, 3, 2)]
        self.right, self.left = self.at(self.a_up, self.b, c), self.at(self.a_down, self.b, c)
        self.upper, self.lower = self.at(self.a, self.b_up, c), self.at(self.a, self.b_down, c)
        self.twin = self.at(self.a, self.b, 1 - c)

    def at(self, a, b, c):
        x, y = (a, b) if self.s == 0 else (b, a)
        return ((x * SIDE + y) * 2 + c, lax.axis_index("head"))


def barrier_with(partners):
    sem = pltpu.get_barrier_semaphore()
    for partner in partners:
        pl.semaphore_signal(sem, inc=1, device_id=partner, device_id_type=MESH)
    pl.semaphore_wait(sem, len(partners))


class Copies:
    def __init__(self, send_sem, recv_sem):
        self.send_sem, self.recv_sem, self.made = send_sem, recv_sem, []

    def start(self, src, dst, device):
        n = len(self.made)
        copy = pltpu.make_async_remote_copy(
            src_ref=src,
            dst_ref=dst,
            send_sem=self.send_sem.at[n],
            recv_sem=self.recv_sem.at[n],
            device_id=device,
            device_id_type=MESH,
        )
        copy.start()
        self.made.append(copy)
        return copy

    def finish_sends(self):
        for copy in self.made:
            copy.wait_send()


def nt(a, b):
    return lax.dot_general(a, b, (((1,), (1,)), ((), ())), preferred_element_type=F32)


def nn(a, b):
    return lax.dot_general(a, b, (((1,), (0,)), ((), ())), preferred_element_type=F32)


def tn(a, b):
    return lax.dot_general(a, b, (((0,), (0,)), ((), ())), preferred_element_type=F32)


def in_turn(*works):
    works = list(works)
    while works:
        for work in list(works):
            if next(work, works) is works:
                works.remove(work)


def index_of_holder(block):
    stretch = block // 2
    late = stretch > LAST // 2
    return jnp.where(late, LAST - stretch, stretch), block % 2 + jnp.where(late, 2, 0)


def write_list(links_ref, named_ref, list_ref):
    shape = (8, BLK)
    block = lax.broadcasted_iota(jnp.int32, shape, 1)
    row = lax.broadcasted_iota(jnp.int32, shape, 0)
    named_ref[...] = block - 1
    named_ref[0:LINKS, :] = links_ref[...]
    named = named_ref[...]
    q_dev, q_local = index_of_holder(block)
    k_dev, k_local = index_of_holder(jnp.maximum(named, 0))
    used = jnp.logical_and(named >= 0, row != LINKS + 1)
    keys = lax.broadcasted_iota(jnp.int32, (BLK, BLK), 0)
    lanes = lax.broadcasted_iota(jnp.int32, (BLK, BLK), 1)
    before = jnp.where(keys < lanes, 1.0, 0.0).astype(BF16)
    out = [jnp.zeros(shape, F32) for _ in range(LIST // BLK)]
    base = jnp.zeros((1, 1), F32)
    for s in range(2):
        half = Half(s)
        q_x, q_y, k_x, k_y = q_dev // 8, (q_dev // 2) % 4, k_dev // 8, (k_dev // 2) % 4
        q_a, q_b = (q_x, q_y) if s == 0 else (q_y, q_x)
        k_a, k_b = (k_x, k_y) if s == 0 else (k_y, k_x)
        meets = jnp.logical_and(q_a == half.a, k_b * 2 + k_dev % 2 == half.g)
        here = jnp.where(jnp.logical_and(used, meets), 1.0, 0.0)
        q_slot = (s * NG + q_b * 2 + q_dev % 2) * LOCAL + q_local
        k_slot = (s * SIDE + k_a) * LOCAL + k_local
        at = base + jnp.sum(nn(here.astype(BF16), before), axis=0, keepdims=True)
        for t in range(LINKS + 1):
            flag = here[t : t + 1, :]
            values = jnp.where(row == 0, q_slot[t : t + 1, :], k_slot[t : t + 1, :]).astype(F32)
            for n in range(LIST // BLK):
                spot = keys.astype(F32) + float(n * BLK)
                hot = jnp.where(spot == at, flag, 0.0).astype(BF16)
                out[n] = out[n] + nt(values.astype(BF16), hot)
            at = at + flag
        base = base + jnp.sum(jnp.sum(here, axis=1, keepdims=True), axis=0, keepdims=True)
    for n in range(LIST // BLK):
        spot = block.astype(F32) + float(n * BLK)
        spare = jnp.where(row == 0, float(NQ), float(NK))
        full = jnp.where(spot < base, out[n], spare)
        list_ref[:, n * BLK : (n + 1) * BLK] = jnp.where(row == 2, base, full).astype(jnp.int32)


N_GATHER = 40


def gather_kernel(
    q_ref, o_ref, k_ref, v_ref, links_ref,
    qg_ref, kg_ref, qt_ref, list_ref,
    named_ref, send_sem, recv_sem, own_sem,
):
    first = Half(0)
    copies = Copies(send_sem, recv_sem)
    go = copies.start
    own = []

    def columns(ref, s):
        return ref.at[:, s * WIDE : (s + 1) * WIDE]

    def keep(src, dst):
        copy = pltpu.make_async_copy(src, dst, own_sem.at[len(own)])
        copy.start()
        own.append(copy)

    def turn(g, a):
        def body(lb, _):
            rows = pl.ds(pl.multiple_of(lb * BLK, BLK), BLK)
            for i in range(HEADS):
                tile = slice(i * HEAD_DIM, (i + 1) * HEAD_DIM)
                qt_ref[g * LOCAL + lb, a, tile, :] = qg_ref[g, a, rows, tile].T
            return 0

        lax.fori_loop(0, LOCAL, body, 0)

    def work(s):
        at = Half(s)
        ka, qa = s * SIDE + at.a, s * NG + at.g
        q, o, k, v = [columns(ref, s) for ref in (q_ref, o_ref, k_ref, v_ref)]
        keep(q, qg_ref.at[qa, 0])
        keep(o, qg_ref.at[qa, 1])
        keep(k, kg_ref.at[ka, 0])
        keep(v, kg_ref.at[ka, 1])
        if s == 0:
            barrier_with([at.right, at.left, at.upper, at.lower, at.twin])
        yield
        kr0 = go(k, kg_ref.at[ka, 0], at.right)
        kl1 = go(v, kg_ref.at[ka, 1], at.left)
        qu0 = go(q, qg_ref.at[qa, 0], at.upper)
        ql1 = go(o, qg_ref.at[qa, 1], at.lower)
        yield
        kr1 = go(v, kg_ref.at[ka, 1], at.right)
        kl0 = go(k, kg_ref.at[ka, 0], at.left)
        qu1 = go(o, qg_ref.at[qa, 1], at.upper)
        ql0 = go(q, qg_ref.at[qa, 0], at.lower)
        tq, to = go(q, qg_ref.at[qa, 0], at.twin), go(o, qg_ref.at[qa, 1], at.twin)
        yield
        if s == 0:
            write_list(links_ref, named_ref, list_ref)
        for copy in own[4 * s : 4 * s + 2]:
            copy.wait()
        turn(qa, 0)
        turn(qa, 1)
        yield

        def on(b, a, device):
            slot = qg_ref.at[s * NG + b * 2 + at.c, a]
            return go(slot, slot, device)

        def mine(b):
            return s * NG + b * 2 + at.c

        def other(b):
            return s * NG + b * 2 + 1 - at.c

        k_down, k_up = kg_ref.at[s * SIDE + at.a_down, 0], kg_ref.at[s * SIDE + at.a_up, 1]
        kr0.wait_recv()
        kr2 = go(k_down, k_down, at.right)
        kl1.wait_recv()
        kl2 = go(k_up, k_up, at.left)
        qu0.wait_recv()
        qu2 = on(at.b_down, 0, at.upper)
        td0 = on(at.b_down, 0, at.twin)
        ql1.wait_recv()
        ql2 = on(at.b_up, 1, at.lower)
        tu1 = on(at.b_up, 1, at.twin)
        yield
        turn(mine(at.b_down), 0)
        turn(mine(at.b_up), 1)
        tq.wait_recv()
        turn(other(at.b), 0)
        to.wait_recv()
        turn(other(at.b), 1)
        yield
        qu1.wait_recv()
        td1 = on(at.b_down, 1, at.twin)
        ql0.wait_recv()
        tu0 = on(at.b_up, 0, at.twin)
        yield
        turn(mine(at.b_down), 1)
        turn(mine(at.b_up), 0)
        td0.wait_recv()
        turn(other(at.b_down), 0)
        tu1.wait_recv()
        turn(other(at.b_up), 1)
        yield
        td1.wait_recv()
        turn(other(at.b_down), 1)
        tu0.wait_recv()
        turn(other(at.b_up), 0)
        yield
        qu2.wait_recv()
        tf0 = on(at.b_far, 0, at.twin)
        ql2.wait_recv()
        tf1 = on(at.b_far, 1, at.twin)
        yield
        turn(mine(at.b_far), 0)
        turn(mine(at.b_far), 1)
        yield
        tf0.wait_recv()
        turn(other(at.b_far), 0)
        tf1.wait_recv()
        turn(other(at.b_far), 1)
        for copy in (kr1, kl0, kr2, kl2):
            copy.wait_recv()

    in_turn(work(0), work(1))
    copies.finish_sends()
    for s in range(2):
        for copy in own[4 * s + 2 : 4 * s + 4]:
            copy.wait()


def gathered(query, out_grad, key, value, links):
    return pl.pallas_call(
        gather_kernel,
        out_shape=(
            jax.ShapeDtypeStruct((2 * NG, 2, ROWS, WIDE), BF16),
            jax.ShapeDtypeStruct((2 * SIDE, 2, ROWS, WIDE), BF16),
            jax.ShapeDtypeStruct((NQ, 2, WIDE, BLK), BF16),
            jax.ShapeDtypeStruct((8, LIST), jnp.int32),
        ),
        in_specs=[whole(pltpu.HBM)] * 4 + [whole(VMEM)],
        out_specs=(whole(VMEM), whole(VMEM), whole(VMEM), whole(VMEM)),
        scratch_shapes=[
            VMEM((8, BLK), jnp.int32),
            pltpu.SemaphoreType.DMA((N_GATHER,)),
            pltpu.SemaphoreType.DMA((N_GATHER,)),
            pltpu.SemaphoreType.DMA((8,)),
        ],
        compiler_params=pltpu.CompilerParams(
            collective_id=0, has_side_effects=True, vmem_limit_bytes=28 * MIB
        ),
        name="gather",
    )(query, out_grad, key, value, links)


class Entry:
    def __init__(self, q_slot, k_slot, qt_ref, kg_ref, causal):
        self.q_slot, self.k_slot = q_slot, k_slot
        self.q_from, self.k_from = q_slot % NQ, k_slot % NK
        self.k_dev = self.k_from // LOCAL
        self.k_rows = pl.ds(pl.multiple_of(self.k_from % LOCAL * BLK, BLK), BLK)
        tiles = [slice(i * HEAD_DIM, (i + 1) * HEAD_DIM) for i in range(HEADS)]
        self.keys = [kg_ref[self.k_dev, 0, self.k_rows, tile] for tile in tiles]
        values = [kg_ref[self.k_dev, 1, self.k_rows, tile] for tile in tiles]
        self.score = [nn(self.keys[i], qt_ref[self.q_from, 0, tiles[i], :]) * (SCALE * LOG2E) for i in range(HEADS)]
        self.dprob = [nn(values[i], qt_ref[self.q_from, 1, tiles[i], :]) for i in range(HEADS)]
        if causal:
            down = lax.broadcasted_iota(jnp.int32, (BLK, BLK), 0)
            live = down <= lax.broadcasted_iota(jnp.int32, (BLK, BLK), 1)
            self.score = [jnp.where(live, score, NEG) for score in self.score]


def each_entry(list_ref, qt_ref, kg_ref, finish):
    def own(s, _):
        x, y, c = place()
        a, b = jnp.where(s == 0, x, y), jnp.where(s == 0, y, x)
        q_slot, k_slot = (s * NG + b * 2 + c) * LOCAL, (s * SIDE + a) * LOCAL
        finish([Entry(q_slot + lb, k_slot + lb, qt_ref, kg_ref, True) for lb in range(LOCAL)])
        return 0

    lax.fori_loop(0, 2, own, 0)

    def listed(n, _):
        spots = [n * UNROLL + u for u in range(UNROLL)]
        finish([Entry(list_ref[0, at], list_ref[1, at], qt_ref, kg_ref, False) for at in spots])
        return 0

    lax.fori_loop(0, (list_ref[2, 0] + UNROLL - 1) // UNROLL, listed, 0)


def stats_kernel(list_ref, qt_ref, kg_ref, part_ref):
    part_ref[:, 0:HEADS, :] = jnp.full((NQ + 1, HEADS, BLK), NEG, F32)
    part_ref[:, HEADS:8, :] = jnp.zeros((NQ + 1, 8 - HEADS, BLK), F32)

    def finish(entries):
        found = []
        for e in entries:
            tops = [jnp.max(score, axis=0, keepdims=True) for score in e.score]
            probs = [jnp.exp2(score - top) for score, top in zip(e.score, tops)]
            sums = [jnp.sum(prob, axis=0, keepdims=True) for prob in probs]
            dots = [jnp.sum(p * d, axis=0, keepdims=True) for p, d in zip(probs, e.dprob)]
            found.append([jnp.concatenate(rows, axis=0) for rows in (tops, sums, dots)])
        for e, (top, total, dot) in zip(entries, found):
            old = part_ref[e.q_slot]
            old_top = old[0:HEADS]
            new_top = jnp.maximum(old_top, top)
            was, now = jnp.exp2(old_top - new_top), jnp.exp2(top - new_top)
            part_ref[e.q_slot, 0:HEADS, :] = new_top
            part_ref[e.q_slot, HEADS : 2 * HEADS, :] = old[HEADS : 2 * HEADS] * was + total * now
            part_ref[e.q_slot, 2 * HEADS : 3 * HEADS, :] = old[2 * HEADS : 3 * HEADS] * was + dot * now

    each_entry(list_ref, qt_ref, kg_ref, finish)


def partial_stats(entries, qt, kg):
    return pl.pallas_call(
        stats_kernel,
        out_shape=jax.ShapeDtypeStruct((NQ + 1, 8, BLK), F32),
        in_specs=[whole(pltpu.SMEM), whole(VMEM), whole(VMEM)],
        out_specs=whole(VMEM),
        compiler_params=pltpu.CompilerParams(vmem_limit_bytes=20 * MIB),
        name="partial_stats",
    )(entries, qt, kg)


def join_kernel(part_ref, full_ref, got_ref, mine_ref, send_sem, recv_sem):
    halves = [Half(0), Half(1)]

    def peer(at, p):
        g = (at.g + p) % NG
        return g, at.at(at.a, g // 2, g % 2)

    twin = halves[0].twin
    partners = [twin]
    for at in halves:
        for b in range(1, SIDE):
            for c in range(2):
                partners.append(at.at(at.a, (at.b + b) % SIDE, c))
    barrier_with(partners)
    copies = Copies(send_sem, recv_sem)
    for at in halves:
        for p in range(1, NG):
            g, device = peer(at, p)
            slots = pl.ds((at.s * NG + g) * LOCAL, LOCAL)
            copies.start(part_ref.at[slots], got_ref.at[at.s, p - 1], device)
    for at in halves:
        mine_ref[at.s] = part_ref[pl.ds((at.s * NG + at.g) * LOCAL, LOCAL)]
    arrived, later = list(copies.made), []
    for at in halves:
        s = at.s
        for copy in arrived[s * (NG - 1) : (s + 1) * (NG - 1)]:
            copy.wait_recv()
        parts = [mine_ref.at[s]] + [got_ref.at[s, p] for p in range(NG - 1)]
        tops = [part[:, 0:HEADS, :] for part in parts]
        top = functools.reduce(jnp.maximum, tops)
        weights = [jnp.exp2(t - top) for t in tops]
        total = sum(part[:, HEADS : 2 * HEADS, :] * w for part, w in zip(parts, weights))
        dot = sum(part[:, 2 * HEADS : 3 * HEADS, :] * w for part, w in zip(parts, weights))
        own = pl.ds((s * NG + at.g) * LOCAL, LOCAL)
        full_ref[own, 0:HEADS, :] = top + jnp.log(total) * LOG2E
        full_ref[own, HEADS : 2 * HEADS, :] = dot / total
        full_ref[own, 2 * HEADS : 8, :] = jnp.zeros((LOCAL, 8 - 2 * HEADS, BLK), F32)
        for p in range(1, NG):
            later.append(copies.start(full_ref.at[own], full_ref.at[own], peer(at, p)[1]))
    for copy in later:
        copy.wait_recv()
    copies.finish_sends()


def joined_stats(part):
    return pl.pallas_call(
        join_kernel,
        out_shape=jax.ShapeDtypeStruct((NQ, 8, BLK), F32),
        in_specs=[whole(VMEM)],
        out_specs=whole(VMEM),
        scratch_shapes=[
            VMEM((2, NG - 1, LOCAL, 8, BLK), F32),
            VMEM((2, LOCAL, 8, BLK), F32),
            pltpu.SemaphoreType.DMA((28,)),
            pltpu.SemaphoreType.DMA((28,)),
        ],
        compiler_params=pltpu.CompilerParams(
            collective_id=1, has_side_effects=True, vmem_limit_bytes=8 * MIB
        ),
        name="join_stats",
    )(part)


def grads_kernel(list_ref, qg_ref, qt_ref, kg_ref, full_ref, dq_ref, dk_ref, dv_ref):
    def clear(ref, count):
        def body(n, _):
            ref[n] = jnp.zeros((BLK, WIDE), BF16)
            return 0

        lax.fori_loop(0, count, body, 0)

    clear(dq_ref, NQ + 1)
    clear(dk_ref, NK + 1)
    clear(dv_ref, NK + 1)

    def finish(entries):
        found = []
        for e in entries:
            rows = pl.ds(pl.multiple_of(e.q_from % LOCAL * BLK, BLK), BLK)
            dq, dk, dv = [], [], []
            for i in range(HEADS):
                tile = slice(i * HEAD_DIM, (i + 1) * HEAD_DIM)
                prob = jnp.exp2(e.score[i] - full_ref[e.q_from, i : i + 1, :])
                delta = full_ref[e.q_from, HEADS + i : HEADS + i + 1, :]
                dscore = (prob * (e.dprob[i] - delta)).astype(BF16)
                dk.append(nn(dscore, qg_ref[e.q_from // LOCAL, 0, rows, tile]))
                dv.append(nn(prob.astype(BF16), qg_ref[e.q_from // LOCAL, 1, rows, tile]))
                dq.append(tn(dscore, e.keys[i]))
            found.append([jnp.concatenate(terms, axis=1).astype(BF16) for terms in (dq, dk, dv)])
        for e, (dq, dk, dv) in zip(entries, found):
            dq_ref[e.q_slot] += dq
            dk_ref[e.k_slot] += dk
            dv_ref[e.k_slot] += dv

    each_entry(list_ref, qt_ref, kg_ref, finish)


def partial_grads(entries, qg, qt, kg, full):
    return pl.pallas_call(
        grads_kernel,
        out_shape=(
            jax.ShapeDtypeStruct((NQ + 1, BLK, WIDE), BF16),
            jax.ShapeDtypeStruct((NK + 1, BLK, WIDE), BF16),
            jax.ShapeDtypeStruct((NK + 1, BLK, WIDE), BF16),
        ),
        in_specs=[whole(pltpu.SMEM)] + [whole(VMEM)] * 4,
        out_specs=(whole(VMEM), whole(VMEM), whole(VMEM)),
        compiler_params=pltpu.CompilerParams(vmem_limit_bytes=34 * MIB),
        name="partial_grads",
    )(entries, qg, qt, kg, full)


N_SUM = 32


def add(dst, first, last, *terms):
    def body(n, _):
        total = terms[0][n].astype(F32)
        for term in terms[1:]:
            total = total + term[n].astype(F32)
        dst[n] = total.astype(BF16)
        return 0

    lax.fori_loop(first, last, body, 0)


def leave(dst, s, scale, *terms):
    for n in range(LOCAL):
        total = terms[0][n].astype(F32)
        for term in terms[1:]:
            total = total + term[n].astype(F32)
        dst[n * BLK : (n + 1) * BLK, s * WIDE : (s + 1) * WIDE] = (total * scale).astype(BF16)


def sum_kernel(
    dq_ref, dk_ref, dv_ref, gq_ref, gk_ref, gv_ref,
    twin_buf, q_all, q_far, q_in, k_far, k_in, v_in, send_sem, recv_sem,
):
    copies = Copies(send_sem, recv_sem)
    go = copies.start
    low, high = pl.ds(0, 2), pl.ds(2, 2)

    def work(s):
        at = Half(s)
        if s == 0:
            barrier_with([at.right, at.left, at.upper, at.lower, at.twin])
        yield

        def keys(ref, a):
            return ref.at[pl.ds((s * SIDE + a) * LOCAL, LOCAL)]

        def queries(b, c):
            return dq_ref.at[pl.ds((s * NG + b * 2 + c) * LOCAL, LOCAL)]

        order = (at.b_far, at.b_up, at.b_down, at.b)
        kr0 = go(keys(dk_ref, at.a_far), k_far.at[s, 0], at.right)
        kl0 = go(keys(dv_ref, at.a_far), k_far.at[s, 1], at.left)
        pairs = [go(queries(b, 1 - at.c), twin_buf.at[s, n], at.twin) for n, b in enumerate(order)]
        yield
        kr1 = go(keys(dv_ref, at.a_up), v_in.at[s, 0], at.right)
        kl1 = go(keys(dk_ref, at.a_down), k_in.at[s, 1], at.left)
        yield

        def take(n):
            pairs[n].wait_recv()
            add(q_all.at[s, n], 0, LOCAL, queries(order[n], at.c), twin_buf.at[s, n])

        take(0)
        qu0 = go(q_all.at[s, 0, low], q_far.at[s, 0, low], at.upper)
        ql0 = go(q_all.at[s, 0, high], q_far.at[s, 0, high], at.lower)
        yield
        take(1)
        qu1 = go(q_all.at[s, 1, high], q_in.at[s, 0, high], at.upper)
        take(2)
        ql1 = go(q_all.at[s, 2, low], q_in.at[s, 1, low], at.lower)
        take(3)
        yield
        qu0.wait_recv()
        add(q_far.at[s, 1], 0, 2, q_all.at[s, 1], q_far.at[s, 0])
        qu2 = go(q_far.at[s, 1, low], q_in.at[s, 0, low], at.upper)
        ql0.wait_recv()
        add(q_far.at[s, 1], 2, LOCAL, q_all.at[s, 2], q_far.at[s, 0])
        ql2 = go(q_far.at[s, 1, high], q_in.at[s, 1, high], at.lower)
        yield
        kr0.wait_recv()
        add(k_far.at[s, 2], 0, LOCAL, keys(dk_ref, at.a_up), k_far.at[s, 0])
        kr2 = go(k_far.at[s, 2], k_in.at[s, 0], at.right)
        kl0.wait_recv()
        add(k_far.at[s, 3], 0, LOCAL, keys(dv_ref, at.a_down), k_far.at[s, 1])
        kl2 = go(k_far.at[s, 3], v_in.at[s, 1], at.left)
        yield
        for copy in (qu1, ql1, qu2, ql2):
            copy.wait_recv()
        leave(gq_ref, s, SCALE, q_all.at[s, 3], q_in.at[s, 0], q_in.at[s, 1])
        yield
        kr1.wait_recv()
        kl2.wait_recv()
        leave(gv_ref, s, 1.0, keys(dv_ref, at.a), v_in.at[s, 0], v_in.at[s, 1])
        kl1.wait_recv()
        kr2.wait_recv()
        leave(gk_ref, s, SCALE, keys(dk_ref, at.a), k_in.at[s, 0], k_in.at[s, 1])

    in_turn(work(0), work(1))
    copies.finish_sends()


def summed(dq, dk, dv):
    grad = jax.ShapeDtypeStruct((ROWS, COLS), BF16)
    block = (LOCAL, BLK, WIDE)
    return pl.pallas_call(
        sum_kernel,
        out_shape=(grad, grad, grad),
        in_specs=[whole(VMEM)] * 3,
        out_specs=(whole(VMEM), whole(VMEM), whole(VMEM)),
        scratch_shapes=[
            VMEM((2, SIDE, *block), BF16),
            VMEM((2, SIDE, *block), BF16),
            VMEM((2, 2, *block), BF16),
            VMEM((2, 2, *block), BF16),
            VMEM((2, 4, *block), BF16),
            VMEM((2, 2, *block), BF16),
            VMEM((2, 2, *block), BF16),
            pltpu.SemaphoreType.DMA((N_SUM,)),
            pltpu.SemaphoreType.DMA((N_SUM,)),
        ],
        compiler_params=pltpu.CompilerParams(
            collective_id=2, has_side_effects=True, vmem_limit_bytes=26 * MIB
        ),
        name="sum_grads",
    )(dq, dk, dv)


def per_device(query, key, value, out_grad, links):
    qg, kg, qt, entries = gathered(query, out_grad, key, value, links.T)
    full = joined_stats(partial_stats(entries, qt, kg))
    return summed(*partial_grads(entries, qg, qt, kg, full))


def solution(mesh):
    spec = P("ctx", "head")
    return jax.shard_map(
        per_device,
        mesh=mesh,
        in_specs=(spec, spec, spec, spec, P()),
        out_specs=(spec, spec, spec),
        check_vma=False,
    )
```

```python
import functools

import jax
import jax.numpy as jnp
from jax import lax
from jax.experimental import pallas as pl
from jax.experimental.pallas import tpu as pltpu
from jax.sharding import PartitionSpec as P

HEAD_DIM = 128
BLK = 128
LINKS = 6
HEADS = 2
SIDE = 4
NG = 8
LOCAL = 4
ROWS = 512
COLS = 512
WIDE = HEADS * HEAD_DIM
NQ = 2 * NG * LOCAL
NK = 2 * SIDE * LOCAL
LAST = 63
UNROLL = 4
LIST = 256
NEG = -1e30
SCALE = HEAD_DIM**-0.5
LOG2E = 1.4426950408889634
MESH = pl.DeviceIdType.MESH
BF16 = jnp.bfloat16
F32 = jnp.float32
VMEM = pltpu.VMEM
MIB = 1 << 20


def whole(space):
    return pl.BlockSpec(memory_space=space)


def pinned(*arrays):
    return [pltpu.with_memory_space_constraint(array, VMEM) for array in arrays]


def place():
    me = lax.axis_index("ctx")
    return me // 8, (me // 2) % 4, me % 2


class Half:
    def __init__(self, s):
        x, y, c = place()
        self.s, self.c = s, c
        self.a, self.b = (x, y) if s == 0 else (y, x)
        self.g = self.b * 2 + c
        self.a_up, self.a_down, self.a_far = [(self.a + n) % SIDE for n in (1, 3, 2)]
        self.b_up, self.b_down, self.b_far = [(self.b + n) % SIDE for n in (1, 3, 2)]
        self.right, self.left = self.at(self.a_up, self.b, c), self.at(self.a_down, self.b, c)
        self.upper, self.lower = self.at(self.a, self.b_up, c), self.at(self.a, self.b_down, c)
        self.twin = self.at(self.a, self.b, 1 - c)

    def at(self, a, b, c):
        x, y = (a, b) if self.s == 0 else (b, a)
        return ((x * SIDE + y) * 2 + c, lax.axis_index("head"))


def barrier_with(partners):
    sem = pltpu.get_barrier_semaphore()
    for partner in partners:
        pl.semaphore_signal(sem, inc=1, device_id=partner, device_id_type=MESH)
    pl.semaphore_wait(sem, len(partners))


class Copies:
    def __init__(self, send_sem, recv_sem):
        self.send_sem, self.recv_sem, self.made = send_sem, recv_sem, []

    def start(self, src, dst, device):
        n = len(self.made)
        copy = pltpu.make_async_remote_copy(
            src_ref=src,
            dst_ref=dst,
            send_sem=self.send_sem.at[n],
            recv_sem=self.recv_sem.at[n],
            device_id=device,
            device_id_type=MESH,
        )
        copy.start()
        self.made.append(copy)
        return copy

    def finish_sends(self):
        for copy in self.made:
            copy.wait_send()


def nt(a, b):
    return lax.dot_general(a, b, (((1,), (1,)), ((), ())), preferred_element_type=F32)


def nn(a, b):
    return lax.dot_general(a, b, (((1,), (0,)), ((), ())), preferred_element_type=F32)


def tn(a, b):
    return lax.dot_general(a, b, (((0,), (0,)), ((), ())), preferred_element_type=F32)


def in_turn(*works):
    works = list(works)
    while works:
        for work in list(works):
            if next(work, works) is works:
                works.remove(work)


def index_of_holder(block):
    stretch = block // 2
    late = stretch > LAST // 2
    return jnp.where(late, LAST - stretch, stretch), block % 2 + jnp.where(late, 2, 0)


def write_list(links_ref, named_ref, list_ref):
    shape = (8, BLK)
    block = lax.broadcasted_iota(jnp.int32, shape, 1)
    row = lax.broadcasted_iota(jnp.int32, shape, 0)
    named_ref[...] = block - 1
    named_ref[0:LINKS, :] = links_ref[...]
    named = named_ref[...]
    q_dev, q_local = index_of_holder(block)
    k_dev, k_local = index_of_holder(jnp.maximum(named, 0))
    used = jnp.logical_and(named >= 0, row != LINKS + 1)
    keys = lax.broadcasted_iota(jnp.int32, (BLK, BLK), 0)
    lanes = lax.broadcasted_iota(jnp.int32, (BLK, BLK), 1)
    before = jnp.where(keys < lanes, 1.0, 0.0).astype(BF16)
    out = [jnp.zeros(shape, F32) for _ in range(LIST // BLK)]
    base = jnp.zeros((1, 1), F32)
    for s in range(2):
        half = Half(s)
        q_x, q_y, k_x, k_y = q_dev // 8, (q_dev // 2) % 4, k_dev // 8, (k_dev // 2) % 4
        q_a, q_b = (q_x, q_y) if s == 0 else (q_y, q_x)
        k_a, k_b = (k_x, k_y) if s == 0 else (k_y, k_x)
        meets = jnp.logical_and(q_a == half.a, k_b * 2 + k_dev % 2 == half.g)
        here = jnp.where(jnp.logical_and(used, meets), 1.0, 0.0)
        q_slot = (s * NG + q_b * 2 + q_dev % 2) * LOCAL + q_local
        k_slot = (s * SIDE + k_a) * LOCAL + k_local
        at = base + jnp.sum(nn(here.astype(BF16), before), axis=0, keepdims=True)
        for t in range(LINKS + 1):
            flag = here[t : t + 1, :]
            values = jnp.where(row == 0, q_slot[t : t + 1, :], k_slot[t : t + 1, :]).astype(F32)
            for n in range(LIST // BLK):
                spot = keys.astype(F32) + float(n * BLK)
                hot = jnp.where(spot == at, flag, 0.0).astype(BF16)
                out[n] = out[n] + nt(values.astype(BF16), hot)
            at = at + flag
        base = base + jnp.sum(jnp.sum(here, axis=1, keepdims=True), axis=0, keepdims=True)
    for n in range(LIST // BLK):
        spot = block.astype(F32) + float(n * BLK)
        spare = jnp.where(row == 0, float(NQ), float(NK))
        full = jnp.where(spot < base, out[n], spare)
        list_ref[:, n * BLK : (n + 1) * BLK] = jnp.where(row == 2, base, full).astype(jnp.int32)


N_GATHER = 40


def gather_kernel(
    q_ref, o_ref, k_ref, v_ref, links_ref,
    qg_ref, kg_ref, qt_ref, list_ref,
    table_ref, named_ref, send_sem, recv_sem, own_sem,
):
    copies = Copies(send_sem, recv_sem)
    go = copies.start
    own = []
    table = pltpu.make_async_copy(links_ref, table_ref, own_sem.at[8])
    table.start()

    def columns(ref, s):
        return ref.at[:, s * WIDE : (s + 1) * WIDE]

    def keep(src, dst):
        copy = pltpu.make_async_copy(src, dst, own_sem.at[len(own)])
        copy.start()
        own.append(copy)

    def turn(g, a):
        def body(lb, _):
            rows = pl.ds(pl.multiple_of(lb * BLK, BLK), BLK)
            for i in range(HEADS):
                tile = slice(i * HEAD_DIM, (i + 1) * HEAD_DIM)
                qt_ref[g * LOCAL + lb, a, tile, :] = qg_ref[g, a, rows, tile].T
            return 0

        lax.fori_loop(0, LOCAL, body, 0)

    def work(s):
        at = Half(s)
        ka, qa = s * SIDE + at.a, s * NG + at.g
        q, o, k, v = [columns(ref, s) for ref in (q_ref, o_ref, k_ref, v_ref)]
        keep(q, qg_ref.at[qa, 0])
        keep(o, qg_ref.at[qa, 1])
        keep(k, kg_ref.at[ka, 0])
        keep(v, kg_ref.at[ka, 1])
        if s == 0:
            barrier_with([at.right, at.left, at.upper, at.lower, at.twin])
        yield
        kr0 = go(k, kg_ref.at[ka, 0], at.right)
        kl1 = go(v, kg_ref.at[ka, 1], at.left)
        qu0 = go(q, qg_ref.at[qa, 0], at.upper)
        ql1 = go(o, qg_ref.at[qa, 1], at.lower)
        yield
        kr1 = go(v, kg_ref.at[ka, 1], at.right)
        kl0 = go(k, kg_ref.at[ka, 0], at.left)
        qu1 = go(o, qg_ref.at[qa, 1], at.upper)
        ql0 = go(q, qg_ref.at[qa, 0], at.lower)
        tq, to = go(q, qg_ref.at[qa, 0], at.twin), go(o, qg_ref.at[qa, 1], at.twin)
        yield
        if s == 0:
            table.wait()
            write_list(table_ref, named_ref, list_ref)
        for copy in own[4 * s : 4 * s + 2]:
            copy.wait()
        turn(qa, 0)
        turn(qa, 1)
        yield

        def on(b, a, device):
            slot = qg_ref.at[s * NG + b * 2 + at.c, a]
            return go(slot, slot, device)

        def mine(b):
            return s * NG + b * 2 + at.c

        def other(b):
            return s * NG + b * 2 + 1 - at.c

        k_down, k_up = kg_ref.at[s * SIDE + at.a_down, 0], kg_ref.at[s * SIDE + at.a_up, 1]
        kr0.wait_recv()
        kr2 = go(k_down, k_down, at.right)
        kl1.wait_recv()
        kl2 = go(k_up, k_up, at.left)
        qu0.wait_recv()
        qu2 = on(at.b_down, 0, at.upper)
        td0 = on(at.b_down, 0, at.twin)
        ql1.wait_recv()
        ql2 = on(at.b_up, 1, at.lower)
        tu1 = on(at.b_up, 1, at.twin)
        yield
        turn(mine(at.b_down), 0)
        turn(mine(at.b_up), 1)
        tq.wait_recv()
        turn(other(at.b), 0)
        to.wait_recv()
        turn(other(at.b), 1)
        yield
        qu1.wait_recv()
        td1 = on(at.b_down, 1, at.twin)
        ql0.wait_recv()
        tu0 = on(at.b_up, 0, at.twin)
        yield
        turn(mine(at.b_down), 1)
        turn(mine(at.b_up), 0)
        td0.wait_recv()
        turn(other(at.b_down), 0)
        tu1.wait_recv()
        turn(other(at.b_up), 1)
        yield
        td1.wait_recv()
        turn(other(at.b_down), 1)
        tu0.wait_recv()
        turn(other(at.b_up), 0)
        yield
        qu2.wait_recv()
        tf0 = on(at.b_far, 0, at.twin)
        ql2.wait_recv()
        tf1 = on(at.b_far, 1, at.twin)
        yield
        turn(mine(at.b_far), 0)
        turn(mine(at.b_far), 1)
        yield
        tf0.wait_recv()
        turn(other(at.b_far), 0)
        tf1.wait_recv()
        turn(other(at.b_far), 1)
        for copy in (kr1, kl0, kr2, kl2):
            copy.wait_recv()

    in_turn(work(0), work(1))
    copies.finish_sends()
    for s in range(2):
        for copy in own[4 * s + 2 : 4 * s + 4]:
            copy.wait()


def gathered(query, out_grad, key, value, links):
    return pl.pallas_call(
        gather_kernel,
        out_shape=(
            VMEM((2 * NG, 2, ROWS, WIDE), BF16),
            VMEM((2 * SIDE, 2, ROWS, WIDE), BF16),
            VMEM((NQ, 2, WIDE, BLK), BF16),
            VMEM((8, LIST), jnp.int32),
        ),
        in_specs=[whole(pltpu.HBM)] * 5,
        out_specs=(whole(VMEM), whole(VMEM), whole(VMEM), whole(VMEM)),
        scratch_shapes=[
            VMEM((LINKS, BLK), jnp.int32),
            VMEM((8, BLK), jnp.int32),
            pltpu.SemaphoreType.DMA((N_GATHER,)),
            pltpu.SemaphoreType.DMA((N_GATHER,)),
            pltpu.SemaphoreType.DMA((9,)),
        ],
        compiler_params=pltpu.CompilerParams(
            collective_id=0, has_side_effects=True, vmem_limit_bytes=8 * MIB
        ),
        name="gather",
    )(*[pltpu.with_memory_space_constraint(v, pltpu.HBM) for v in (query, out_grad, key, value, links)])


class Entry:
    def __init__(self, q_slot, k_slot, qt_ref, kg_ref, causal):
        self.q_slot, self.k_slot = q_slot, k_slot
        self.q_from, self.k_from = q_slot % NQ, k_slot % NK
        self.k_dev = self.k_from // LOCAL
        self.k_rows = pl.ds(pl.multiple_of(self.k_from % LOCAL * BLK, BLK), BLK)
        tiles = [slice(i * HEAD_DIM, (i + 1) * HEAD_DIM) for i in range(HEADS)]
        self.keys = [kg_ref[self.k_dev, 0, self.k_rows, tile] for tile in tiles]
        values = [kg_ref[self.k_dev, 1, self.k_rows, tile] for tile in tiles]
        self.score = [nn(self.keys[i], qt_ref[self.q_from, 0, tiles[i], :]) * (SCALE * LOG2E) for i in range(HEADS)]
        self.dprob = [nn(values[i], qt_ref[self.q_from, 1, tiles[i], :]) for i in range(HEADS)]
        if causal:
            down = lax.broadcasted_iota(jnp.int32, (BLK, BLK), 0)
            live = down <= lax.broadcasted_iota(jnp.int32, (BLK, BLK), 1)
            self.score = [jnp.where(live, score, NEG) for score in self.score]


def each_entry(list_ref, qt_ref, kg_ref, finish):
    def own(s, _):
        x, y, c = place()
        a, b = jnp.where(s == 0, x, y), jnp.where(s == 0, y, x)
        q_slot, k_slot = (s * NG + b * 2 + c) * LOCAL, (s * SIDE + a) * LOCAL
        finish([Entry(q_slot + lb, k_slot + lb, qt_ref, kg_ref, True) for lb in range(LOCAL)])
        return 0

    lax.fori_loop(0, 2, own, 0)

    def listed(n, _):
        spots = [n * UNROLL + u for u in range(UNROLL)]
        finish([Entry(list_ref[0, at], list_ref[1, at], qt_ref, kg_ref, False) for at in spots])
        return 0

    lax.fori_loop(0, (list_ref[2, 0] + UNROLL - 1) // UNROLL, listed, 0)


def stats_kernel(list_ref, qt_ref, kg_ref, part_ref):
    part_ref[:, 0:HEADS, :] = jnp.full((NQ + 1, HEADS, BLK), NEG, F32)
    part_ref[:, HEADS:8, :] = jnp.zeros((NQ + 1, 8 - HEADS, BLK), F32)

    def finish(entries):
        found = []
        for e in entries:
            tops = [jnp.max(score, axis=0, keepdims=True) for score in e.score]
            probs = [jnp.exp2(score - top) for score, top in zip(e.score, tops)]
            sums = [jnp.sum(prob, axis=0, keepdims=True) for prob in probs]
            dots = [jnp.sum(p * d, axis=0, keepdims=True) for p, d in zip(probs, e.dprob)]
            found.append([jnp.concatenate(rows, axis=0) for rows in (tops, sums, dots)])
        for e, (top, total, dot) in zip(entries, found):
            old = part_ref[e.q_slot]
            old_top = old[0:HEADS]
            new_top = jnp.maximum(old_top, top)
            was, now = jnp.exp2(old_top - new_top), jnp.exp2(top - new_top)
            part_ref[e.q_slot, 0:HEADS, :] = new_top
            part_ref[e.q_slot, HEADS : 2 * HEADS, :] = old[HEADS : 2 * HEADS] * was + total * now
            part_ref[e.q_slot, 2 * HEADS : 3 * HEADS, :] = old[2 * HEADS : 3 * HEADS] * was + dot * now

    each_entry(list_ref, qt_ref, kg_ref, finish)


def partial_stats(entries, qt, kg):
    return pl.pallas_call(
        stats_kernel,
        out_shape=VMEM((NQ + 1, 8, BLK), F32),
        in_specs=[whole(pltpu.SMEM), whole(VMEM), whole(VMEM)],
        out_specs=whole(VMEM),
        compiler_params=pltpu.CompilerParams(vmem_limit_bytes=8 * MIB),
        name="partial_stats",
    )(entries, *pinned(qt, kg))


def join_kernel(part_ref, full_ref, got_ref, mine_ref, send_sem, recv_sem):
    halves = [Half(0), Half(1)]

    def peer(at, p):
        g = (at.g + p) % NG
        return g, at.at(at.a, g // 2, g % 2)

    twin = halves[0].twin
    partners = [twin]
    for at in halves:
        for b in range(1, SIDE):
            for c in range(2):
                partners.append(at.at(at.a, (at.b + b) % SIDE, c))
    barrier_with(partners)
    copies = Copies(send_sem, recv_sem)
    for at in halves:
        for p in range(1, NG):
            g, device = peer(at, p)
            slots = pl.ds((at.s * NG + g) * LOCAL, LOCAL)
            copies.start(part_ref.at[slots], got_ref.at[at.s, p - 1], device)
    for at in halves:
        mine_ref[at.s] = part_ref[pl.ds((at.s * NG + at.g) * LOCAL, LOCAL)]
    arrived, later = list(copies.made), []
    for at in halves:
        s = at.s
        for copy in arrived[s * (NG - 1) : (s + 1) * (NG - 1)]:
            copy.wait_recv()
        parts = [mine_ref.at[s]] + [got_ref.at[s, p] for p in range(NG - 1)]
        tops = [part[:, 0:HEADS, :] for part in parts]
        top = functools.reduce(jnp.maximum, tops)
        weights = [jnp.exp2(t - top) for t in tops]
        total = sum(part[:, HEADS : 2 * HEADS, :] * w for part, w in zip(parts, weights))
        dot = sum(part[:, 2 * HEADS : 3 * HEADS, :] * w for part, w in zip(parts, weights))
        own = pl.ds((s * NG + at.g) * LOCAL, LOCAL)
        full_ref[own, 0:HEADS, :] = top + jnp.log(total) * LOG2E
        full_ref[own, HEADS : 2 * HEADS, :] = dot / total
        full_ref[own, 2 * HEADS : 8, :] = jnp.zeros((LOCAL, 8 - 2 * HEADS, BLK), F32)
        for p in range(1, NG):
            later.append(copies.start(full_ref.at[own], full_ref.at[own], peer(at, p)[1]))
    for copy in later:
        copy.wait_recv()
    copies.finish_sends()


def joined_stats(part):
    return pl.pallas_call(
        join_kernel,
        out_shape=VMEM((NQ, 8, BLK), F32),
        in_specs=[whole(VMEM)],
        out_specs=whole(VMEM),
        scratch_shapes=[
            VMEM((2, NG - 1, LOCAL, 8, BLK), F32),
            VMEM((2, LOCAL, 8, BLK), F32),
            pltpu.SemaphoreType.DMA((28,)),
            pltpu.SemaphoreType.DMA((28,)),
        ],
        compiler_params=pltpu.CompilerParams(
            collective_id=1, has_side_effects=True, vmem_limit_bytes=8 * MIB
        ),
        name="join_stats",
    )(*pinned(part))


def grads_kernel(list_ref, qg_ref, qt_ref, kg_ref, full_ref, dq_ref, dk_ref, dv_ref):
    def clear(ref, count):
        def body(n, _):
            ref[n] = jnp.zeros((BLK, WIDE), BF16)
            return 0

        lax.fori_loop(0, count, body, 0)

    clear(dq_ref, NQ + 1)
    clear(dk_ref, NK + 1)
    clear(dv_ref, NK + 1)

    def finish(entries):
        found = []
        for e in entries:
            rows = pl.ds(pl.multiple_of(e.q_from % LOCAL * BLK, BLK), BLK)
            dq, dk, dv = [], [], []
            for i in range(HEADS):
                tile = slice(i * HEAD_DIM, (i + 1) * HEAD_DIM)
                prob = jnp.exp2(e.score[i] - full_ref[e.q_from, i : i + 1, :])
                delta = full_ref[e.q_from, HEADS + i : HEADS + i + 1, :]
                dscore = (prob * (e.dprob[i] - delta)).astype(BF16)
                dk.append(nn(dscore, qg_ref[e.q_from // LOCAL, 0, rows, tile]))
                dv.append(nn(prob.astype(BF16), qg_ref[e.q_from // LOCAL, 1, rows, tile]))
                dq.append(tn(dscore, e.keys[i]))
            found.append([jnp.concatenate(terms, axis=1).astype(BF16) for terms in (dq, dk, dv)])
        for e, (dq, dk, dv) in zip(entries, found):
            dq_ref[e.q_slot] += dq
            dk_ref[e.k_slot] += dk
            dv_ref[e.k_slot] += dv

    each_entry(list_ref, qt_ref, kg_ref, finish)


def partial_grads(entries, qg, qt, kg, full):
    return pl.pallas_call(
        grads_kernel,
        out_shape=(
            VMEM((NQ + 1, BLK, WIDE), BF16),
            VMEM((NK + 1, BLK, WIDE), BF16),
            VMEM((NK + 1, BLK, WIDE), BF16),
        ),
        in_specs=[whole(pltpu.SMEM)] + [whole(VMEM)] * 4,
        out_specs=(whole(VMEM), whole(VMEM), whole(VMEM)),
        compiler_params=pltpu.CompilerParams(vmem_limit_bytes=8 * MIB),
        name="partial_grads",
    )(entries, *pinned(qg, qt, kg, full))


N_SUM = 32


def add(dst, first, last, *terms):
    def body(n, _):
        total = terms[0][n].astype(F32)
        for term in terms[1:]:
            total = total + term[n].astype(F32)
        dst[n] = total.astype(BF16)
        return 0

    lax.fori_loop(first, last, body, 0)


def leave(dst, s, scale, *terms):
    for n in range(LOCAL):
        total = terms[0][n].astype(F32)
        for term in terms[1:]:
            total = total + term[n].astype(F32)
        dst[n * BLK : (n + 1) * BLK, s * WIDE : (s + 1) * WIDE] = (total * scale).astype(BF16)


def sum_kernel(
    dq_ref, dk_ref, dv_ref, gq_ref, gk_ref, gv_ref,
    twin_buf, q_all, q_far, q_in, k_far, k_in, v_in, send_sem, recv_sem,
):
    copies = Copies(send_sem, recv_sem)
    go = copies.start
    low, high = pl.ds(0, 2), pl.ds(2, 2)

    def work(s):
        at = Half(s)
        if s == 0:
            barrier_with([at.right, at.left, at.upper, at.lower, at.twin])
        yield

        def keys(ref, a):
            return ref.at[pl.ds((s * SIDE + a) * LOCAL, LOCAL)]

        def queries(b, c):
            return dq_ref.at[pl.ds((s * NG + b * 2 + c) * LOCAL, LOCAL)]

        order = (at.b_far, at.b_up, at.b_down, at.b)
        kr0 = go(keys(dk_ref, at.a_far), k_far.at[s, 0], at.right)
        kl0 = go(keys(dv_ref, at.a_far), k_far.at[s, 1], at.left)
        pairs = [go(queries(b, 1 - at.c), twin_buf.at[s, n], at.twin) for n, b in enumerate(order)]
        yield
        kr1 = go(keys(dv_ref, at.a_up), v_in.at[s, 0], at.right)
        kl1 = go(keys(dk_ref, at.a_down), k_in.at[s, 1], at.left)
        yield

        def take(n):
            pairs[n].wait_recv()
            add(q_all.at[s, n], 0, LOCAL, queries(order[n], at.c), twin_buf.at[s, n])

        take(0)
        qu0 = go(q_all.at[s, 0, low], q_far.at[s, 0, low], at.upper)
        ql0 = go(q_all.at[s, 0, high], q_far.at[s, 0, high], at.lower)
        yield
        take(1)
        qu1 = go(q_all.at[s, 1, high], q_in.at[s, 0, high], at.upper)
        take(2)
        ql1 = go(q_all.at[s, 2, low], q_in.at[s, 1, low], at.lower)
        take(3)
        yield
        qu0.wait_recv()
        add(q_far.at[s, 1], 0, 2, q_all.at[s, 1], q_far.at[s, 0])
        qu2 = go(q_far.at[s, 1, low], q_in.at[s, 0, low], at.upper)
        ql0.wait_recv()
        add(q_far.at[s, 1], 2, LOCAL, q_all.at[s, 2], q_far.at[s, 0])
        ql2 = go(q_far.at[s, 1, high], q_in.at[s, 1, high], at.lower)
        yield
        kr0.wait_recv()
        add(k_far.at[s, 2], 0, LOCAL, keys(dk_ref, at.a_up), k_far.at[s, 0])
        kr2 = go(k_far.at[s, 2], k_in.at[s, 0], at.right)
        kl0.wait_recv()
        add(k_far.at[s, 3], 0, LOCAL, keys(dv_ref, at.a_down), k_far.at[s, 1])
        kl2 = go(k_far.at[s, 3], v_in.at[s, 1], at.left)
        yield
        for copy in (qu1, ql1, qu2, ql2):
            copy.wait_recv()
        leave(gq_ref, s, SCALE, q_all.at[s, 3], q_in.at[s, 0], q_in.at[s, 1])
        yield
        kr1.wait_recv()
        kl2.wait_recv()
        leave(gv_ref, s, 1.0, keys(dv_ref, at.a), v_in.at[s, 0], v_in.at[s, 1])
        kl1.wait_recv()
        kr2.wait_recv()
        leave(gk_ref, s, SCALE, keys(dk_ref, at.a), k_in.at[s, 0], k_in.at[s, 1])

    in_turn(work(0), work(1))
    copies.finish_sends()


def summed(dq, dk, dv):
    grad = jax.ShapeDtypeStruct((ROWS, COLS), BF16)
    block = (LOCAL, BLK, WIDE)
    return pl.pallas_call(
        sum_kernel,
        out_shape=(grad, grad, grad),
        in_specs=[whole(VMEM)] * 3,
        out_specs=(whole(VMEM), whole(VMEM), whole(VMEM)),
        scratch_shapes=[
            VMEM((2, SIDE, *block), BF16),
            VMEM((2, SIDE, *block), BF16),
            VMEM((2, 2, *block), BF16),
            VMEM((2, 2, *block), BF16),
            VMEM((2, 4, *block), BF16),
            VMEM((2, 2, *block), BF16),
            VMEM((2, 2, *block), BF16),
            pltpu.SemaphoreType.DMA((N_SUM,)),
            pltpu.SemaphoreType.DMA((N_SUM,)),
        ],
        compiler_params=pltpu.CompilerParams(
            collective_id=2, has_side_effects=True, vmem_limit_bytes=16 * MIB
        ),
        name="sum_grads",
    )(*pinned(dq, dk, dv))


def per_device(query, key, value, out_grad, links):
    qg, kg, qt, entries = gathered(query, out_grad, key, value, links.T)
    full = joined_stats(partial_stats(entries, qt, kg))
    return summed(*partial_grads(entries, qg, qt, kg, full))


def solution(mesh):
    spec = P("ctx", "head")
    return jax.shard_map(
        per_device,
        mesh=mesh,
        in_specs=(spec, spec, spec, spec, P()),
        out_specs=(spec, spec, spec),
        check_vma=False,
    )
```

```python
import functools

import jax
import jax.numpy as jnp
from jax import lax
from jax.experimental import pallas as pl
from jax.experimental.pallas import tpu as pltpu
from jax.sharding import PartitionSpec as P

HEAD_DIM = 128
BLK = 128
LINKS = 6
HEADS = 2
SIDE = 4
NG = 8
LOCAL = 4
ROWS = 512
COLS = 512
WIDE = HEADS * HEAD_DIM
NQ = 2 * NG * LOCAL
NK = 2 * SIDE * LOCAL
LAST = 63
TILES = (slice(0, HEAD_DIM), slice(HEAD_DIM, WIDE))
STATS_AT_ONCE = 4
GRADS_AT_ONCE = 8
LIST = 256
NEG = -1e30
SCALE = HEAD_DIM**-0.5
LOG2E = 1.4426950408889634
MESH = pl.DeviceIdType.MESH
BF16 = jnp.bfloat16
F32 = jnp.float32
VMEM = pltpu.VMEM
MIB = 1 << 20


def whole(space):
    return pl.BlockSpec(memory_space=space)


def pinned(*arrays):
    return [pltpu.with_memory_space_constraint(array, VMEM) for array in arrays]


def place():
    me = lax.axis_index("ctx")
    return me // 8, (me // 2) % 4, me % 2


class Half:
    def __init__(self, s):
        x, y, c = place()
        self.s, self.c = s, c
        self.a, self.b = (x, y) if s == 0 else (y, x)
        self.g = self.b * 2 + c
        self.a_up, self.a_down, self.a_far = [(self.a + n) % SIDE for n in (1, 3, 2)]
        self.b_up, self.b_down, self.b_far = [(self.b + n) % SIDE for n in (1, 3, 2)]
        self.right, self.left = self.at(self.a_up, self.b, c), self.at(self.a_down, self.b, c)
        self.upper, self.lower = self.at(self.a, self.b_up, c), self.at(self.a, self.b_down, c)
        self.twin = self.at(self.a, self.b, 1 - c)

    def at(self, a, b, c):
        x, y = (a, b) if self.s == 0 else (b, a)
        return ((x * SIDE + y) * 2 + c, lax.axis_index("head"))


def barrier_with(partners):
    sem = pltpu.get_barrier_semaphore()
    for partner in partners:
        pl.semaphore_signal(sem, inc=1, device_id=partner, device_id_type=MESH)
    pl.semaphore_wait(sem, len(partners))


class Copies:
    def __init__(self, send_sem, recv_sem):
        self.send_sem, self.recv_sem, self.made = send_sem, recv_sem, []

    def start(self, src, dst, device):
        n = len(self.made)
        copy = pltpu.make_async_remote_copy(
            src_ref=src,
            dst_ref=dst,
            send_sem=self.send_sem.at[n],
            recv_sem=self.recv_sem.at[n],
            device_id=device,
            device_id_type=MESH,
        )
        copy.start()
        self.made.append(copy)
        return copy

    def finish_sends(self):
        for copy in self.made:
            copy.wait_send()


def nt(a, b):
    return lax.dot_general(a, b, (((1,), (1,)), ((), ())), preferred_element_type=F32)


def nn(a, b):
    return lax.dot_general(a, b, (((1,), (0,)), ((), ())), preferred_element_type=F32)


def tn(a, b):
    return lax.dot_general(a, b, (((0,), (0,)), ((), ())), preferred_element_type=F32)


def in_turn(*works):
    works = list(works)
    while works:
        for work in list(works):
            if next(work, works) is works:
                works.remove(work)


def index_of_holder(block):
    stretch = block // 2
    late = stretch > LAST // 2
    return jnp.where(late, LAST - stretch, stretch), block % 2 + jnp.where(late, 2, 0)


def write_list(links_ref, named_ref, list_ref):
    shape = (8, BLK)
    block = lax.broadcasted_iota(jnp.int32, shape, 1)
    row = lax.broadcasted_iota(jnp.int32, shape, 0)
    named_ref[...] = block - 1
    named_ref[0:LINKS, :] = links_ref[...]
    named = named_ref[...]
    q_dev, q_local = index_of_holder(block)
    k_dev, k_local = index_of_holder(jnp.maximum(named, 0))
    within = jnp.logical_or(row > LINKS, jnp.logical_and(row == LINKS, block % 2 == 1))
    used = jnp.logical_and(named >= 0, jnp.logical_not(within))
    keys = lax.broadcasted_iota(jnp.int32, (BLK, BLK), 0)
    lanes = lax.broadcasted_iota(jnp.int32, (BLK, BLK), 1)
    before = jnp.where(keys < lanes, 1.0, 0.0).astype(BF16)
    out = [jnp.zeros(shape, F32) for _ in range(LIST // BLK)]
    base = jnp.zeros((1, 1), F32)
    for s in range(2):
        half = Half(s)
        q_x, q_y, k_x, k_y = q_dev // 8, (q_dev // 2) % 4, k_dev // 8, (k_dev // 2) % 4
        q_a, q_b = (q_x, q_y) if s == 0 else (q_y, q_x)
        k_a, k_b = (k_x, k_y) if s == 0 else (k_y, k_x)
        meets = jnp.logical_and(q_a == half.a, k_b * 2 + k_dev % 2 == half.g)
        here = jnp.where(jnp.logical_and(used, meets), 1.0, 0.0)
        q_slot = (s * NG + q_b * 2 + q_dev % 2) * LOCAL + q_local
        k_slot = (s * SIDE + k_a) * LOCAL + k_local
        at = base + jnp.sum(nn(here.astype(BF16), before), axis=0, keepdims=True)
        for t in range(LINKS + 1):
            flag = here[t : t + 1, :]
            values = jnp.where(row == 0, q_slot[t : t + 1, :], k_slot[t : t + 1, :]).astype(F32)
            for n in range(LIST // BLK):
                spot = keys.astype(F32) + float(n * BLK)
                hot = jnp.where(spot == at, flag, 0.0).astype(BF16)
                out[n] = out[n] + nt(values.astype(BF16), hot)
            at = at + flag
        base = base + jnp.sum(jnp.sum(here, axis=1, keepdims=True), axis=0, keepdims=True)
    for n in range(LIST // BLK):
        spot = block.astype(F32) + float(n * BLK)
        spare = jnp.where(row == 0, float(NQ), float(NK))
        full = jnp.where(spot < base, out[n], spare)
        list_ref[:, n * BLK : (n + 1) * BLK] = jnp.where(row == 2, base, full).astype(jnp.int32)


class Entry:
    def __init__(self, q_to, k_to, keys, values, queries_t, out_grads_t, causal=False):
        self.q_to, self.k_to, self.keys = q_to, k_to, keys
        self.score = [nn(k, q) * (SCALE * LOG2E) for k, q in zip(keys, queries_t)]
        self.dprob = [nn(v, o) for v, o in zip(values, out_grads_t)]
        if causal:
            down = lax.broadcasted_iota(jnp.int32, (BLK, BLK), 0)
            live = down <= lax.broadcasted_iota(jnp.int32, (BLK, BLK), 1)
            self.score = [jnp.where(live, score, NEG) for score in self.score]


def met(q_slot, k_slot, qt_ref, kg_ref, q_to=None, k_to=None, causal=False):
    keys, values = [[kg_ref[k_slot // LOCAL, n, rows_of(k_slot), tile] for tile in TILES] for n in range(2)]
    turned = [[qt_ref[q_slot, n, tile, :] for tile in TILES] for n in range(2)]
    q_to, k_to = q_slot if q_to is None else q_to, k_slot if k_to is None else k_to
    entry = Entry(q_to, k_to, keys, values, *turned, causal)
    entry.q_slot = q_slot
    return entry


def rows_of(slot):
    return pl.ds(pl.multiple_of(slot % LOCAL * BLK, BLK), BLK)


ITSELF = tuple((n, n) for n in range(LOCAL))
BEFORE = ((1, 0), (3, 2))


def listed_entries(list_ref, qt_ref, kg_ref, at_once, finish):
    def body(n, _):
        entries = []
        for u in range(at_once):
            q_to, k_to = list_ref[0, n * at_once + u], list_ref[1, n * at_once + u]
            entries.append(met(q_to % NQ, k_to % NK, qt_ref, kg_ref, q_to, k_to))
        finish(entries)
        return 0

    lax.fori_loop(0, (list_ref[2, 0] + at_once - 1) // at_once, body, 0)


def add_stats(part_ref, entries):
    found = []
    for e in entries:
        tops = [jnp.max(score, axis=0, keepdims=True) for score in e.score]
        probs = [jnp.exp2(score - top) for score, top in zip(e.score, tops)]
        sums = [jnp.sum(prob, axis=0, keepdims=True) for prob in probs]
        dots = [jnp.sum(p * d, axis=0, keepdims=True) for p, d in zip(probs, e.dprob)]
        found.append([jnp.concatenate(rows, axis=0) for rows in (tops, sums, dots)])
    for e, (top, total, dot) in zip(entries, found):
        old = part_ref[e.q_to]
        old_top = old[0:HEADS]
        new_top = jnp.maximum(old_top, top)
        was, now = jnp.exp2(old_top - new_top), jnp.exp2(top - new_top)
        part_ref[e.q_to, 0:HEADS, :] = new_top
        part_ref[e.q_to, HEADS : 2 * HEADS, :] = old[HEADS : 2 * HEADS] * was + total * now
        part_ref[e.q_to, 2 * HEADS : 3 * HEADS, :] = old[2 * HEADS : 3 * HEADS] * was + dot * now


def add_grads(dq_ref, dk_ref, dv_ref, stats, queries, out_grads, entries):
    found = []
    for e in entries:
        rows = stats(e)
        dq, dk, dv = [], [], []
        for i in range(HEADS):
            prob = jnp.exp2(e.score[i] - rows[i : i + 1])
            dscore = (prob * (e.dprob[i] - rows[HEADS + i : HEADS + i + 1])).astype(BF16)
            dk.append(nn(dscore, queries(e, i)))
            dv.append(nn(prob.astype(BF16), out_grads(e, i)))
            dq.append(tn(dscore, e.keys[i]))
        found.append([jnp.concatenate(terms, axis=1) for terms in (dq, dk, dv)])
    for e, (dq, dk, dv) in zip(entries, found):
        dq_ref[e.q_to] += dq.astype(dq_ref.dtype)
        dk_ref[e.k_to] += dk.astype(dk_ref.dtype)
        dv_ref[e.k_to] += dv.astype(dv_ref.dtype)


def clear(ref, count):
    def body(n, _):
        ref[n] = jnp.zeros(ref.shape[1:], ref.dtype)
        return 0

    lax.fori_loop(0, count, body, 0)


N_GATHER = 40


def gather_kernel(
    q_ref, o_ref, k_ref, v_ref, links_ref,
    qg_ref, kg_ref, qt_ref, list_ref, part_ref, dq_ref, dk_ref, dv_ref,
    table_ref, named_ref, send_sem, recv_sem, own_sem,
):
    copies = Copies(send_sem, recv_sem)
    go = copies.start
    own = []
    table = pltpu.make_async_copy(links_ref, table_ref, own_sem.at[8])
    table.start()

    def columns(ref, s):
        return ref.at[:, s * WIDE : (s + 1) * WIDE]

    def keep(src, dst):
        copy = pltpu.make_async_copy(src, dst, own_sem.at[len(own)])
        copy.start()
        own.append(copy)

    def turn(g, a):
        def body(lb, _):
            rows = pl.ds(pl.multiple_of(lb * BLK, BLK), BLK)
            for tile in TILES:
                qt_ref[g * LOCAL + lb, a, tile, :] = qg_ref[g, a, rows, tile].T
            return 0

        lax.fori_loop(0, LOCAL, body, 0)

    def work(s):
        at = Half(s)
        ka, qa = s * SIDE + at.a, s * NG + at.g
        q, o, k, v = [columns(ref, s) for ref in (q_ref, o_ref, k_ref, v_ref)]
        keep(q, qg_ref.at[qa, 0])
        keep(o, qg_ref.at[qa, 1])
        keep(k, kg_ref.at[ka, 0])
        keep(v, kg_ref.at[ka, 1])
        if s == 0:
            barrier_with([at.right, at.left, at.upper, at.lower, at.twin])
        yield
        qu0 = go(q, qg_ref.at[qa, 0], at.upper)
        ql1 = go(o, qg_ref.at[qa, 1], at.lower)
        yield
        kr0 = go(k, kg_ref.at[ka, 0], at.right)
        kl1 = go(v, kg_ref.at[ka, 1], at.left)
        yield
        qu1 = go(o, qg_ref.at[qa, 1], at.upper)
        ql0 = go(q, qg_ref.at[qa, 0], at.lower)
        yield
        kr1 = go(v, kg_ref.at[ka, 1], at.right)
        kl0 = go(k, kg_ref.at[ka, 0], at.left)
        tq, to = go(q, qg_ref.at[qa, 0], at.twin), go(o, qg_ref.at[qa, 1], at.twin)
        yield
        if s == 0:
            table.wait()
            write_list(table_ref, named_ref, list_ref)
            part_ref[:, 0:HEADS, :] = jnp.full((NQ + 1, HEADS, BLK), NEG, F32)
            part_ref[:, HEADS:8, :] = jnp.zeros((NQ + 1, 8 - HEADS, BLK), F32)
        for copy in own[4 * s : 4 * s + 4]:
            copy.wait()
        turn(qa, 0)
        turn(qa, 1)
        yield
        for pairs in (ITSELF, BEFORE):
            meet = functools.partial(met, qt_ref=qt_ref, kg_ref=kg_ref, causal=pairs is ITSELF)
            add_stats(part_ref, [meet(qa * LOCAL + m, ka * LOCAL + n) for m, n in pairs])
        if s == 0:
            clear(dq_ref, NQ + 1)
        else:
            clear(dk_ref, NK + 1)
            clear(dv_ref, NK + 1)
        yield

        def on(b, a, device):
            slot = qg_ref.at[s * NG + b * 2 + at.c, a]
            return go(slot, slot, device)

        def mine(b):
            return s * NG + b * 2 + at.c

        def other(b):
            return s * NG + b * 2 + 1 - at.c

        k_down, k_up = kg_ref.at[s * SIDE + at.a_down, 0], kg_ref.at[s * SIDE + at.a_up, 1]
        qu0.wait_recv()
        qu2 = on(at.b_down, 0, at.upper)
        td0 = on(at.b_down, 0, at.twin)
        ql1.wait_recv()
        ql2 = on(at.b_up, 1, at.lower)
        tu1 = on(at.b_up, 1, at.twin)
        yield
        kr0.wait_recv()
        kr2 = go(k_down, k_down, at.right)
        kl1.wait_recv()
        kl2 = go(k_up, k_up, at.left)
        yield
        turn(mine(at.b_down), 0)
        turn(mine(at.b_up), 1)
        tq.wait_recv()
        turn(other(at.b), 0)
        to.wait_recv()
        turn(other(at.b), 1)
        yield
        qu1.wait_recv()
        td1 = on(at.b_down, 1, at.twin)
        ql0.wait_recv()
        tu0 = on(at.b_up, 0, at.twin)
        yield
        turn(mine(at.b_down), 1)
        turn(mine(at.b_up), 0)
        td0.wait_recv()
        turn(other(at.b_down), 0)
        tu1.wait_recv()
        turn(other(at.b_up), 1)
        yield
        td1.wait_recv()
        turn(other(at.b_down), 1)
        tu0.wait_recv()
        turn(other(at.b_up), 0)
        yield
        qu2.wait_recv()
        tf0 = on(at.b_far, 0, at.twin)
        ql2.wait_recv()
        tf1 = on(at.b_far, 1, at.twin)
        yield
        turn(mine(at.b_far), 0)
        turn(mine(at.b_far), 1)
        yield
        tf0.wait_recv()
        turn(other(at.b_far), 0)
        tf1.wait_recv()
        turn(other(at.b_far), 1)
        for copy in (kr1, kl0, kr2, kl2):
            copy.wait_recv()

    in_turn(work(0), work(1))
    copies.finish_sends()


def gathered(query, out_grad, key, value, links):
    return pl.pallas_call(
        gather_kernel,
        out_shape=(
            VMEM((2 * NG, 2, ROWS, WIDE), BF16),
            VMEM((2 * SIDE, 2, ROWS, WIDE), BF16),
            VMEM((NQ, 2, WIDE, BLK), BF16),
            VMEM((8, LIST), jnp.int32),
            VMEM((NQ + 1, 8, BLK), F32),
            VMEM((NQ + 1, BLK, WIDE), BF16),
            VMEM((NK + 1, BLK, WIDE), BF16),
            VMEM((NK + 1, BLK, WIDE), BF16),
        ),
        in_specs=[whole(pltpu.HBM)] * 5,
        out_specs=(whole(VMEM),) * 8,
        scratch_shapes=[
            VMEM((LINKS, BLK), jnp.int32),
            VMEM((8, BLK), jnp.int32),
            pltpu.SemaphoreType.DMA((N_GATHER,)),
            pltpu.SemaphoreType.DMA((N_GATHER,)),
            pltpu.SemaphoreType.DMA((9,)),
        ],
        compiler_params=pltpu.CompilerParams(
            collective_id=0, has_side_effects=True, vmem_limit_bytes=8 * MIB
        ),
        name="gather",
    )(query, out_grad, key, value, pltpu.with_memory_space_constraint(links, pltpu.HBM))


def stats_kernel(list_ref, qt_ref, kg_ref, first_ref, part_ref):
    del first_ref
    listed_entries(list_ref, qt_ref, kg_ref, STATS_AT_ONCE, functools.partial(add_stats, part_ref))


def partial_stats(entries, qt, kg, part):
    return pl.pallas_call(
        stats_kernel,
        out_shape=VMEM((NQ + 1, 8, BLK), F32),
        in_specs=[whole(pltpu.SMEM)] + [whole(VMEM)] * 3,
        out_specs=whole(VMEM),
        input_output_aliases={3: 0},
        compiler_params=pltpu.CompilerParams(vmem_limit_bytes=8 * MIB),
        name="partial_stats",
    )(entries, *pinned(qt, kg, part))


def merged(parts):
    tops = [part[:, 0:HEADS, :] for part in parts]
    top = functools.reduce(jnp.maximum, tops)
    weights = [jnp.exp2(t - top) for t in tops]
    total = sum(part[:, HEADS : 2 * HEADS, :] * w for part, w in zip(parts, weights))
    dot = sum(part[:, 2 * HEADS : 3 * HEADS, :] * w for part, w in zip(parts, weights))
    return top, total, dot


def join_kernel(part_ref, full_ref, got_ref, near_ref, twin_ref, send_sem, recv_sem):
    halves = [Half(0), Half(1)]

    def around(at):
        return [(b, at.at(at.a, b, at.c)) for b in (at.b_up, at.b_down, at.b_far)]

    def chip(at, b):
        return pl.ds((at.s * NG + b * 2) * LOCAL, 2 * LOCAL)

    twin = halves[0].twin
    barrier_with([twin] + [device for at in halves for _, device in around(at)])
    copies = Copies(send_sem, recv_sem)
    first = [
        [copies.start(part_ref.at[chip(at, b)], got_ref.at[at.s, n], device) for n, (b, device) in enumerate(around(at))]
        for at in halves
    ]
    for at in halves:
        for copy in first[at.s]:
            copy.wait_recv()
        got = [part_ref.at[chip(at, at.b)]] + [got_ref.at[at.s, n] for n in range(SIDE - 1)]
        for n, rows in enumerate(merged(got)):
            near_ref[at.s, :, n * HEADS : (n + 1) * HEADS, :] = rows
        near_ref[at.s, :, 3 * HEADS : 8, :] = jnp.zeros((2 * LOCAL, 8 - 3 * HEADS, BLK), F32)
    swap = copies.start(near_ref, twin_ref, twin)
    swap.wait_recv()
    later = []
    for at in halves:
        top, total, dot = merged([near_ref.at[at.s], twin_ref.at[at.s]])
        own = chip(at, at.b)
        full_ref[own, 0:HEADS, :] = top + jnp.log(total) * LOG2E
        full_ref[own, HEADS : 2 * HEADS, :] = dot / total
        full_ref[own, 2 * HEADS : 8, :] = jnp.zeros((2 * LOCAL, 8 - 2 * HEADS, BLK), F32)
        later += [copies.start(full_ref.at[own], full_ref.at[own], device) for _, device in around(at)]
    for copy in later:
        copy.wait_recv()
    copies.finish_sends()


def joined_stats(part):
    return pl.pallas_call(
        join_kernel,
        out_shape=VMEM((NQ, 8, BLK), F32),
        in_specs=[whole(VMEM)],
        out_specs=whole(VMEM),
        scratch_shapes=[
            VMEM((2, SIDE - 1, 2 * LOCAL, 8, BLK), F32),
            VMEM((2, 2 * LOCAL, 8, BLK), F32),
            VMEM((2, 2 * LOCAL, 8, BLK), F32),
            pltpu.SemaphoreType.DMA((13,)),
            pltpu.SemaphoreType.DMA((13,)),
        ],
        compiler_params=pltpu.CompilerParams(
            collective_id=1, has_side_effects=True, vmem_limit_bytes=8 * MIB
        ),
        name="join_stats",
    )(*pinned(part))


def grads_kernel(
    list_ref, qg_ref, qt_ref, kg_ref, full_ref, zero_q, zero_k, zero_v, dq_ref, dk_ref, dv_ref
):
    del zero_q, zero_k, zero_v

    def tiles(n):
        return lambda e, i: qg_ref[e.q_slot // LOCAL, n, rows_of(e.q_slot), TILES[i]]

    finish = functools.partial(
        add_grads, dq_ref, dk_ref, dv_ref, lambda e: full_ref[e.q_slot], tiles(0), tiles(1)
    )
    listed_entries(list_ref, qt_ref, kg_ref, GRADS_AT_ONCE, finish)


def partial_grads(entries, qg, qt, kg, full, dq, dk, dv):
    return pl.pallas_call(
        grads_kernel,
        out_shape=(
            VMEM((NQ + 1, BLK, WIDE), BF16),
            VMEM((NK + 1, BLK, WIDE), BF16),
            VMEM((NK + 1, BLK, WIDE), BF16),
        ),
        in_specs=[whole(pltpu.SMEM)] + [whole(VMEM)] * 7,
        out_specs=(whole(VMEM),) * 3,
        input_output_aliases={5: 0, 6: 1, 7: 2},
        compiler_params=pltpu.CompilerParams(vmem_limit_bytes=8 * MIB),
        name="partial_grads",
    )(entries, *pinned(qg, qt, kg, full, dq, dk, dv))


N_SUM = 32


def add(dst, first, last, *terms):
    def body(n, _):
        total = terms[0][n].astype(F32)
        for term in terms[1:]:
            total = total + term[n].astype(F32)
        dst[n] = total.astype(BF16)
        return 0

    lax.fori_loop(first, last, body, 0)


def leave(dst, s, scale, *terms):
    for n in range(LOCAL):
        total = terms[0][n].astype(F32)
        for term in terms[1:]:
            total = total + term[n].astype(F32)
        dst[n * BLK : (n + 1) * BLK, s * WIDE : (s + 1) * WIDE] = (total * scale).astype(BF16)


def sum_kernel(
    dq_ref, dk_ref, dv_ref, full_ref, q_ref, o_ref, k_ref, v_ref, gq_ref, gk_ref, gv_ref,
    own_ref, own_q, own_k, own_v, twin_buf, q_all, q_far, q_in, k_far, k_in, v_in, send_sem, recv_sem, own_sem,
):
    copies = Copies(send_sem, recv_sem)
    go = copies.start
    low, high = pl.ds(0, 2), pl.ds(2, 2)
    kept = [
        pltpu.make_async_copy(ref, own_ref.at[n], own_sem.at[n])
        for n, ref in enumerate((q_ref, o_ref, k_ref, v_ref))
    ]
    for copy in kept:
        copy.start()

    def own_grads(at, pairs):
        def block(n, lb):
            return [
                own_ref[n, lb * BLK : (lb + 1) * BLK, (at.s * HEADS + i) * HEAD_DIM : (at.s * HEADS + i + 1) * HEAD_DIM]
                for i in range(HEADS)
            ]

        def turned(n, lb):
            return [tile.T for tile in block(n, lb)]

        base = at.s * LOCAL
        entries = []
        for m, n in pairs:
            e = Entry(base + m, base + n, block(2, n), block(3, n), turned(0, m), turned(1, m), pairs is ITSELF)
            e.local = m
            entries.append(e)

        def stats(e):
            return full_ref[(at.s * NG + at.g) * LOCAL + e.local]

        add_grads(
            own_q, own_k, own_v, stats, lambda e, i: block(0, e.local)[i], lambda e, i: block(1, e.local)[i], entries
        )


    def work(s):
        at = Half(s)
        if s == 0:
            barrier_with([at.right, at.left, at.upper, at.lower, at.twin])
        yield

        def mine(ref):
            return ref.at[pl.ds(s * LOCAL, LOCAL)]

        def keys(ref, a):
            return ref.at[pl.ds((s * SIDE + a) * LOCAL, LOCAL)]

        def queries(b, c):
            return dq_ref.at[pl.ds((s * NG + b * 2 + c) * LOCAL, LOCAL)]

        order = (at.b_far, at.b_up, at.b_down, at.b)
        kr0 = go(keys(dk_ref, at.a_far), k_far.at[s, 0], at.right)
        kl0 = go(keys(dv_ref, at.a_far), k_far.at[s, 1], at.left)
        pairs = [go(queries(b, 1 - at.c), twin_buf.at[s, n], at.twin) for n, b in enumerate(order)]
        yield
        kr1 = go(keys(dv_ref, at.a_up), v_in.at[s, 0], at.right)
        kl1 = go(keys(dk_ref, at.a_down), k_in.at[s, 1], at.left)
        yield
        for ref in (own_q, own_k, own_v):
            clear(ref.at[pl.ds(s * LOCAL, LOCAL)], LOCAL)
        if s == 0:
            for copy in kept:
                copy.wait()
        own_grads(at, ITSELF)
        own_grads(at, BEFORE)
        yield

        def take(n):
            pairs[n].wait_recv()
            add(q_all.at[s, n], 0, LOCAL, queries(order[n], at.c), twin_buf.at[s, n])

        take(0)
        qu0 = go(q_all.at[s, 0, low], q_far.at[s, 0, low], at.upper)
        ql0 = go(q_all.at[s, 0, high], q_far.at[s, 0, high], at.lower)
        yield
        take(1)
        qu1 = go(q_all.at[s, 1, high], q_in.at[s, 0, high], at.upper)
        take(2)
        ql1 = go(q_all.at[s, 2, low], q_in.at[s, 1, low], at.lower)
        take(3)
        yield
        qu0.wait_recv()
        add(q_far.at[s, 1], 0, 2, q_all.at[s, 1], q_far.at[s, 0])
        qu2 = go(q_far.at[s, 1, low], q_in.at[s, 0, low], at.upper)
        ql0.wait_recv()
        add(q_far.at[s, 1], 2, LOCAL, q_all.at[s, 2], q_far.at[s, 0])
        ql2 = go(q_far.at[s, 1, high], q_in.at[s, 1, high], at.lower)
        yield
        kr0.wait_recv()
        add(k_far.at[s, 2], 0, LOCAL, keys(dk_ref, at.a_up), k_far.at[s, 0])
        kr2 = go(k_far.at[s, 2], k_in.at[s, 0], at.right)
        kl0.wait_recv()
        add(k_far.at[s, 3], 0, LOCAL, keys(dv_ref, at.a_down), k_far.at[s, 1])
        kl2 = go(k_far.at[s, 3], v_in.at[s, 1], at.left)
        yield
        for copy in (qu1, ql1, qu2, ql2):
            copy.wait_recv()
        leave(gq_ref, s, SCALE, mine(own_q), q_all.at[s, 3], q_in.at[s, 0], q_in.at[s, 1])
        yield
        kr1.wait_recv()
        kl2.wait_recv()
        leave(gv_ref, s, 1.0, mine(own_v), keys(dv_ref, at.a), v_in.at[s, 0], v_in.at[s, 1])
        kl1.wait_recv()
        kr2.wait_recv()
        leave(gk_ref, s, SCALE, mine(own_k), keys(dk_ref, at.a), k_in.at[s, 0], k_in.at[s, 1])

    in_turn(work(0), work(1))
    copies.finish_sends()


def summed(dq, dk, dv, full, *args):
    grad = jax.ShapeDtypeStruct((ROWS, COLS), BF16)
    block = (LOCAL, BLK, WIDE)
    return pl.pallas_call(
        sum_kernel,
        out_shape=(grad, grad, grad),
        in_specs=[whole(VMEM)] * 4 + [whole(pltpu.HBM)] * 4,
        out_specs=(whole(VMEM),) * 3,
        scratch_shapes=[
            VMEM((4, ROWS, COLS), BF16),
            VMEM((2 * LOCAL, BLK, WIDE), F32),
            VMEM((2 * LOCAL, BLK, WIDE), F32),
            VMEM((2 * LOCAL, BLK, WIDE), F32),
            VMEM((2, SIDE, *block), BF16),
            VMEM((2, SIDE, *block), BF16),
            VMEM((2, 2, *block), BF16),
            VMEM((2, 2, *block), BF16),
            VMEM((2, 4, *block), BF16),
            VMEM((2, 2, *block), BF16),
            VMEM((2, 2, *block), BF16),
            pltpu.SemaphoreType.DMA((N_SUM,)),
            pltpu.SemaphoreType.DMA((N_SUM,)),
            pltpu.SemaphoreType.DMA((4,)),
        ],
        compiler_params=pltpu.CompilerParams(
            collective_id=2, has_side_effects=True, vmem_limit_bytes=20 * MIB
        ),
        name="sum_grads",
    )(*pinned(dq, dk, dv, full), *args)


def per_device(query, key, value, out_grad, links):
    args = [pltpu.with_memory_space_constraint(v, pltpu.HBM) for v in (query, out_grad, key, value)]
    qg, kg, qt, entries, part, dq, dk, dv = gathered(*args, links.T)
    full = joined_stats(partial_stats(entries, qt, kg, part))
    dq, dk, dv = partial_grads(entries, qg, qt, kg, full, dq, dk, dv)
    return summed(dq, dk, dv, full, *args)


def solution(mesh):
    spec = P("ctx", "head")
    return jax.shard_map(
        per_device,
        mesh=mesh,
        in_specs=(spec, spec, spec, spec, P()),
        out_specs=(spec, spec, spec),
        check_vma=False,
    )
```

```python
import functools

import jax
import jax.numpy as jnp
from jax import lax
from jax.experimental import pallas as pl
from jax.experimental.pallas import tpu as pltpu
from jax.sharding import PartitionSpec as P

HEAD_DIM = 128
BLK = 128
LINKS = 6
HEADS = 2
SIDE = 4
NG = 8
LOCAL = 4
ROWS = 512
COLS = 512
WIDE = HEADS * HEAD_DIM
NQ = 2 * NG * LOCAL
NK = 2 * SIDE * LOCAL
TURNED = 2 * WIDE
LAST = 63
TILES = (slice(0, HEAD_DIM), slice(HEAD_DIM, WIDE))
AT_ONCE = 8
LIST = 256
NEG = -1e30
SCALE = HEAD_DIM**-0.5
LOG2E = 1.4426950408889634
MESH = pl.DeviceIdType.MESH
BF16 = jnp.bfloat16
F32 = jnp.float32
VMEM = pltpu.VMEM
MIB = 1 << 20


def whole(space):
    return pl.BlockSpec(memory_space=space)


def pinned(*arrays):
    return [pltpu.with_memory_space_constraint(array, VMEM) for array in arrays]


def place():
    me = lax.axis_index("ctx")
    return me // 8, (me // 2) % 4, me % 2


class Half:
    def __init__(self, s):
        x, y, c = place()
        self.s, self.c = s, c
        self.a, self.b = (x, y) if s == 0 else (y, x)
        self.g = self.b * 2 + c
        self.a_up, self.a_down, self.a_far = [(self.a + n) % SIDE for n in (1, 3, 2)]
        self.b_up, self.b_down, self.b_far = [(self.b + n) % SIDE for n in (1, 3, 2)]
        self.right, self.left = self.at(self.a_up, self.b, c), self.at(self.a_down, self.b, c)
        self.upper, self.lower = self.at(self.a, self.b_up, c), self.at(self.a, self.b_down, c)
        self.twin = self.at(self.a, self.b, 1 - c)

    def at(self, a, b, c):
        x, y = (a, b) if self.s == 0 else (b, a)
        return ((x * SIDE + y) * 2 + c, lax.axis_index("head"))


def barrier_with(partners):
    sem = pltpu.get_barrier_semaphore()
    for partner in partners:
        pl.semaphore_signal(sem, inc=1, device_id=partner, device_id_type=MESH)
    pl.semaphore_wait(sem, len(partners))


class Copies:
    def __init__(self, send_sem, recv_sem):
        self.send_sem, self.recv_sem, self.made = send_sem, recv_sem, []

    def start(self, src, dst, device):
        n = len(self.made)
        copy = pltpu.make_async_remote_copy(
            src_ref=src,
            dst_ref=dst,
            send_sem=self.send_sem.at[n],
            recv_sem=self.recv_sem.at[n],
            device_id=device,
            device_id_type=MESH,
        )
        copy.start()
        self.made.append(copy)
        return copy

    def finish_sends(self):
        for copy in self.made:
            copy.wait_send()


def nt(a, b):
    return lax.dot_general(a, b, (((1,), (1,)), ((), ())), preferred_element_type=F32)


def nn(a, b):
    return lax.dot_general(a, b, (((1,), (0,)), ((), ())), preferred_element_type=F32)


def tn(a, b):
    return lax.dot_general(a, b, (((0,), (0,)), ((), ())), preferred_element_type=F32)


def in_turn(*works):
    works = list(works)
    while works:
        for work in list(works):
            if next(work, works) is works:
                works.remove(work)


def index_of_holder(block):
    stretch = block // 2
    late = stretch > LAST // 2
    return jnp.where(late, LAST - stretch, stretch), block % 2 + jnp.where(late, 2, 0)


def write_list(links_ref, named_ref, list_ref):
    shape = (8, BLK)
    block = lax.broadcasted_iota(jnp.int32, shape, 1)
    row = lax.broadcasted_iota(jnp.int32, shape, 0)
    named_ref[...] = block - 1
    named_ref[0:LINKS, :] = links_ref[...]
    named = named_ref[...]
    q_dev, q_local = index_of_holder(block)
    k_dev, k_local = index_of_holder(jnp.maximum(named, 0))
    within = jnp.logical_or(row > LINKS, jnp.logical_and(row == LINKS, block % 2 == 1))
    used = jnp.logical_and(named >= 0, jnp.logical_not(within))
    keys = lax.broadcasted_iota(jnp.int32, (BLK, BLK), 0)
    lanes = lax.broadcasted_iota(jnp.int32, (BLK, BLK), 1)
    before = jnp.where(keys < lanes, 1.0, 0.0).astype(BF16)
    out = [jnp.zeros(shape, F32) for _ in range(LIST // BLK)]
    base = jnp.zeros((1, 1), F32)
    for s in range(2):
        half = Half(s)
        q_x, q_y, k_x, k_y = q_dev // 8, (q_dev // 2) % 4, k_dev // 8, (k_dev // 2) % 4
        q_a, q_b = (q_x, q_y) if s == 0 else (q_y, q_x)
        k_a, k_b = (k_x, k_y) if s == 0 else (k_y, k_x)
        meets = jnp.logical_and(q_a == half.a, k_b * 2 + k_dev % 2 == half.g)
        here = jnp.where(jnp.logical_and(used, meets), 1.0, 0.0)
        q_slot = (s * NG + q_b * 2 + q_dev % 2) * LOCAL + q_local
        k_slot = (s * SIDE + k_a) * LOCAL + k_local
        at = base + jnp.sum(nn(here.astype(BF16), before), axis=0, keepdims=True)
        for t in range(LINKS + 1):
            flag = here[t : t + 1, :]
            values = jnp.where(row == 0, q_slot[t : t + 1, :], k_slot[t : t + 1, :]).astype(F32)
            for n in range(LIST // BLK):
                spot = keys.astype(F32) + float(n * BLK)
                hot = jnp.where(spot == at, flag, 0.0).astype(BF16)
                out[n] = out[n] + nt(values.astype(BF16), hot)
            at = at + flag
        base = base + jnp.sum(jnp.sum(here, axis=1, keepdims=True), axis=0, keepdims=True)
    for n in range(LIST // BLK):
        spot = block.astype(F32) + float(n * BLK)
        spare = jnp.where(row == 0, float(NQ), float(NK))
        full = jnp.where(row == 2, base, jnp.where(spot < base, out[n], spare)).astype(jnp.int32)
        q, k = jnp.bitwise_and(full[0:1, :], NQ - 1), jnp.bitwise_and(full[1:2, :], NK - 1)
        for at_row, values in ((3, first_row(k)), (4, q * TURNED), (5, first_row(q))):
            full = jnp.where(row == at_row, values, full)
        list_ref[:, n * BLK : (n + 1) * BLK] = full


def first_row(slot):
    return slot // LOCAL * (2 * ROWS) + slot % LOCAL * BLK


def rows(first, count=BLK):
    return pl.ds(pl.multiple_of(first, BLK), count)


class Entry:
    def __init__(self, q_to, k_to, keys, values, queries_t, out_grads_t, causal=False):
        self.q_to, self.k_to, self.keys = q_to, k_to, keys
        self.score = [nn(k, q) * (SCALE * LOG2E) for k, q in zip(keys, queries_t)]
        self.dprob = [nn(v, o) for v, o in zip(values, out_grads_t)]
        if causal:
            down = lax.broadcasted_iota(jnp.int32, (BLK, BLK), 0)
            live = down <= lax.broadcasted_iota(jnp.int32, (BLK, BLK), 1)
            self.score = [jnp.where(live, score, NEG) for score in self.score]


def met(q_to, k_to, k_row, turned_row, qt_ref, kg_ref, causal=False):
    keys, values = [[kg_ref[rows(k_row + n * ROWS), tile] for tile in TILES] for n in range(2)]
    turned = [[qt_ref[rows(turned_row + n * WIDE + tile.start), :] for tile in TILES] for n in range(2)]
    return Entry(q_to, k_to, keys, values, *turned, causal)


ITSELF = tuple((n, n) for n in range(LOCAL))
BEFORE = ((1, 0), (3, 2))


def listed_entries(list_ref, qt_ref, kg_ref, finish):
    def body(n, _):
        entries = []
        for at in [n * AT_ONCE + u for u in range(AT_ONCE)]:
            q_to, k_to, _, k_row, turned_row, q_row = [list_ref[m, at] for m in range(6)]
            e = met(q_to, k_to, k_row, turned_row, qt_ref, kg_ref)
            e.q_row = q_row
            entries.append(e)
        finish(entries)
        return 0

    lax.fori_loop(0, lax.div(list_ref[2, 0] + (AT_ONCE - 1), AT_ONCE), body, 0)


def add_stats(part_ref, entries):
    found = []
    for e in entries:
        tops = [jnp.max(score, axis=0, keepdims=True) for score in e.score]
        probs = [jnp.exp2(score - top) for score, top in zip(e.score, tops)]
        sums = [jnp.sum(prob, axis=0, keepdims=True) for prob in probs]
        dots = [jnp.sum(p * d, axis=0, keepdims=True) for p, d in zip(probs, e.dprob)]
        found.append([jnp.concatenate(lines, axis=0) for lines in (tops, sums, dots)])
    for e, (top, total, dot) in zip(entries, found):
        old = part_ref[e.q_to]
        old_top = old[0:HEADS]
        new_top = jnp.maximum(old_top, top)
        was, now = jnp.exp2(old_top - new_top), jnp.exp2(top - new_top)
        part_ref[e.q_to, 0:HEADS, :] = new_top
        part_ref[e.q_to, HEADS : 2 * HEADS, :] = old[HEADS : 2 * HEADS] * was + total * now
        part_ref[e.q_to, 2 * HEADS : 3 * HEADS, :] = old[2 * HEADS : 3 * HEADS] * was + dot * now


def add_grads(dq_ref, dk_ref, dv_ref, stats, queries, out_grads, entries):
    found = []
    for e in entries:
        known = stats(e)
        dq, dk, dv = [], [], []
        for i in range(HEADS):
            prob = jnp.exp2(e.score[i] - known[i : i + 1])
            dscore = (prob * (e.dprob[i] - known[HEADS + i : HEADS + i + 1])).astype(BF16)
            dk.append(nn(dscore, queries(e, i)))
            dv.append(nn(prob.astype(BF16), out_grads(e, i)))
            dq.append(tn(dscore, e.keys[i]))
        found.append([jnp.concatenate(terms, axis=1) for terms in (dq, dk, dv)])
    for e, (dq, dk, dv) in zip(entries, found):
        dq_ref[e.q_to] += dq.astype(dq_ref.dtype)
        dk_ref[e.k_to] += dk.astype(dk_ref.dtype)
        dv_ref[e.k_to] += dv.astype(dv_ref.dtype)


def clear(ref, count):
    def body(n, _):
        ref[n] = jnp.zeros(ref.shape[1:], ref.dtype)
        return 0

    lax.fori_loop(0, count, body, 0)


N_GATHER = 40


def gather_kernel(
    q_ref, o_ref, k_ref, v_ref, links_ref,
    qg_ref, kg_ref, qt_ref, list_ref, part_ref, dq_ref, dk_ref, dv_ref,
    table_ref, named_ref, send_sem, recv_sem, own_sem,
):
    copies = Copies(send_sem, recv_sem)
    go = copies.start
    own = []
    table = pltpu.make_async_copy(links_ref, table_ref, own_sem.at[8])
    table.start()

    def columns(ref, s):
        return ref.at[:, s * WIDE : (s + 1) * WIDE]

    def part(ref, at, n):
        return ref.at[rows((at * 2 + n) * ROWS, ROWS)]

    def keep(src, dst):
        copy = pltpu.make_async_copy(src, dst, own_sem.at[len(own)])
        copy.start()
        own.append(copy)

    def turn(g, a):
        def body(lb, _):
            for tile in TILES:
                turned = (g * LOCAL + lb) * TURNED + a * WIDE + tile.start
                qt_ref[rows(turned), :] = qg_ref[rows((g * 2 + a) * ROWS + lb * BLK), tile].T
            return 0

        lax.fori_loop(0, LOCAL, body, 0)

    def work(s):
        at = Half(s)
        ka, qa = s * SIDE + at.a, s * NG + at.g
        q, o, k, v = [columns(ref, s) for ref in (q_ref, o_ref, k_ref, v_ref)]
        keep(q, part(qg_ref, qa, 0))
        keep(o, part(qg_ref, qa, 1))
        keep(k, part(kg_ref, ka, 0))
        keep(v, part(kg_ref, ka, 1))
        if s == 0:
            barrier_with([at.right, at.left, at.upper, at.lower, at.twin])
        yield
        qu0 = go(q, part(qg_ref, qa, 0), at.upper)
        ql1 = go(o, part(qg_ref, qa, 1), at.lower)
        yield
        kr0 = go(k, part(kg_ref, ka, 0), at.right)
        kl1 = go(v, part(kg_ref, ka, 1), at.left)
        yield
        qu1 = go(o, part(qg_ref, qa, 1), at.upper)
        ql0 = go(q, part(qg_ref, qa, 0), at.lower)
        yield
        kr1 = go(v, part(kg_ref, ka, 1), at.right)
        kl0 = go(k, part(kg_ref, ka, 0), at.left)
        tq, to = go(q, part(qg_ref, qa, 0), at.twin), go(o, part(qg_ref, qa, 1), at.twin)
        yield
        if s == 0:
            table.wait()
            write_list(table_ref, named_ref, list_ref)
            part_ref[:, 0:HEADS, :] = jnp.full((NQ + 1, HEADS, BLK), NEG, F32)
            part_ref[:, HEADS:8, :] = jnp.zeros((NQ + 1, 8 - HEADS, BLK), F32)
        for copy in own[4 * s : 4 * s + 4]:
            copy.wait()
        turn(qa, 0)
        turn(qa, 1)
        yield
        for pairs in (ITSELF, BEFORE):
            entries = []
            for m, n in pairs:
                q_slot, k_slot = qa * LOCAL + m, ka * LOCAL + n
                k_row, turned_row = ka * (2 * ROWS) + n * BLK, q_slot * TURNED
                entries.append(met(q_slot, k_slot, k_row, turned_row, qt_ref, kg_ref, pairs is ITSELF))
            add_stats(part_ref, entries)
        if s == 0:
            clear(dq_ref, NQ + 1)
        else:
            clear(dk_ref, NK + 1)
            clear(dv_ref, NK + 1)
        yield

        def on(b, a, device):
            slot = part(qg_ref, s * NG + b * 2 + at.c, a)
            return go(slot, slot, device)

        def mine(b):
            return s * NG + b * 2 + at.c

        def other(b):
            return s * NG + b * 2 + 1 - at.c

        k_down, k_up = part(kg_ref, s * SIDE + at.a_down, 0), part(kg_ref, s * SIDE + at.a_up, 1)
        qu0.wait_recv()
        qu2 = on(at.b_down, 0, at.upper)
        td0 = on(at.b_down, 0, at.twin)
        ql1.wait_recv()
        ql2 = on(at.b_up, 1, at.lower)
        tu1 = on(at.b_up, 1, at.twin)
        yield
        kr0.wait_recv()
        kr2 = go(k_down, k_down, at.right)
        kl1.wait_recv()
        kl2 = go(k_up, k_up, at.left)
        yield
        turn(mine(at.b_down), 0)
        turn(mine(at.b_up), 1)
        tq.wait_recv()
        turn(other(at.b), 0)
        to.wait_recv()
        turn(other(at.b), 1)
        yield
        qu1.wait_recv()
        td1 = on(at.b_down, 1, at.twin)
        ql0.wait_recv()
        tu0 = on(at.b_up, 0, at.twin)
        yield
        turn(mine(at.b_down), 1)
        turn(mine(at.b_up), 0)
        td0.wait_recv()
        turn(other(at.b_down), 0)
        tu1.wait_recv()
        turn(other(at.b_up), 1)
        yield
        td1.wait_recv()
        turn(other(at.b_down), 1)
        tu0.wait_recv()
        turn(other(at.b_up), 0)
        yield
        qu2.wait_recv()
        tf0 = on(at.b_far, 0, at.twin)
        ql2.wait_recv()
        tf1 = on(at.b_far, 1, at.twin)
        yield
        turn(mine(at.b_far), 0)
        turn(mine(at.b_far), 1)
        yield
        tf0.wait_recv()
        turn(other(at.b_far), 0)
        tf1.wait_recv()
        turn(other(at.b_far), 1)
        for copy in (kr1, kl0, kr2, kl2):
            copy.wait_recv()

    in_turn(work(0), work(1))
    copies.finish_sends()


def gathered(query, out_grad, key, value, links):
    return pl.pallas_call(
        gather_kernel,
        out_shape=(
            VMEM((2 * NG * 2 * ROWS, WIDE), BF16),
            VMEM((2 * SIDE * 2 * ROWS, WIDE), BF16),
            VMEM((NQ * TURNED, BLK), BF16),
            VMEM((8, LIST), jnp.int32),
            VMEM((NQ + 1, 8, BLK), F32),
            VMEM((NQ + 1, BLK, WIDE), BF16),
            VMEM((NK + 1, BLK, WIDE), BF16),
            VMEM((NK + 1, BLK, WIDE), BF16),
        ),
        in_specs=[whole(pltpu.HBM)] * 5,
        out_specs=(whole(VMEM),) * 8,
        scratch_shapes=[
            VMEM((LINKS, BLK), jnp.int32),
            VMEM((8, BLK), jnp.int32),
            pltpu.SemaphoreType.DMA((N_GATHER,)),
            pltpu.SemaphoreType.DMA((N_GATHER,)),
            pltpu.SemaphoreType.DMA((9,)),
        ],
        compiler_params=pltpu.CompilerParams(
            collective_id=0, has_side_effects=True, vmem_limit_bytes=8 * MIB
        ),
        name="gather",
    )(query, out_grad, key, value, pltpu.with_memory_space_constraint(links, pltpu.HBM))


def stats_kernel(list_ref, qt_ref, kg_ref, first_ref, part_ref):
    del first_ref
    listed_entries(list_ref, qt_ref, kg_ref, functools.partial(add_stats, part_ref))


def partial_stats(entries, qt, kg, part):
    return pl.pallas_call(
        stats_kernel,
        out_shape=VMEM((NQ + 1, 8, BLK), F32),
        in_specs=[whole(pltpu.SMEM)] + [whole(VMEM)] * 3,
        out_specs=whole(VMEM),
        input_output_aliases={3: 0},
        compiler_params=pltpu.CompilerParams(vmem_limit_bytes=8 * MIB),
        name="partial_stats",
    )(entries, *pinned(qt, kg, part))


def merged(parts):
    tops = [part[:, 0:HEADS, :] for part in parts]
    top = functools.reduce(jnp.maximum, tops)
    weights = [jnp.exp2(t - top) for t in tops]
    total = sum(part[:, HEADS : 2 * HEADS, :] * w for part, w in zip(parts, weights))
    dot = sum(part[:, 2 * HEADS : 3 * HEADS, :] * w for part, w in zip(parts, weights))
    return top, total, dot


def join_kernel(part_ref, full_ref, got_ref, near_ref, twin_ref, send_sem, recv_sem):
    halves = [Half(0), Half(1)]

    def around(at):
        return [(b, at.at(at.a, b, at.c)) for b in (at.b_up, at.b_down, at.b_far)]

    def chip(at, b):
        return pl.ds((at.s * NG + b * 2) * LOCAL, 2 * LOCAL)

    twin, three, two = halves[0].twin, pl.ds(0, 3 * HEADS), pl.ds(0, 2 * HEADS)
    barrier_with([twin] + [device for at in halves for _, device in around(at)])
    copies = Copies(send_sem, recv_sem)
    first = [
        [
            copies.start(part_ref.at[chip(at, b), three], got_ref.at[at.s, n, :, three], device)
            for n, (b, device) in enumerate(around(at))
        ]
        for at in halves
    ]
    for at in halves:
        for copy in first[at.s]:
            copy.wait_recv()
        got = [part_ref.at[chip(at, at.b)]] + [got_ref.at[at.s, n] for n in range(SIDE - 1)]
        for n, line in enumerate(merged(got)):
            near_ref[at.s, :, n * HEADS : (n + 1) * HEADS, :] = line
    swap = copies.start(near_ref.at[:, :, three], twin_ref.at[:, :, three], twin)
    swap.wait_recv()
    later = []
    for at in halves:
        top, total, dot = merged([near_ref.at[at.s], twin_ref.at[at.s]])
        own = chip(at, at.b)
        full_ref[own, 0:HEADS, :] = top + jnp.log(total) * LOG2E
        full_ref[own, HEADS : 2 * HEADS, :] = dot / total
        for _, device in around(at):
            later.append(copies.start(full_ref.at[own, two], full_ref.at[own, two], device))
    for copy in later:
        copy.wait_recv()
    copies.finish_sends()


def joined_stats(part):
    return pl.pallas_call(
        join_kernel,
        out_shape=VMEM((NQ, 8, BLK), F32),
        in_specs=[whole(VMEM)],
        out_specs=whole(VMEM),
        scratch_shapes=[
            VMEM((2, SIDE - 1, 2 * LOCAL, 8, BLK), F32),
            VMEM((2, 2 * LOCAL, 8, BLK), F32),
            VMEM((2, 2 * LOCAL, 8, BLK), F32),
            pltpu.SemaphoreType.DMA((13,)),
            pltpu.SemaphoreType.DMA((13,)),
        ],
        compiler_params=pltpu.CompilerParams(
            collective_id=1, has_side_effects=True, vmem_limit_bytes=8 * MIB
        ),
        name="join_stats",
    )(*pinned(part))


def grads_kernel(
    list_ref, qg_ref, qt_ref, kg_ref, full_ref, zero_q, zero_k, zero_v, dq_ref, dk_ref, dv_ref
):
    del zero_q, zero_k, zero_v

    def tiles(n):
        return lambda e, i: qg_ref[rows(e.q_row + n * ROWS), TILES[i]]

    finish = functools.partial(
        add_grads, dq_ref, dk_ref, dv_ref, lambda e: full_ref[jnp.bitwise_and(e.q_to, NQ - 1)], tiles(0), tiles(1)
    )
    listed_entries(list_ref, qt_ref, kg_ref, finish)


def partial_grads(entries, qg, qt, kg, full, dq, dk, dv):
    return pl.pallas_call(
        grads_kernel,
        out_shape=(
            VMEM((NQ + 1, BLK, WIDE), BF16),
            VMEM((NK + 1, BLK, WIDE), BF16),
            VMEM((NK + 1, BLK, WIDE), BF16),
        ),
        in_specs=[whole(pltpu.SMEM)] + [whole(VMEM)] * 7,
        out_specs=(whole(VMEM),) * 3,
        input_output_aliases={5: 0, 6: 1, 7: 2},
        compiler_params=pltpu.CompilerParams(vmem_limit_bytes=8 * MIB),
        name="partial_grads",
    )(entries, *pinned(qg, qt, kg, full, dq, dk, dv))


N_SUM = 32


def add(dst, first, last, *terms):
    def body(n, _):
        total = terms[0][n].astype(F32)
        for term in terms[1:]:
            total = total + term[n].astype(F32)
        dst[n] = total.astype(BF16)
        return 0

    lax.fori_loop(first, last, body, 0)


def leave(dst, s, scale, *terms):
    for n in range(LOCAL):
        total = terms[0][n].astype(F32)
        for term in terms[1:]:
            total = total + term[n].astype(F32)
        dst[n * BLK : (n + 1) * BLK, s * WIDE : (s + 1) * WIDE] = (total * scale).astype(BF16)


def sum_kernel(
    dq_ref, dk_ref, dv_ref, full_ref, q_ref, o_ref, k_ref, v_ref, gq_ref, gk_ref, gv_ref,
    own_ref, own_q, own_k, own_v, twin_buf, q_all, q_far, q_in, k_far, k_in, v_in, send_sem, recv_sem, own_sem,
):
    copies = Copies(send_sem, recv_sem)
    go = copies.start
    low, high = pl.ds(0, 2), pl.ds(2, 2)
    kept = [
        pltpu.make_async_copy(ref, own_ref.at[n], own_sem.at[n])
        for n, ref in enumerate((q_ref, o_ref, k_ref, v_ref))
    ]
    for copy in kept:
        copy.start()

    def own_grads(at, pairs):
        def block(n, lb):
            return [
                own_ref[n, lb * BLK : (lb + 1) * BLK, (at.s * HEADS + i) * HEAD_DIM : (at.s * HEADS + i + 1) * HEAD_DIM]
                for i in range(HEADS)
            ]

        def turned(n, lb):
            return [tile.T for tile in block(n, lb)]

        base = at.s * LOCAL
        entries = []
        for m, n in pairs:
            e = Entry(base + m, base + n, block(2, n), block(3, n), turned(0, m), turned(1, m), pairs is ITSELF)
            e.local = m
            entries.append(e)

        def stats(e):
            return full_ref[(at.s * NG + at.g) * LOCAL + e.local]

        add_grads(
            own_q, own_k, own_v, stats, lambda e, i: block(0, e.local)[i], lambda e, i: block(1, e.local)[i], entries
        )


    def work(s):
        at = Half(s)
        if s == 0:
            barrier_with([at.right, at.left, at.upper, at.lower, at.twin])
        yield

        def mine(ref):
            return ref.at[pl.ds(s * LOCAL, LOCAL)]

        def keys(ref, a):
            return ref.at[pl.ds((s * SIDE + a) * LOCAL, LOCAL)]

        def queries(b, c):
            return dq_ref.at[pl.ds((s * NG + b * 2 + c) * LOCAL, LOCAL)]

        order = (at.b_far, at.b_up, at.b_down, at.b)
        kr0 = go(keys(dk_ref, at.a_far), k_far.at[s, 0], at.right)
        kl0 = go(keys(dv_ref, at.a_far), k_far.at[s, 1], at.left)
        pairs = [go(queries(b, 1 - at.c), twin_buf.at[s, n], at.twin) for n, b in enumerate(order)]
        yield
        kr1 = go(keys(dv_ref, at.a_up), v_in.at[s, 0], at.right)
        kl1 = go(keys(dk_ref, at.a_down), k_in.at[s, 1], at.left)
        yield
        for ref in (own_q, own_k, own_v):
            clear(ref.at[pl.ds(s * LOCAL, LOCAL)], LOCAL)
        if s == 0:
            for copy in kept:
                copy.wait()
        own_grads(at, ITSELF)
        own_grads(at, BEFORE)
        yield

        def take(n):
            pairs[n].wait_recv()
            add(q_all.at[s, n], 0, LOCAL, queries(order[n], at.c), twin_buf.at[s, n])

        take(0)
        qu0 = go(q_all.at[s, 0, low], q_far.at[s, 0, low], at.upper)
        ql0 = go(q_all.at[s, 0, high], q_far.at[s, 0, high], at.lower)
        yield
        take(1)
        qu1 = go(q_all.at[s, 1, high], q_in.at[s, 0, high], at.upper)
        take(2)
        ql1 = go(q_all.at[s, 2, low], q_in.at[s, 1, low], at.lower)
        take(3)
        yield
        qu0.wait_recv()
        add(q_far.at[s, 1], 0, 2, q_all.at[s, 1], q_far.at[s, 0])
        qu2 = go(q_far.at[s, 1, low], q_in.at[s, 0, low], at.upper)
        ql0.wait_recv()
        add(q_far.at[s, 1], 2, LOCAL, q_all.at[s, 2], q_far.at[s, 0])
        ql2 = go(q_far.at[s, 1, high], q_in.at[s, 1, high], at.lower)
        yield
        kr0.wait_recv()
        add(k_far.at[s, 2], 0, LOCAL, keys(dk_ref, at.a_up), k_far.at[s, 0])
        kr2 = go(k_far.at[s, 2], k_in.at[s, 0], at.right)
        kl0.wait_recv()
        add(k_far.at[s, 3], 0, LOCAL, keys(dv_ref, at.a_down), k_far.at[s, 1])
        kl2 = go(k_far.at[s, 3], v_in.at[s, 1], at.left)
        yield
        for copy in (qu1, ql1, qu2, ql2):
            copy.wait_recv()
        leave(gq_ref, s, SCALE, mine(own_q), q_all.at[s, 3], q_in.at[s, 0], q_in.at[s, 1])
        yield
        kr1.wait_recv()
        kl2.wait_recv()
        leave(gv_ref, s, 1.0, mine(own_v), keys(dv_ref, at.a), v_in.at[s, 0], v_in.at[s, 1])
        kl1.wait_recv()
        kr2.wait_recv()
        leave(gk_ref, s, SCALE, mine(own_k), keys(dk_ref, at.a), k_in.at[s, 0], k_in.at[s, 1])

    in_turn(work(0), work(1))
    copies.finish_sends()


def summed(dq, dk, dv, full, *args):
    grad = jax.ShapeDtypeStruct((ROWS, COLS), BF16)
    block = (LOCAL, BLK, WIDE)
    return pl.pallas_call(
        sum_kernel,
        out_shape=(grad, grad, grad),
        in_specs=[whole(VMEM)] * 4 + [whole(pltpu.HBM)] * 4,
        out_specs=(whole(VMEM),) * 3,
        scratch_shapes=[
            VMEM((4, ROWS, COLS), BF16),
            VMEM((2 * LOCAL, BLK, WIDE), F32),
            VMEM((2 * LOCAL, BLK, WIDE), F32),
            VMEM((2 * LOCAL, BLK, WIDE), F32),
            VMEM((2, SIDE, *block), BF16),
            VMEM((2, SIDE, *block), BF16),
            VMEM((2, 2, *block), BF16),
            VMEM((2, 2, *block), BF16),
            VMEM((2, 4, *block), BF16),
            VMEM((2, 2, *block), BF16),
            VMEM((2, 2, *block), BF16),
            pltpu.SemaphoreType.DMA((N_SUM,)),
            pltpu.SemaphoreType.DMA((N_SUM,)),
            pltpu.SemaphoreType.DMA((4,)),
        ],
        compiler_params=pltpu.CompilerParams(
            collective_id=2, has_side_effects=True, vmem_limit_bytes=20 * MIB
        ),
        name="sum_grads",
    )(*pinned(dq, dk, dv, full), *args)


def leave_kernel(*refs):
    *ins_and_outs, sem = refs
    copies = [pltpu.make_async_copy(ins_and_outs[n], ins_and_outs[n + 3], sem.at[n]) for n in range(3)]
    for copy in copies:
        copy.start()
    for copy in copies:
        copy.wait()


def left(*grads):
    return pl.pallas_call(
        leave_kernel,
        out_shape=(pltpu.HBM((ROWS, COLS), BF16),) * 3,
        in_specs=[whole(VMEM)] * 3,
        out_specs=(whole(pltpu.HBM),) * 3,
        scratch_shapes=[pltpu.SemaphoreType.DMA((3,))],
        compiler_params=pltpu.CompilerParams(vmem_limit_bytes=4 * MIB),
        name="leave",
    )(*pinned(*grads))


def per_device(query, key, value, out_grad, links):
    args = [pltpu.with_memory_space_constraint(v, pltpu.HBM) for v in (query, out_grad, key, value)]
    qg, kg, qt, entries, part, dq, dk, dv = gathered(*args, links.T)
    full = joined_stats(partial_stats(entries, qt, kg, part))
    dq, dk, dv = partial_grads(entries, qg, qt, kg, full, dq, dk, dv)
    return left(*summed(dq, dk, dv, full, *args))


def solution(mesh):
    spec = P("ctx", "head")
    return jax.shard_map(
        per_device,
        mesh=mesh,
        in_specs=(spec, spec, spec, spec, P()),
        out_specs=(spec, spec, spec),
        check_vma=False,
    )
```

```python
import functools

import jax
import jax.numpy as jnp
from jax import lax
from jax.experimental import pallas as pl
from jax.experimental.pallas import tpu as pltpu
from jax.sharding import PartitionSpec as P

HEAD_DIM = 128
BLK = 128
LINKS = 6
HEADS = 2
SIDE = 4
NG = 8
LOCAL = 4
ROWS = 512
COLS = 512
WIDE = HEADS * HEAD_DIM
NQ = 2 * NG * LOCAL
NK = 2 * SIDE * LOCAL
TURNED = 2 * WIDE
CHIPS = 2 * SIDE
LINES = 2 * LOCAL * HEADS
LAST = 63
TILES = (slice(0, HEAD_DIM), slice(HEAD_DIM, WIDE))
MANY = 16
FEW = 8
LIST = 256
NEG = -1e30
SCALE = HEAD_DIM**-0.5
LOG2E = 1.4426950408889634
MESH = pl.DeviceIdType.MESH
BF16 = jnp.bfloat16
F32 = jnp.float32
VMEM = pltpu.VMEM
MIB = 1 << 20


def whole(space):
    return pl.BlockSpec(memory_space=space)


def pinned(*arrays):
    return [pltpu.with_memory_space_constraint(array, VMEM) for array in arrays]


def place():
    me = lax.axis_index("ctx")
    return me // 8, (me // 2) % 4, me % 2


class Half:
    def __init__(self, s):
        x, y, c = place()
        self.s, self.c = s, c
        self.a, self.b = (x, y) if s == 0 else (y, x)
        self.g = self.b * 2 + c
        self.a_up, self.a_down, self.a_far = [(self.a + n) % SIDE for n in (1, 3, 2)]
        self.b_up, self.b_down, self.b_far = [(self.b + n) % SIDE for n in (1, 3, 2)]
        self.right, self.left = self.at(self.a_up, self.b, c), self.at(self.a_down, self.b, c)
        self.upper, self.lower = self.at(self.a, self.b_up, c), self.at(self.a, self.b_down, c)
        self.twin = self.at(self.a, self.b, 1 - c)

    def at(self, a, b, c):
        x, y = (a, b) if self.s == 0 else (b, a)
        return ((x * SIDE + y) * 2 + c, lax.axis_index("head"))


def barrier_with(partners):
    sem = pltpu.get_barrier_semaphore()
    for partner in partners:
        pl.semaphore_signal(sem, inc=1, device_id=partner, device_id_type=MESH)
    pl.semaphore_wait(sem, len(partners))


class Copies:
    def __init__(self, send_sem, recv_sem):
        self.send_sem, self.recv_sem, self.made = send_sem, recv_sem, []

    def start(self, src, dst, device):
        n = len(self.made)
        copy = pltpu.make_async_remote_copy(
            src_ref=src,
            dst_ref=dst,
            send_sem=self.send_sem.at[n],
            recv_sem=self.recv_sem.at[n],
            device_id=device,
            device_id_type=MESH,
        )
        copy.start()
        self.made.append(copy)
        return copy

    def finish_sends(self):
        for copy in self.made:
            copy.wait_send()


def nt(a, b):
    return lax.dot_general(a, b, (((1,), (1,)), ((), ())), preferred_element_type=F32)


def nn(a, b):
    return lax.dot_general(a, b, (((1,), (0,)), ((), ())), preferred_element_type=F32)


def tn(a, b):
    return lax.dot_general(a, b, (((0,), (0,)), ((), ())), preferred_element_type=F32)


def in_turn(*works):
    works = list(works)
    while works:
        for work in list(works):
            if next(work, works) is works:
                works.remove(work)


def index_of_holder(block):
    stretch = block // 2
    late = stretch > LAST // 2
    return jnp.where(late, LAST - stretch, stretch), block % 2 + jnp.where(late, 2, 0)


def write_list(links_ref, named_ref, list_ref):
    shape = (8, BLK)
    block = lax.broadcasted_iota(jnp.int32, shape, 1)
    row = lax.broadcasted_iota(jnp.int32, shape, 0)
    named_ref[...] = block - 1
    named_ref[0:LINKS, :] = links_ref[...]
    named = named_ref[...]
    q_dev, q_local = index_of_holder(block)
    k_dev, k_local = index_of_holder(jnp.maximum(named, 0))
    within = jnp.logical_or(row > LINKS, jnp.logical_and(row == LINKS, block % 2 == 1))
    used = jnp.logical_and(named >= 0, jnp.logical_not(within))
    keys = lax.broadcasted_iota(jnp.int32, (BLK, BLK), 0)
    lanes = lax.broadcasted_iota(jnp.int32, (BLK, BLK), 1)
    before = jnp.where(keys < lanes, 1.0, 0.0).astype(BF16)
    out = [jnp.zeros(shape, F32) for _ in range(LIST // BLK)]
    base = jnp.zeros((1, 1), F32)
    for s in range(2):
        half = Half(s)
        q_x, q_y, k_x, k_y = q_dev // 8, (q_dev // 2) % 4, k_dev // 8, (k_dev // 2) % 4
        q_a, q_b = (q_x, q_y) if s == 0 else (q_y, q_x)
        k_a, k_b = (k_x, k_y) if s == 0 else (k_y, k_x)
        meets = jnp.logical_and(q_a == half.a, k_b * 2 + k_dev % 2 == half.g)
        here = jnp.where(jnp.logical_and(used, meets), 1.0, 0.0)
        q_slot = (s * NG + q_b * 2 + q_dev % 2) * LOCAL + q_local
        k_slot = (s * SIDE + k_a) * LOCAL + k_local
        at = base + jnp.sum(nn(here.astype(BF16), before), axis=0, keepdims=True)
        for t in range(LINKS + 1):
            flag = here[t : t + 1, :]
            values = jnp.where(row == 0, q_slot[t : t + 1, :], k_slot[t : t + 1, :]).astype(F32)
            for n in range(LIST // BLK):
                spot = keys.astype(F32) + float(n * BLK)
                hot = jnp.where(spot == at, flag, 0.0).astype(BF16)
                out[n] = out[n] + nt(values.astype(BF16), hot)
            at = at + flag
        base = base + jnp.sum(jnp.sum(here, axis=1, keepdims=True), axis=0, keepdims=True)
    for n in range(LIST // BLK):
        spot = block.astype(F32) + float(n * BLK)
        spare = jnp.where(row == 0, float(NQ), float(NK))
        full = jnp.where(row == 2, base, jnp.where(spot < base, out[n], spare)).astype(jnp.int32)
        q, k = jnp.bitwise_and(full[0:1, :], NQ - 1), jnp.bitwise_and(full[1:2, :], NK - 1)
        for at_row, values in ((3, first_row(k)), (4, q * TURNED), (5, first_row(q))):
            full = jnp.where(row == at_row, values, full)
        list_ref[:, n * BLK : (n + 1) * BLK] = full


def first_row(slot):
    return slot // LOCAL * (2 * ROWS) + slot % LOCAL * BLK


def rows(first, count=BLK):
    return pl.ds(pl.multiple_of(first, BLK), count)


class Entry:
    def __init__(self, q_to, k_to, keys, values, queries_t, out_grads_t, causal=False):
        self.q_to, self.k_to, self.keys = q_to, k_to, keys
        self.score = [nn(k, q) * (SCALE * LOG2E) for k, q in zip(keys, queries_t)]
        self.dprob = [nn(v, o) for v, o in zip(values, out_grads_t)]
        if causal:
            down = lax.broadcasted_iota(jnp.int32, (BLK, BLK), 0)
            live = down <= lax.broadcasted_iota(jnp.int32, (BLK, BLK), 1)
            self.score = [jnp.where(live, score, NEG) for score in self.score]


def met(q_to, k_to, k_row, turned_row, qt_ref, kg_ref, causal=False):
    keys, values = [[kg_ref[rows(k_row + n * ROWS), tile] for tile in TILES] for n in range(2)]
    turned = [[qt_ref[rows(turned_row + n * WIDE + tile.start), :] for tile in TILES] for n in range(2)]
    return Entry(q_to, k_to, keys, values, *turned, causal)


ITSELF = tuple((n, n) for n in range(LOCAL))
BEFORE = ((1, 0), (3, 2))


def listed_entries(list_ref, qt_ref, kg_ref, finish):
    def batch(first, count):
        entries = []
        for at in [first + u for u in range(count)]:
            q_to, k_to, _, k_row, turned_row, q_row = [list_ref[m, at] for m in range(6)]
            e = met(q_to, k_to, k_row, turned_row, qt_ref, kg_ref)
            e.q_row = q_row
            entries.append(e)
        finish(entries)
        return 0

    full = lax.div(list_ref[2, 0], MANY)
    rest = list_ref[2, 0] - full * MANY
    lax.fori_loop(0, full, lambda n, _: batch(n * MANY, MANY), 0)
    lax.fori_loop(0, lax.div(rest + (FEW - 1), FEW), lambda n, _: batch(full * MANY + n * FEW, FEW), 0)


def stats_place(q_slot):
    return lax.div(q_slot, 2 * LOCAL), pl.ds(lax.rem(q_slot, 2 * LOCAL) * HEADS, HEADS)


def add_stats(part_ref, entries):
    found = []
    for e in entries:
        tops = [jnp.max(score, axis=0, keepdims=True) for score in e.score]
        probs = [jnp.exp2(score - top) for score, top in zip(e.score, tops)]
        sums = [jnp.sum(prob, axis=0, keepdims=True) for prob in probs]
        dots = [jnp.sum(p * d, axis=0, keepdims=True) for p, d in zip(probs, e.dprob)]
        found.append([jnp.concatenate(lines, axis=0) for lines in (tops, sums, dots)])
    for e, (top, total, dot) in zip(entries, found):
        chip, lines = stats_place(e.q_to)
        old_top = part_ref[chip, 0, lines, :]
        new_top = jnp.maximum(old_top, top)
        was, now = jnp.exp2(old_top - new_top), jnp.exp2(top - new_top)
        part_ref[chip, 0, lines, :] = new_top
        part_ref[chip, 1, lines, :] = part_ref[chip, 1, lines, :] * was + total * now
        part_ref[chip, 2, lines, :] = part_ref[chip, 2, lines, :] * was + dot * now


def add_grads(dq_ref, dk_ref, dv_ref, full_ref, stats_slot, queries, out_grads, entries):
    found = []
    for e in entries:
        chip, lines = stats_place(stats_slot(e))
        lse, delta = full_ref[chip, 0, lines, :], full_ref[chip, 1, lines, :]
        dq, dk, dv = [], [], []
        for i in range(HEADS):
            prob = jnp.exp2(e.score[i] - lse[i : i + 1])
            dscore = (prob * (e.dprob[i] - delta[i : i + 1])).astype(BF16)
            dk.append(nn(dscore, queries(e, i)))
            dv.append(nn(prob.astype(BF16), out_grads(e, i)))
            dq.append(tn(dscore, e.keys[i]))
        found.append([jnp.concatenate(terms, axis=1) for terms in (dq, dk, dv)])
    for e, (dq, dk, dv) in zip(entries, found):
        dq_ref[e.q_to] += dq.astype(dq_ref.dtype)
        dk_ref[e.k_to] += dk.astype(dk_ref.dtype)
        dv_ref[e.k_to] += dv.astype(dv_ref.dtype)


def clear(ref, count):
    def body(n, _):
        ref[n] = jnp.zeros(ref.shape[1:], ref.dtype)
        return 0

    lax.fori_loop(0, count, body, 0)


N_GATHER = 40


def gather_kernel(
    q_ref, o_ref, k_ref, v_ref, links_ref,
    qg_ref, kg_ref, qt_ref, list_ref, part_ref, dq_ref, dk_ref, dv_ref,
    table_ref, named_ref, send_sem, recv_sem, own_sem,
):
    copies = Copies(send_sem, recv_sem)
    go = copies.start
    own = []
    table = pltpu.make_async_copy(links_ref, table_ref, own_sem.at[8])
    table.start()

    def columns(ref, s):
        return ref.at[:, s * WIDE : (s + 1) * WIDE]

    def part(ref, at, n):
        return ref.at[rows((at * 2 + n) * ROWS, ROWS)]

    def keep(src, dst):
        copy = pltpu.make_async_copy(src, dst, own_sem.at[len(own)])
        copy.start()
        own.append(copy)

    def turn(g, a):
        def body(lb, _):
            for tile in TILES:
                turned = (g * LOCAL + lb) * TURNED + a * WIDE + tile.start
                qt_ref[rows(turned), :] = qg_ref[rows((g * 2 + a) * ROWS + lb * BLK), tile].T
            return 0

        lax.fori_loop(0, LOCAL, body, 0)

    def work(s):
        at = Half(s)
        ka, qa = s * SIDE + at.a, s * NG + at.g
        q, o, k, v = [columns(ref, s) for ref in (q_ref, o_ref, k_ref, v_ref)]
        keep(q, part(qg_ref, qa, 0))
        keep(o, part(qg_ref, qa, 1))
        keep(k, part(kg_ref, ka, 0))
        keep(v, part(kg_ref, ka, 1))
        if s == 0:
            barrier_with([at.right, at.left, at.upper, at.lower, at.twin])
        yield
        qu0 = go(q, part(qg_ref, qa, 0), at.upper)
        ql1 = go(o, part(qg_ref, qa, 1), at.lower)
        yield
        kr0 = go(k, part(kg_ref, ka, 0), at.right)
        kl1 = go(v, part(kg_ref, ka, 1), at.left)
        yield
        qu1 = go(o, part(qg_ref, qa, 1), at.upper)
        ql0 = go(q, part(qg_ref, qa, 0), at.lower)
        yield
        kr1 = go(v, part(kg_ref, ka, 1), at.right)
        kl0 = go(k, part(kg_ref, ka, 0), at.left)
        tq, to = go(q, part(qg_ref, qa, 0), at.twin), go(o, part(qg_ref, qa, 1), at.twin)
        yield
        if s == 0:
            table.wait()
            write_list(table_ref, named_ref, list_ref)
            part_ref[:, 0] = jnp.full((CHIPS + 1, LINES, BLK), NEG, F32)
            part_ref[:, 1:3] = jnp.zeros((CHIPS + 1, 2, LINES, BLK), F32)
        for copy in own[4 * s : 4 * s + 4]:
            copy.wait()
        turn(qa, 0)
        turn(qa, 1)
        yield
        for pairs in (ITSELF, BEFORE):
            entries = []
            for m, n in pairs:
                q_slot, k_slot = qa * LOCAL + m, ka * LOCAL + n
                k_row, turned_row = ka * (2 * ROWS) + n * BLK, q_slot * TURNED
                entries.append(met(q_slot, k_slot, k_row, turned_row, qt_ref, kg_ref, pairs is ITSELF))
            add_stats(part_ref, entries)
        if s == 0:
            clear(dq_ref, NQ + 1)
        else:
            clear(dk_ref, NK + 1)
            clear(dv_ref, NK + 1)
        yield

        def on(b, a, device):
            slot = part(qg_ref, s * NG + b * 2 + at.c, a)
            return go(slot, slot, device)

        def mine(b):
            return s * NG + b * 2 + at.c

        def other(b):
            return s * NG + b * 2 + 1 - at.c

        k_down, k_up = part(kg_ref, s * SIDE + at.a_down, 0), part(kg_ref, s * SIDE + at.a_up, 1)
        qu0.wait_recv()
        qu2 = on(at.b_down, 0, at.upper)
        td0 = on(at.b_down, 0, at.twin)
        ql1.wait_recv()
        ql2 = on(at.b_up, 1, at.lower)
        tu1 = on(at.b_up, 1, at.twin)
        yield
        kr0.wait_recv()
        kr2 = go(k_down, k_down, at.right)
        kl1.wait_recv()
        kl2 = go(k_up, k_up, at.left)
        yield
        turn(mine(at.b_down), 0)
        turn(mine(at.b_up), 1)
        tq.wait_recv()
        turn(other(at.b), 0)
        to.wait_recv()
        turn(other(at.b), 1)
        yield
        qu1.wait_recv()
        td1 = on(at.b_down, 1, at.twin)
        ql0.wait_recv()
        tu0 = on(at.b_up, 0, at.twin)
        yield
        turn(mine(at.b_down), 1)
        turn(mine(at.b_up), 0)
        td0.wait_recv()
        turn(other(at.b_down), 0)
        tu1.wait_recv()
        turn(other(at.b_up), 1)
        yield
        td1.wait_recv()
        turn(other(at.b_down), 1)
        tu0.wait_recv()
        turn(other(at.b_up), 0)
        yield
        qu2.wait_recv()
        tf0 = on(at.b_far, 0, at.twin)
        ql2.wait_recv()
        tf1 = on(at.b_far, 1, at.twin)
        yield
        turn(mine(at.b_far), 0)
        turn(mine(at.b_far), 1)
        yield
        tf0.wait_recv()
        turn(other(at.b_far), 0)
        tf1.wait_recv()
        turn(other(at.b_far), 1)
        for copy in (kr1, kl0, kr2, kl2):
            copy.wait_recv()

    in_turn(work(0), work(1))
    copies.finish_sends()


def gathered(query, out_grad, key, value, links):
    return pl.pallas_call(
        gather_kernel,
        out_shape=(
            VMEM((2 * NG * 2 * ROWS, WIDE), BF16),
            VMEM((2 * SIDE * 2 * ROWS, WIDE), BF16),
            VMEM((NQ * TURNED, BLK), BF16),
            VMEM((8, LIST), jnp.int32),
            VMEM((CHIPS + 1, 3, LINES, BLK), F32),
            VMEM((NQ + 1, BLK, WIDE), BF16),
            VMEM((NK + 1, BLK, WIDE), BF16),
            VMEM((NK + 1, BLK, WIDE), BF16),
        ),
        in_specs=[whole(pltpu.HBM)] * 5,
        out_specs=(whole(VMEM),) * 8,
        scratch_shapes=[
            VMEM((LINKS, BLK), jnp.int32),
            VMEM((8, BLK), jnp.int32),
            pltpu.SemaphoreType.DMA((N_GATHER,)),
            pltpu.SemaphoreType.DMA((N_GATHER,)),
            pltpu.SemaphoreType.DMA((9,)),
        ],
        compiler_params=pltpu.CompilerParams(
            collective_id=0, has_side_effects=True, vmem_limit_bytes=8 * MIB
        ),
        name="gather",
    )(query, out_grad, key, value, pltpu.with_memory_space_constraint(links, pltpu.HBM))


def stats_kernel(list_ref, qt_ref, kg_ref, first_ref, part_ref):
    del first_ref
    listed_entries(list_ref, qt_ref, kg_ref, functools.partial(add_stats, part_ref))


def partial_stats(entries, qt, kg, part):
    return pl.pallas_call(
        stats_kernel,
        out_shape=VMEM((CHIPS + 1, 3, LINES, BLK), F32),
        in_specs=[whole(pltpu.SMEM)] + [whole(VMEM)] * 3,
        out_specs=whole(VMEM),
        input_output_aliases={3: 0},
        compiler_params=pltpu.CompilerParams(vmem_limit_bytes=8 * MIB),
        name="partial_stats",
    )(entries, *pinned(qt, kg, part))


def merged(parts):
    tops = [part[0] for part in parts]
    top = functools.reduce(jnp.maximum, tops)
    weights = [jnp.exp2(t - top) for t in tops]
    total = sum(part[1] * w for part, w in zip(parts, weights))
    dot = sum(part[2] * w for part, w in zip(parts, weights))
    return top, total, dot


def join_kernel(part_ref, full_ref, got_ref, near_ref, twin_ref, send_sem, recv_sem):
    halves = [Half(0), Half(1)]

    def around(at):
        return [(b, at.at(at.a, b, at.c)) for b in (at.b_far, at.b_up, at.b_down)]

    twin = halves[0].twin
    barrier_with([twin] + [device for at in halves for _, device in around(at)])
    copies = Copies(send_sem, recv_sem)
    first = [[], []]
    for n in range(SIDE - 1):
        for at in halves:
            b, device = around(at)[n]
            first[at.s].append(copies.start(part_ref.at[at.s * SIDE + b], got_ref.at[at.s, n], device))
    for at in halves:
        for copy in first[at.s]:
            copy.wait_recv()
        got = [part_ref[at.s * SIDE + at.b]] + [got_ref[at.s, n] for n in range(SIDE - 1)]
        for n, line in enumerate(merged(got)):
            near_ref[at.s, n] = line
    swap = copies.start(near_ref, twin_ref, twin)
    swap.wait_recv()
    later = []
    for at in halves:
        top, total, dot = merged([near_ref[at.s], twin_ref[at.s]])
        own = at.s * SIDE + at.b
        full_ref[own, 0] = top + jnp.log(total) * LOG2E
        full_ref[own, 1] = dot / total
        for _, device in around(at):
            later.append(copies.start(full_ref.at[own], full_ref.at[own], device))
    for copy in later:
        copy.wait_recv()
    copies.finish_sends()


def joined_stats(part):
    return pl.pallas_call(
        join_kernel,
        out_shape=VMEM((CHIPS, 2, LINES, BLK), F32),
        in_specs=[whole(VMEM)],
        out_specs=whole(VMEM),
        scratch_shapes=[
            VMEM((2, SIDE - 1, 3, LINES, BLK), F32),
            VMEM((2, 3, LINES, BLK), F32),
            VMEM((2, 3, LINES, BLK), F32),
            pltpu.SemaphoreType.DMA((13,)),
            pltpu.SemaphoreType.DMA((13,)),
        ],
        compiler_params=pltpu.CompilerParams(
            collective_id=1, has_side_effects=True, vmem_limit_bytes=8 * MIB
        ),
        name="join_stats",
    )(*pinned(part))


def grads_kernel(
    list_ref, qg_ref, qt_ref, kg_ref, full_ref, zero_q, zero_k, zero_v, dq_ref, dk_ref, dv_ref
):
    del zero_q, zero_k, zero_v

    def tiles(n):
        return lambda e, i: qg_ref[rows(e.q_row + n * ROWS), TILES[i]]

    finish = functools.partial(
        add_grads, dq_ref, dk_ref, dv_ref, full_ref, lambda e: jnp.bitwise_and(e.q_to, NQ - 1), tiles(0), tiles(1)
    )
    listed_entries(list_ref, qt_ref, kg_ref, finish)


def partial_grads(entries, qg, qt, kg, full, dq, dk, dv):
    return pl.pallas_call(
        grads_kernel,
        out_shape=(
            VMEM((NQ + 1, BLK, WIDE), BF16),
            VMEM((NK + 1, BLK, WIDE), BF16),
            VMEM((NK + 1, BLK, WIDE), BF16),
        ),
        in_specs=[whole(pltpu.SMEM)] + [whole(VMEM)] * 7,
        out_specs=(whole(VMEM),) * 3,
        input_output_aliases={5: 0, 6: 1, 7: 2},
        compiler_params=pltpu.CompilerParams(vmem_limit_bytes=8 * MIB),
        name="partial_grads",
    )(entries, *pinned(qg, qt, kg, full, dq, dk, dv))


N_SUM = 32


def add(dst, first, last, *terms):
    def body(n, _):
        total = terms[0][n].astype(F32)
        for term in terms[1:]:
            total = total + term[n].astype(F32)
        dst[n] = total.astype(BF16)
        return 0

    lax.fori_loop(first, last, body, 0)


def leave(dst, s, scale, *terms):
    for n in range(LOCAL):
        total = terms[0][n].astype(F32)
        for term in terms[1:]:
            total = total + term[n].astype(F32)
        dst[n * BLK : (n + 1) * BLK, s * WIDE : (s + 1) * WIDE] = (total * scale).astype(BF16)


def sum_kernel(
    dq_ref, dk_ref, dv_ref, full_ref, q_ref, o_ref, k_ref, v_ref, gq_ref, gk_ref, gv_ref,
    own_ref, own_q, own_k, own_v, twin_buf, q_all, q_far, q_in, k_far, k_in, v_in, send_sem, recv_sem, own_sem,
):
    copies = Copies(send_sem, recv_sem)
    go = copies.start
    low, high = pl.ds(0, 2), pl.ds(2, 2)
    kept = [
        pltpu.make_async_copy(ref, own_ref.at[n], own_sem.at[n])
        for n, ref in enumerate((q_ref, o_ref, k_ref, v_ref))
    ]
    for copy in kept:
        copy.start()

    def own_grads(at, pairs):
        def block(n, lb):
            return [
                own_ref[n, lb * BLK : (lb + 1) * BLK, (at.s * HEADS + i) * HEAD_DIM : (at.s * HEADS + i + 1) * HEAD_DIM]
                for i in range(HEADS)
            ]

        def turned(n, lb):
            return [tile.T for tile in block(n, lb)]

        base = at.s * LOCAL
        entries = []
        for m, n in pairs:
            e = Entry(base + m, base + n, block(2, n), block(3, n), turned(0, m), turned(1, m), pairs is ITSELF)
            e.local = m
            entries.append(e)

        def stats_slot(e):
            return (at.s * NG + at.g) * LOCAL + e.local

        add_grads(
            own_q, own_k, own_v, full_ref, stats_slot,
            lambda e, i: block(0, e.local)[i], lambda e, i: block(1, e.local)[i], entries,
        )


    def work(s):
        at = Half(s)
        if s == 0:
            barrier_with([at.right, at.left, at.upper, at.lower, at.twin])
        yield

        def mine(ref):
            return ref.at[pl.ds(s * LOCAL, LOCAL)]

        def keys(ref, a):
            return ref.at[pl.ds((s * SIDE + a) * LOCAL, LOCAL)]

        def queries(b, c):
            return dq_ref.at[pl.ds((s * NG + b * 2 + c) * LOCAL, LOCAL)]

        order = (at.b_far, at.b_up, at.b_down, at.b)
        kr0 = go(keys(dk_ref, at.a_far), k_far.at[s, 0], at.right)
        kl0 = go(keys(dv_ref, at.a_far), k_far.at[s, 1], at.left)
        pairs = [go(queries(b, 1 - at.c), twin_buf.at[s, n], at.twin) for n, b in enumerate(order)]
        yield
        kr1 = go(keys(dv_ref, at.a_up), v_in.at[s, 0], at.right)
        kl1 = go(keys(dk_ref, at.a_down), k_in.at[s, 1], at.left)
        yield
        for ref in (own_q, own_k, own_v):
            clear(ref.at[pl.ds(s * LOCAL, LOCAL)], LOCAL)
        if s == 0:
            for copy in kept:
                copy.wait()
        own_grads(at, ITSELF)
        own_grads(at, BEFORE)
        yield

        def take(n):
            pairs[n].wait_recv()
            add(q_all.at[s, n], 0, LOCAL, queries(order[n], at.c), twin_buf.at[s, n])

        take(0)
        qu0 = go(q_all.at[s, 0, low], q_far.at[s, 0, low], at.upper)
        ql0 = go(q_all.at[s, 0, high], q_far.at[s, 0, high], at.lower)
        yield
        take(1)
        qu1 = go(q_all.at[s, 1, high], q_in.at[s, 0, high], at.upper)
        take(2)
        ql1 = go(q_all.at[s, 2, low], q_in.at[s, 1, low], at.lower)
        take(3)
        yield
        qu0.wait_recv()
        add(q_far.at[s, 1], 0, 2, q_all.at[s, 1], q_far.at[s, 0])
        qu2 = go(q_far.at[s, 1, low], q_in.at[s, 0, low], at.upper)
        ql0.wait_recv()
        add(q_far.at[s, 1], 2, LOCAL, q_all.at[s, 2], q_far.at[s, 0])
        ql2 = go(q_far.at[s, 1, high], q_in.at[s, 1, high], at.lower)
        yield
        kr0.wait_recv()
        add(k_far.at[s, 2], 0, LOCAL, keys(dk_ref, at.a_up), k_far.at[s, 0])
        kr2 = go(k_far.at[s, 2], k_in.at[s, 0], at.right)
        kl0.wait_recv()
        add(k_far.at[s, 3], 0, LOCAL, keys(dv_ref, at.a_down), k_far.at[s, 1])
        kl2 = go(k_far.at[s, 3], v_in.at[s, 1], at.left)
        yield
        for copy in (qu1, ql1, qu2, ql2):
            copy.wait_recv()
        leave(gq_ref, s, SCALE, mine(own_q), q_all.at[s, 3], q_in.at[s, 0], q_in.at[s, 1])
        yield
        kr1.wait_recv()
        kl2.wait_recv()
        leave(gv_ref, s, 1.0, mine(own_v), keys(dv_ref, at.a), v_in.at[s, 0], v_in.at[s, 1])
        kl1.wait_recv()
        kr2.wait_recv()
        leave(gk_ref, s, SCALE, mine(own_k), keys(dk_ref, at.a), k_in.at[s, 0], k_in.at[s, 1])

    in_turn(work(0), work(1))
    copies.finish_sends()


def summed(dq, dk, dv, full, *args):
    grad = jax.ShapeDtypeStruct((ROWS, COLS), BF16)
    block = (LOCAL, BLK, WIDE)
    return pl.pallas_call(
        sum_kernel,
        out_shape=(grad, grad, grad),
        in_specs=[whole(VMEM)] * 4 + [whole(pltpu.HBM)] * 4,
        out_specs=(whole(VMEM),) * 3,
        scratch_shapes=[
            VMEM((4, ROWS, COLS), BF16),
            VMEM((2 * LOCAL, BLK, WIDE), F32),
            VMEM((2 * LOCAL, BLK, WIDE), F32),
            VMEM((2 * LOCAL, BLK, WIDE), F32),
            VMEM((2, SIDE, *block), BF16),
            VMEM((2, SIDE, *block), BF16),
            VMEM((2, 2, *block), BF16),
            VMEM((2, 2, *block), BF16),
            VMEM((2, 4, *block), BF16),
            VMEM((2, 2, *block), BF16),
            VMEM((2, 2, *block), BF16),
            pltpu.SemaphoreType.DMA((N_SUM,)),
            pltpu.SemaphoreType.DMA((N_SUM,)),
            pltpu.SemaphoreType.DMA((4,)),
        ],
        compiler_params=pltpu.CompilerParams(
            collective_id=2, has_side_effects=True, vmem_limit_bytes=20 * MIB
        ),
        name="sum_grads",
    )(*pinned(dq, dk, dv, full), *args)


def leave_kernel(*refs):
    *ins_and_outs, sem = refs
    copies = [pltpu.make_async_copy(ins_and_outs[n], ins_and_outs[n + 3], sem.at[n]) for n in range(3)]
    for copy in copies:
        copy.start()
    for copy in copies:
        copy.wait()


def left(*grads):
    return pl.pallas_call(
        leave_kernel,
        out_shape=(pltpu.HBM((ROWS, COLS), BF16),) * 3,
        in_specs=[whole(VMEM)] * 3,
        out_specs=(whole(pltpu.HBM),) * 3,
        scratch_shapes=[pltpu.SemaphoreType.DMA((3,))],
        compiler_params=pltpu.CompilerParams(vmem_limit_bytes=4 * MIB),
        name="leave",
    )(*pinned(*grads))


def per_device(query, key, value, out_grad, links):
    args = [pltpu.with_memory_space_constraint(v, pltpu.HBM) for v in (query, out_grad, key, value)]
    qg, kg, qt, entries, part, dq, dk, dv = gathered(*args, links.T)
    full = joined_stats(partial_stats(entries, qt, kg, part))
    dq, dk, dv = partial_grads(entries, qg, qt, kg, full, dq, dk, dv)
    return left(*summed(dq, dk, dv, full, *args))


def solution(mesh):
    spec = P("ctx", "head")
    return jax.shard_map(
        per_device,
        mesh=mesh,
        in_specs=(spec, spec, spec, spec, P()),
        out_specs=(spec, spec, spec),
        check_vma=False,
    )
```

```python
import functools

import jax
import jax.numpy as jnp
from jax import lax
from jax.experimental import pallas as pl
from jax.experimental.pallas import tpu as pltpu
from jax.sharding import PartitionSpec as P

HEAD_DIM = 128
BLK = 128
LINKS = 6
HEADS = 2
SIDE = 4
NG = 8
LOCAL = 4
ROWS = 512
COLS = 512
WIDE = HEADS * HEAD_DIM
NQ = 2 * SIDE * LOCAL
NK = 2 * NG * LOCAL
TURNED = 2 * WIDE
HOLDERS = 2 * SIDE
LINES = LOCAL * HEADS
LAST = 63
TILES = (slice(0, HEAD_DIM), slice(HEAD_DIM, WIDE))
MANY = 16
FEW = 8
LIST = 256
NEG = -1e30
SCALE = HEAD_DIM**-0.5
LOG2E = 1.4426950408889634
MESH = pl.DeviceIdType.MESH
BF16 = jnp.bfloat16
F32 = jnp.float32
VMEM = pltpu.VMEM
MIB = 1 << 20


def whole(space):
    return pl.BlockSpec(memory_space=space)


def pinned(*arrays):
    return [pltpu.with_memory_space_constraint(array, VMEM) for array in arrays]


def place():
    me = lax.axis_index("ctx")
    return me // 8, (me // 2) % 4, me % 2


class Half:
    def __init__(self, s):
        x, y, c = place()
        self.s, self.c = s, c
        self.a, self.b = (x, y) if s == 0 else (y, x)
        self.q_at, self.k_at = s * SIDE + self.b, s * NG + self.a * 2 + c
        self.a_up, self.a_down, self.a_far = [(self.a + n) % SIDE for n in (1, 3, 2)]
        self.b_up, self.b_down, self.b_far = [(self.b + n) % SIDE for n in (1, 3, 2)]
        self.right, self.left = self.at(self.a_up, self.b, c), self.at(self.a_down, self.b, c)
        self.upper, self.lower = self.at(self.a, self.b_up, c), self.at(self.a, self.b_down, c)
        self.twin = self.at(self.a, self.b, 1 - c)

    def at(self, a, b, c):
        x, y = (a, b) if self.s == 0 else (b, a)
        return ((x * SIDE + y) * 2 + c, lax.axis_index("head"))


def barrier_with(partners):
    sem = pltpu.get_barrier_semaphore()
    for partner in partners:
        pl.semaphore_signal(sem, inc=1, device_id=partner, device_id_type=MESH)
    pl.semaphore_wait(sem, len(partners))


class Copies:
    def __init__(self, send_sem, recv_sem):
        self.send_sem, self.recv_sem, self.made = send_sem, recv_sem, []

    def start(self, src, dst, device):
        n = len(self.made)
        copy = pltpu.make_async_remote_copy(
            src_ref=src,
            dst_ref=dst,
            send_sem=self.send_sem.at[n],
            recv_sem=self.recv_sem.at[n],
            device_id=device,
            device_id_type=MESH,
        )
        copy.start()
        self.made.append(copy)
        return copy

    def finish_sends(self):
        for copy in self.made:
            copy.wait_send()


def nt(a, b):
    return lax.dot_general(a, b, (((1,), (1,)), ((), ())), preferred_element_type=F32)


def nn(a, b):
    return lax.dot_general(a, b, (((1,), (0,)), ((), ())), preferred_element_type=F32)


def tn(a, b):
    return lax.dot_general(a, b, (((0,), (0,)), ((), ())), preferred_element_type=F32)


def in_turn(*works):
    works = list(works)
    while works:
        for work in list(works):
            if next(work, works) is works:
                works.remove(work)


def index_of_holder(block):
    stretch = block // 2
    late = stretch > LAST // 2
    return jnp.where(late, LAST - stretch, stretch), block % 2 + jnp.where(late, 2, 0)


def write_list(links_ref, named_ref, list_ref):
    shape = (8, BLK)
    block = lax.broadcasted_iota(jnp.int32, shape, 1)
    row = lax.broadcasted_iota(jnp.int32, shape, 0)
    named_ref[...] = block - 1
    named_ref[0:LINKS, :] = links_ref[...]
    named = named_ref[...]
    q_dev, q_local = index_of_holder(block)
    k_dev, k_local = index_of_holder(jnp.maximum(named, 0))
    within = jnp.logical_or(row > LINKS, jnp.logical_and(row == LINKS, block % 2 == 1))
    used = jnp.logical_and(named >= 0, jnp.logical_not(within))
    keys = lax.broadcasted_iota(jnp.int32, (BLK, BLK), 0)
    lanes = lax.broadcasted_iota(jnp.int32, (BLK, BLK), 1)
    before = jnp.where(keys < lanes, 1.0, 0.0).astype(BF16)
    out = [jnp.zeros(shape, F32) for _ in range(LIST // BLK)]
    base = jnp.zeros((1, 1), F32)
    for s in range(2):
        half = Half(s)
        q_x, q_y, k_x, k_y = q_dev // 8, (q_dev // 2) % 4, k_dev // 8, (k_dev // 2) % 4
        q_a, q_b = (q_x, q_y) if s == 0 else (q_y, q_x)
        k_a, k_b = (k_x, k_y) if s == 0 else (k_y, k_x)
        meets = jnp.logical_and(q_a * 2 + q_dev % 2 == half.a * 2 + half.c, k_b == half.b)
        here = jnp.where(jnp.logical_and(used, meets), 1.0, 0.0)
        q_slot = (s * SIDE + q_b) * LOCAL + q_local
        k_slot = (s * NG + k_a * 2 + k_dev % 2) * LOCAL + k_local
        at = base + jnp.sum(nn(here.astype(BF16), before), axis=0, keepdims=True)
        for t in range(LINKS + 1):
            flag = here[t : t + 1, :]
            values = jnp.where(row == 0, q_slot[t : t + 1, :], k_slot[t : t + 1, :]).astype(F32)
            for n in range(LIST // BLK):
                spot = keys.astype(F32) + float(n * BLK)
                hot = jnp.where(spot == at, flag, 0.0).astype(BF16)
                out[n] = out[n] + nt(values.astype(BF16), hot)
            at = at + flag
        base = base + jnp.sum(jnp.sum(here, axis=1, keepdims=True), axis=0, keepdims=True)
    for n in range(LIST // BLK):
        spot = block.astype(F32) + float(n * BLK)
        spare = jnp.where(row == 0, float(NQ), float(NK))
        full = jnp.where(row == 2, base, jnp.where(spot < base, out[n], spare)).astype(jnp.int32)
        q, k = jnp.bitwise_and(full[0:1, :], NQ - 1), jnp.bitwise_and(full[1:2, :], NK - 1)
        for at_row, values in ((3, first_row(k)), (4, q * TURNED), (5, first_row(q))):
            full = jnp.where(row == at_row, values, full)
        list_ref[:, n * BLK : (n + 1) * BLK] = full


def first_row(slot):
    return slot // LOCAL * (2 * ROWS) + slot % LOCAL * BLK


def rows(first, count=BLK):
    return pl.ds(pl.multiple_of(first, BLK), count)


class Entry:
    def __init__(self, q_to, k_to, keys, values, queries_t, out_grads_t, causal=False):
        self.q_to, self.k_to, self.keys = q_to, k_to, keys
        self.score = [nn(k, q) * (SCALE * LOG2E) for k, q in zip(keys, queries_t)]
        self.dprob = [nn(v, o) for v, o in zip(values, out_grads_t)]
        if causal:
            down = lax.broadcasted_iota(jnp.int32, (BLK, BLK), 0)
            live = down <= lax.broadcasted_iota(jnp.int32, (BLK, BLK), 1)
            self.score = [jnp.where(live, score, NEG) for score in self.score]


def met(q_to, k_to, k_row, turned_row, qt_ref, kg_ref, causal=False):
    keys, values = [[kg_ref[rows(k_row + n * ROWS), tile] for tile in TILES] for n in range(2)]
    turned = [[qt_ref[rows(turned_row + n * WIDE + tile.start), :] for tile in TILES] for n in range(2)]
    return Entry(q_to, k_to, keys, values, *turned, causal)


ITSELF = tuple((n, n) for n in range(LOCAL))
BEFORE = ((1, 0), (3, 2))


def listed_entries(list_ref, qt_ref, kg_ref, finish):
    def batch(first, count):
        entries = []
        for at in [first + u for u in range(count)]:
            q_to, k_to, _, k_row, turned_row, q_row = [list_ref[m, at] for m in range(6)]
            e = met(q_to, k_to, k_row, turned_row, qt_ref, kg_ref)
            e.q_row = q_row
            entries.append(e)
        finish(entries)
        return 0

    full = lax.div(list_ref[2, 0], MANY)
    rest = list_ref[2, 0] - full * MANY
    lax.fori_loop(0, full, lambda n, _: batch(n * MANY, MANY), 0)
    lax.fori_loop(0, lax.div(rest + (FEW - 1), FEW), lambda n, _: batch(full * MANY + n * FEW, FEW), 0)


def stats_place(q_slot):
    return lax.div(q_slot, LOCAL), pl.ds(lax.rem(q_slot, LOCAL) * HEADS, HEADS)


def add_stats(part_ref, entries):
    found = []
    for e in entries:
        tops = [jnp.max(score, axis=0, keepdims=True) for score in e.score]
        probs = [jnp.exp2(score - top) for score, top in zip(e.score, tops)]
        sums = [jnp.sum(prob, axis=0, keepdims=True) for prob in probs]
        dots = [jnp.sum(p * d, axis=0, keepdims=True) for p, d in zip(probs, e.dprob)]
        found.append([jnp.concatenate(lines, axis=0) for lines in (tops, sums, dots)])
    for e, (top, total, dot) in zip(entries, found):
        holder, lines = stats_place(e.q_to)
        old_top = part_ref[holder, 0, lines, :]
        new_top = jnp.maximum(old_top, top)
        was, now = jnp.exp2(old_top - new_top), jnp.exp2(top - new_top)
        part_ref[holder, 0, lines, :] = new_top
        part_ref[holder, 1, lines, :] = part_ref[holder, 1, lines, :] * was + total * now
        part_ref[holder, 2, lines, :] = part_ref[holder, 2, lines, :] * was + dot * now


def add_grads(dq_ref, dk_ref, dv_ref, full_ref, stats_slot, queries, out_grads, entries):
    found = []
    for e in entries:
        holder, lines = stats_place(stats_slot(e))
        lse, delta = full_ref[holder, 0, lines, :], full_ref[holder, 1, lines, :]
        dq, dk, dv = [], [], []
        for i in range(HEADS):
            prob = jnp.exp2(e.score[i] - lse[i : i + 1])
            dscore = (prob * (e.dprob[i] - delta[i : i + 1])).astype(BF16)
            dk.append(nn(dscore, queries(e, i)))
            dv.append(nn(prob.astype(BF16), out_grads(e, i)))
            dq.append(tn(dscore, e.keys[i]))
        found.append([jnp.concatenate(terms, axis=1) for terms in (dq, dk, dv)])
    for e, (dq, dk, dv) in zip(entries, found):
        dq_ref[e.q_to] += dq.astype(dq_ref.dtype)
        dk_ref[e.k_to] += dk.astype(dk_ref.dtype)
        dv_ref[e.k_to] += dv.astype(dv_ref.dtype)


def clear(ref, count):
    def body(n, _):
        ref[n] = jnp.zeros(ref.shape[1:], ref.dtype)
        return 0

    lax.fori_loop(0, count, body, 0)


N_GATHER = 40


def gather_kernel(
    q_ref, o_ref, k_ref, v_ref, links_ref,
    qg_ref, kg_ref, qt_ref, list_ref, part_ref, dq_ref, dk_ref, dv_ref,
    table_ref, named_ref, send_sem, recv_sem, own_sem,
):
    copies = Copies(send_sem, recv_sem)
    go = copies.start
    own = []
    table = pltpu.make_async_copy(links_ref, table_ref, own_sem.at[8])
    table.start()

    def columns(ref, s):
        return ref.at[:, s * WIDE : (s + 1) * WIDE]

    def part(ref, at, n):
        return ref.at[rows((at * 2 + n) * ROWS, ROWS)]

    def keep(src, dst):
        copy = pltpu.make_async_copy(src, dst, own_sem.at[len(own)])
        copy.start()
        own.append(copy)

    def turn(g, a):
        def body(lb, _):
            for tile in TILES:
                turned = (g * LOCAL + lb) * TURNED + a * WIDE + tile.start
                qt_ref[rows(turned), :] = qg_ref[rows((g * 2 + a) * ROWS + lb * BLK), tile].T
            return 0

        lax.fori_loop(0, LOCAL, body, 0)

    def work(s):
        at = Half(s)
        ka, qa = at.k_at, at.q_at
        q, o, k, v = [columns(ref, s) for ref in (q_ref, o_ref, k_ref, v_ref)]
        keep(q, part(qg_ref, qa, 0))
        keep(o, part(qg_ref, qa, 1))
        keep(k, part(kg_ref, ka, 0))
        keep(v, part(kg_ref, ka, 1))
        if s == 0:
            barrier_with([at.right, at.left, at.upper, at.lower, at.twin])
        yield
        kr0 = go(k, part(kg_ref, ka, 0), at.right)
        kl1 = go(v, part(kg_ref, ka, 1), at.left)
        yield
        qu0 = go(q, part(qg_ref, qa, 0), at.upper)
        ql1 = go(o, part(qg_ref, qa, 1), at.lower)
        yield
        kr1 = go(v, part(kg_ref, ka, 1), at.right)
        kl0 = go(k, part(kg_ref, ka, 0), at.left)
        twins = [go(k, part(kg_ref, ka, 0), at.twin), go(v, part(kg_ref, ka, 1), at.twin)]
        yield
        qu1 = go(o, part(qg_ref, qa, 1), at.upper)
        ql0 = go(q, part(qg_ref, qa, 0), at.lower)
        yield
        if s == 0:
            table.wait()
            write_list(table_ref, named_ref, list_ref)
            part_ref[:, 0] = jnp.full((HOLDERS + 1, LINES, BLK), NEG, F32)
            part_ref[:, 1:3] = jnp.zeros((HOLDERS + 1, 2, LINES, BLK), F32)
        for copy in own[4 * s : 4 * s + 4]:
            copy.wait()
        turn(qa, 0)
        turn(qa, 1)
        yield
        for pairs in (ITSELF, BEFORE):
            entries = []
            for m, n in pairs:
                q_slot, k_slot = qa * LOCAL + m, ka * LOCAL + n
                k_row, turned_row = ka * (2 * ROWS) + n * BLK, q_slot * TURNED
                entries.append(met(q_slot, k_slot, k_row, turned_row, qt_ref, kg_ref, pairs is ITSELF))
            add_stats(part_ref, entries)
        if s == 0:
            clear(dk_ref, NK + 1)
        else:
            clear(dq_ref, NQ + 1)
            clear(dv_ref, NK + 1)
        yield

        def on(ref, holder, n, device):
            slot = part(ref, holder, n)
            return go(slot, slot, device)

        def keys(a):
            return s * NG + a * 2 + at.c

        def queries(b):
            return s * SIDE + b

        kr0.wait_recv()
        kr2 = on(kg_ref, keys(at.a_down), 0, at.right)
        twins.append(on(kg_ref, keys(at.a_down), 0, at.twin))
        kl1.wait_recv()
        kl2 = on(kg_ref, keys(at.a_up), 1, at.left)
        twins.append(on(kg_ref, keys(at.a_up), 1, at.twin))
        yield
        qu0.wait_recv()
        qu2 = on(qg_ref, queries(at.b_down), 0, at.upper)
        ql1.wait_recv()
        ql2 = on(qg_ref, queries(at.b_up), 1, at.lower)
        yield
        turn(queries(at.b_down), 0)
        turn(queries(at.b_up), 1)
        yield
        kr1.wait_recv()
        twins.append(on(kg_ref, keys(at.a_down), 1, at.twin))
        kl0.wait_recv()
        twins.append(on(kg_ref, keys(at.a_up), 0, at.twin))
        yield
        qu1.wait_recv()
        turn(queries(at.b_down), 1)
        ql0.wait_recv()
        turn(queries(at.b_up), 0)
        yield
        kr2.wait_recv()
        twins.append(on(kg_ref, keys(at.a_far), 0, at.twin))
        kl2.wait_recv()
        twins.append(on(kg_ref, keys(at.a_far), 1, at.twin))
        yield
        qu2.wait_recv()
        turn(queries(at.b_far), 0)
        ql2.wait_recv()
        turn(queries(at.b_far), 1)
        for copy in twins:
            copy.wait_recv()

    in_turn(work(0), work(1))
    copies.finish_sends()


def gathered(query, out_grad, key, value, links):
    return pl.pallas_call(
        gather_kernel,
        out_shape=(
            VMEM((2 * SIDE * 2 * ROWS, WIDE), BF16),
            VMEM((2 * NG * 2 * ROWS, WIDE), BF16),
            VMEM((NQ * TURNED, BLK), BF16),
            VMEM((8, LIST), jnp.int32),
            VMEM((HOLDERS + 1, 3, LINES, BLK), F32),
            VMEM((NQ + 1, BLK, WIDE), BF16),
            VMEM((NK + 1, BLK, WIDE), BF16),
            VMEM((NK + 1, BLK, WIDE), BF16),
        ),
        in_specs=[whole(pltpu.HBM)] * 5,
        out_specs=(whole(VMEM),) * 8,
        scratch_shapes=[
            VMEM((LINKS, BLK), jnp.int32),
            VMEM((8, BLK), jnp.int32),
            pltpu.SemaphoreType.DMA((N_GATHER,)),
            pltpu.SemaphoreType.DMA((N_GATHER,)),
            pltpu.SemaphoreType.DMA((9,)),
        ],
        compiler_params=pltpu.CompilerParams(
            collective_id=0, has_side_effects=True, vmem_limit_bytes=8 * MIB
        ),
        name="gather",
    )(query, out_grad, key, value, pltpu.with_memory_space_constraint(links, pltpu.HBM))


def stats_kernel(list_ref, qt_ref, kg_ref, first_ref, part_ref):
    del first_ref
    listed_entries(list_ref, qt_ref, kg_ref, functools.partial(add_stats, part_ref))


def partial_stats(entries, qt, kg, part):
    return pl.pallas_call(
        stats_kernel,
        out_shape=VMEM((HOLDERS + 1, 3, LINES, BLK), F32),
        in_specs=[whole(pltpu.SMEM)] + [whole(VMEM)] * 3,
        out_specs=whole(VMEM),
        input_output_aliases={3: 0},
        compiler_params=pltpu.CompilerParams(vmem_limit_bytes=8 * MIB),
        name="partial_stats",
    )(entries, *pinned(qt, kg, part))


def merged(parts):
    tops = [part[0] for part in parts]
    top = functools.reduce(jnp.maximum, tops)
    weights = [jnp.exp2(t - top) for t in tops]
    total = sum(part[1] * w for part, w in zip(parts, weights))
    dot = sum(part[2] * w for part, w in zip(parts, weights))
    return top, total, dot


def join_kernel(part_ref, full_ref, got_ref, send_sem, recv_sem):
    halves = [Half(0), Half(1)]

    def around(at):
        return [(b, at.at(at.a, b, at.c)) for b in (at.b_far, at.b_up, at.b_down)]

    barrier_with([device for at in halves for _, device in around(at)])
    copies = Copies(send_sem, recv_sem)
    first = [[], []]
    for n in range(SIDE - 1):
        for at in halves:
            b, device = around(at)[n]
            first[at.s].append(copies.start(part_ref.at[at.s * SIDE + b], got_ref.at[at.s, n], device))
    later = []
    for at in halves:
        for copy in first[at.s]:
            copy.wait_recv()
        top, total, dot = merged([part_ref[at.q_at]] + [got_ref[at.s, n] for n in range(SIDE - 1)])
        full_ref[at.q_at, 0] = top + jnp.log(total) * LOG2E
        full_ref[at.q_at, 1] = dot / total
        for _, device in around(at):
            later.append(copies.start(full_ref.at[at.q_at], full_ref.at[at.q_at], device))
    for copy in later:
        copy.wait_recv()
    copies.finish_sends()


def joined_stats(part):
    return pl.pallas_call(
        join_kernel,
        out_shape=VMEM((HOLDERS, 2, LINES, BLK), F32),
        in_specs=[whole(VMEM)],
        out_specs=whole(VMEM),
        scratch_shapes=[
            VMEM((2, SIDE - 1, 3, LINES, BLK), F32),
            pltpu.SemaphoreType.DMA((12,)),
            pltpu.SemaphoreType.DMA((12,)),
        ],
        compiler_params=pltpu.CompilerParams(
            collective_id=1, has_side_effects=True, vmem_limit_bytes=8 * MIB
        ),
        name="join_stats",
    )(*pinned(part))


def grads_kernel(
    list_ref, qg_ref, qt_ref, kg_ref, full_ref, zero_q, zero_k, zero_v, dq_ref, dk_ref, dv_ref
):
    del zero_q, zero_k, zero_v

    def tiles(n):
        return lambda e, i: qg_ref[rows(e.q_row + n * ROWS), TILES[i]]

    finish = functools.partial(
        add_grads, dq_ref, dk_ref, dv_ref, full_ref, lambda e: jnp.bitwise_and(e.q_to, NQ - 1), tiles(0), tiles(1)
    )
    listed_entries(list_ref, qt_ref, kg_ref, finish)


def partial_grads(entries, qg, qt, kg, full, dq, dk, dv):
    return pl.pallas_call(
        grads_kernel,
        out_shape=(
            VMEM((NQ + 1, BLK, WIDE), BF16),
            VMEM((NK + 1, BLK, WIDE), BF16),
            VMEM((NK + 1, BLK, WIDE), BF16),
        ),
        in_specs=[whole(pltpu.SMEM)] + [whole(VMEM)] * 7,
        out_specs=(whole(VMEM),) * 3,
        input_output_aliases={5: 0, 6: 1, 7: 2},
        compiler_params=pltpu.CompilerParams(vmem_limit_bytes=8 * MIB),
        name="partial_grads",
    )(entries, *pinned(qg, qt, kg, full, dq, dk, dv))


N_SUM = 40


def add(dst, first, last, *terms):
    def body(n, _):
        total = terms[0][n].astype(F32)
        for term in terms[1:]:
            total = total + term[n].astype(F32)
        dst[n] = total.astype(BF16)
        return 0

    lax.fori_loop(first, last, body, 0)


def leave(dst, s, scale, *terms):
    for n in range(LOCAL):
        total = terms[0][n].astype(F32)
        for term in terms[1:]:
            total = total + term[n].astype(F32)
        dst[n * BLK : (n + 1) * BLK, s * WIDE : (s + 1) * WIDE] = (total * scale).astype(BF16)


def sum_kernel(
    dq_ref, dk_ref, dv_ref, full_ref, q_ref, o_ref, k_ref, v_ref, gq_ref, gk_ref, gv_ref,
    own_ref, own_q, own_k, own_v, twin_buf, k_all, q_far, q_in, k_far, k_in, v_in, send_sem, recv_sem, own_sem,
):
    copies = Copies(send_sem, recv_sem)
    go = copies.start
    low, high = pl.ds(0, 2), pl.ds(2, 2)
    kept = [
        pltpu.make_async_copy(ref, own_ref.at[n], own_sem.at[n])
        for n, ref in enumerate((q_ref, o_ref, k_ref, v_ref))
    ]
    for copy in kept:
        copy.start()

    def own_grads(at, pairs):
        def block(n, lb):
            return [
                own_ref[n, lb * BLK : (lb + 1) * BLK, (at.s * HEADS + i) * HEAD_DIM : (at.s * HEADS + i + 1) * HEAD_DIM]
                for i in range(HEADS)
            ]

        def turned(n, lb):
            return [tile.T for tile in block(n, lb)]

        base = at.s * LOCAL
        entries = []
        for m, n in pairs:
            e = Entry(base + m, base + n, block(2, n), block(3, n), turned(0, m), turned(1, m), pairs is ITSELF)
            e.local = m
            entries.append(e)

        def stats_slot(e):
            return at.q_at * LOCAL + e.local

        add_grads(
            own_q, own_k, own_v, full_ref, stats_slot,
            lambda e, i: block(0, e.local)[i], lambda e, i: block(1, e.local)[i], entries,
        )


    def work(s):
        at = Half(s)
        if s == 0:
            barrier_with([at.right, at.left, at.upper, at.lower, at.twin])
        yield

        def mine(ref):
            return ref.at[pl.ds(s * LOCAL, LOCAL)]

        def keys(ref, a, c):
            return ref.at[pl.ds((s * NG + a * 2 + c) * LOCAL, LOCAL)]

        def queries(b):
            return dq_ref.at[pl.ds((s * SIDE + b) * LOCAL, LOCAL)]

        order = (at.a_far, at.a_up, at.a_down, at.a)
        pairs = [
            [go(keys(ref, a, 1 - at.c), twin_buf.at[s, n, t], at.twin) for t, ref in enumerate((dk_ref, dv_ref))]
            for n, a in enumerate(order)
        ]
        qu0 = go(queries(at.b_far).at[low], q_far.at[s, 0, low], at.upper)
        ql0 = go(queries(at.b_far).at[high], q_far.at[s, 0, high], at.lower)
        yield
        qu1 = go(queries(at.b_up).at[high], q_in.at[s, 0, high], at.upper)
        ql1 = go(queries(at.b_down).at[low], q_in.at[s, 1, low], at.lower)
        yield

        def take(n, t):
            pairs[n][t].wait_recv()
            ref = (dk_ref, dv_ref)[t]
            add(k_all.at[s, n, t], 0, LOCAL, keys(ref, order[n], at.c), twin_buf.at[s, n, t])
            return k_all.at[s, n, t]

        kr0 = go(take(0, 0), k_far.at[s, 0], at.right)
        kl0 = go(take(0, 1), k_far.at[s, 1], at.left)
        yield
        kr1 = go(take(1, 1), v_in.at[s, 0], at.right)
        kl1 = go(take(2, 0), k_in.at[s, 1], at.left)
        yield
        qu0.wait_recv()
        add(q_far.at[s, 1], 0, 2, queries(at.b_up), q_far.at[s, 0])
        qu2 = go(q_far.at[s, 1, low], q_in.at[s, 0, low], at.upper)
        ql0.wait_recv()
        add(q_far.at[s, 1], 2, LOCAL, queries(at.b_down), q_far.at[s, 0])
        ql2 = go(q_far.at[s, 1, high], q_in.at[s, 1, high], at.lower)
        yield
        for n, t in ((1, 0), (2, 1), (3, 0), (3, 1)):
            take(n, t)
        for ref in (own_q, own_k, own_v):
            clear(mine(ref), LOCAL)
        if s == 0:
            for copy in kept:
                copy.wait()
        own_grads(at, ITSELF)
        own_grads(at, BEFORE)
        yield
        kr0.wait_recv()
        add(k_far.at[s, 2], 0, LOCAL, k_all.at[s, 1, 0], k_far.at[s, 0])
        kr2 = go(k_far.at[s, 2], k_in.at[s, 0], at.right)
        kl0.wait_recv()
        add(k_far.at[s, 3], 0, LOCAL, k_all.at[s, 2, 1], k_far.at[s, 1])
        kl2 = go(k_far.at[s, 3], v_in.at[s, 1], at.left)
        yield
        for copy in (qu1, ql1, qu2, ql2):
            copy.wait_recv()
        leave(gq_ref, s, SCALE, mine(own_q), queries(at.b), q_in.at[s, 0], q_in.at[s, 1])
        yield
        kr1.wait_recv()
        kl2.wait_recv()
        leave(gv_ref, s, 1.0, mine(own_v), k_all.at[s, 3, 1], v_in.at[s, 0], v_in.at[s, 1])
        kl1.wait_recv()
        kr2.wait_recv()
        leave(gk_ref, s, SCALE, mine(own_k), k_all.at[s, 3, 0], k_in.at[s, 0], k_in.at[s, 1])

    in_turn(work(0), work(1))
    copies.finish_sends()


def summed(dq, dk, dv, full, *args):
    grad = jax.ShapeDtypeStruct((ROWS, COLS), BF16)
    block = (LOCAL, BLK, WIDE)
    return pl.pallas_call(
        sum_kernel,
        out_shape=(grad, grad, grad),
        in_specs=[whole(VMEM)] * 4 + [whole(pltpu.HBM)] * 4,
        out_specs=(whole(VMEM),) * 3,
        scratch_shapes=[
            VMEM((4, ROWS, COLS), BF16),
            VMEM((2 * LOCAL, BLK, WIDE), F32),
            VMEM((2 * LOCAL, BLK, WIDE), F32),
            VMEM((2 * LOCAL, BLK, WIDE), F32),
            VMEM((2, SIDE, 2, *block), BF16),
            VMEM((2, SIDE, 2, *block), BF16),
            VMEM((2, 2, *block), BF16),
            VMEM((2, 2, *block), BF16),
            VMEM((2, 4, *block), BF16),
            VMEM((2, 2, *block), BF16),
            VMEM((2, 2, *block), BF16),
            pltpu.SemaphoreType.DMA((N_SUM,)),
            pltpu.SemaphoreType.DMA((N_SUM,)),
            pltpu.SemaphoreType.DMA((4,)),
        ],
        compiler_params=pltpu.CompilerParams(
            collective_id=2, has_side_effects=True, vmem_limit_bytes=24 * MIB
        ),
        name="sum_grads",
    )(*pinned(dq, dk, dv, full), *args)


def leave_kernel(*refs):
    *ins_and_outs, sem = refs
    copies = [pltpu.make_async_copy(ins_and_outs[n], ins_and_outs[n + 3], sem.at[n]) for n in range(3)]
    for copy in copies:
        copy.start()
    for copy in copies:
        copy.wait()


def left(*grads):
    return pl.pallas_call(
        leave_kernel,
        out_shape=(pltpu.HBM((ROWS, COLS), BF16),) * 3,
        in_specs=[whole(VMEM)] * 3,
        out_specs=(whole(pltpu.HBM),) * 3,
        scratch_shapes=[pltpu.SemaphoreType.DMA((3,))],
        compiler_params=pltpu.CompilerParams(vmem_limit_bytes=4 * MIB),
        name="leave",
    )(*pinned(*grads))


def per_device(query, key, value, out_grad, links):
    args = [pltpu.with_memory_space_constraint(v, pltpu.HBM) for v in (query, out_grad, key, value)]
    qg, kg, qt, entries, part, dq, dk, dv = gathered(*args, links.T)
    full = joined_stats(partial_stats(entries, qt, kg, part))
    dq, dk, dv = partial_grads(entries, qg, qt, kg, full, dq, dk, dv)
    return left(*summed(dq, dk, dv, full, *args))


def solution(mesh):
    spec = P("ctx", "head")
    return jax.shard_map(
        per_device,
        mesh=mesh,
        in_specs=(spec, spec, spec, spec, P()),
        out_specs=(spec, spec, spec),
        check_vma=False,
    )
```

```python
import functools

import jax
import jax.numpy as jnp
from jax import lax
from jax.experimental import pallas as pl
from jax.experimental.pallas import tpu as pltpu
from jax.sharding import PartitionSpec as P

HEAD_DIM = 128
BLK = 128
LINKS = 6
HEADS = 2
SIDE = 4
NG = 8
LOCAL = 4
ROWS = 512
COLS = 512
WIDE = HEADS * HEAD_DIM
NQ = 2 * SIDE * LOCAL
NK = 2 * NG * LOCAL
TURNED = 2 * WIDE
HOLDERS = 2 * SIDE
LINES = LOCAL * HEADS
LAST = 63
TILES = (slice(0, HEAD_DIM), slice(HEAD_DIM, WIDE))
MANY, SOME, FEW = 16, 8, 4
LIST = 256
NEG = -1e30
SCALE = HEAD_DIM**-0.5
LOG2E = 1.4426950408889634
MESH = pl.DeviceIdType.MESH
BF16 = jnp.bfloat16
F32 = jnp.float32
VMEM = pltpu.VMEM
MIB = 1 << 20


def whole(space):
    return pl.BlockSpec(memory_space=space)


def pinned(*arrays):
    return [pltpu.with_memory_space_constraint(array, VMEM) for array in arrays]


def place():
    me = lax.axis_index("ctx")
    return me // 8, (me // 2) % 4, me % 2


class Half:
    def __init__(self, s):
        x, y, c = place()
        self.s, self.c = s, c
        self.a, self.b = (x, y) if s == 0 else (y, x)
        self.q_at, self.k_at = s * SIDE + self.b, s * NG + self.a * 2 + c
        self.a_up, self.a_down, self.a_far = [(self.a + n) % SIDE for n in (1, 3, 2)]
        self.b_up, self.b_down, self.b_far = [(self.b + n) % SIDE for n in (1, 3, 2)]
        self.right, self.left = self.at(self.a_up, self.b, c), self.at(self.a_down, self.b, c)
        self.upper, self.lower = self.at(self.a, self.b_up, c), self.at(self.a, self.b_down, c)
        self.twin = self.at(self.a, self.b, 1 - c)

    def at(self, a, b, c):
        x, y = (a, b) if self.s == 0 else (b, a)
        return ((x * SIDE + y) * 2 + c, lax.axis_index("head"))


def barrier_with(partners):
    sem = pltpu.get_barrier_semaphore()
    for partner in partners:
        pl.semaphore_signal(sem, inc=1, device_id=partner, device_id_type=MESH)
    pl.semaphore_wait(sem, len(partners))


class Copies:
    def __init__(self, send_sem, recv_sem):
        self.send_sem, self.recv_sem, self.made = send_sem, recv_sem, []

    def start(self, src, dst, device):
        n = len(self.made)
        copy = pltpu.make_async_remote_copy(
            src_ref=src,
            dst_ref=dst,
            send_sem=self.send_sem.at[n],
            recv_sem=self.recv_sem.at[n],
            device_id=device,
            device_id_type=MESH,
        )
        copy.start()
        self.made.append(copy)
        return copy

    def finish_sends(self):
        for copy in self.made:
            copy.wait_send()


def nt(a, b):
    return lax.dot_general(a, b, (((1,), (1,)), ((), ())), preferred_element_type=F32)


def nn(a, b):
    return lax.dot_general(a, b, (((1,), (0,)), ((), ())), preferred_element_type=F32)


def tn(a, b):
    return lax.dot_general(a, b, (((0,), (0,)), ((), ())), preferred_element_type=F32)


def in_turn(*works):
    works = list(works)
    while works:
        for work in list(works):
            if next(work, works) is works:
                works.remove(work)


def index_of_holder(block):
    stretch = block // 2
    late = stretch > LAST // 2
    return jnp.where(late, LAST - stretch, stretch), block % 2 + jnp.where(late, 2, 0)


def write_list(links_ref, named_ref, list_ref):
    shape = (8, BLK)
    block = lax.broadcasted_iota(jnp.int32, shape, 1)
    row = lax.broadcasted_iota(jnp.int32, shape, 0)
    named_ref[...] = block - 1
    named_ref[0:LINKS, :] = links_ref[...]
    named = named_ref[...]
    q_dev, q_local = index_of_holder(block)
    k_dev, k_local = index_of_holder(jnp.maximum(named, 0))
    within = jnp.logical_or(row > LINKS, jnp.logical_and(row == LINKS, block % 2 == 1))
    used = jnp.logical_and(named >= 0, jnp.logical_not(within))
    keys = lax.broadcasted_iota(jnp.int32, (BLK, BLK), 0)
    lanes = lax.broadcasted_iota(jnp.int32, (BLK, BLK), 1)
    before = jnp.where(keys < lanes, 1.0, 0.0).astype(BF16)
    out = [jnp.zeros(shape, F32) for _ in range(LIST // BLK)]
    base = jnp.zeros((1, 1), F32)
    for s in range(2):
        half = Half(s)
        q_x, q_y, k_x, k_y = q_dev // 8, (q_dev // 2) % 4, k_dev // 8, (k_dev // 2) % 4
        q_a, q_b = (q_x, q_y) if s == 0 else (q_y, q_x)
        k_a, k_b = (k_x, k_y) if s == 0 else (k_y, k_x)
        meets = jnp.logical_and(q_a * 2 + q_dev % 2 == half.a * 2 + half.c, k_b == half.b)
        here = jnp.where(jnp.logical_and(used, meets), 1.0, 0.0)
        q_slot = (s * SIDE + q_b) * LOCAL + q_local
        k_slot = (s * NG + k_a * 2 + k_dev % 2) * LOCAL + k_local
        at = base + jnp.sum(nn(here.astype(BF16), before), axis=0, keepdims=True)
        for t in range(LINKS + 1):
            flag = here[t : t + 1, :]
            values = jnp.where(row == 0, q_slot[t : t + 1, :], k_slot[t : t + 1, :]).astype(F32)
            for n in range(LIST // BLK):
                spot = keys.astype(F32) + float(n * BLK)
                hot = jnp.where(spot == at, flag, 0.0).astype(BF16)
                out[n] = out[n] + nt(values.astype(BF16), hot)
            at = at + flag
        base = base + jnp.sum(jnp.sum(here, axis=1, keepdims=True), axis=0, keepdims=True)
    for n in range(LIST // BLK):
        spot = block.astype(F32) + float(n * BLK)
        spare = jnp.where(row == 0, float(NQ), float(NK))
        full = jnp.where(row == 2, base, jnp.where(spot < base, out[n], spare)).astype(jnp.int32)
        q, k = jnp.bitwise_and(full[0:1, :], NQ - 1), jnp.bitwise_and(full[1:2, :], NK - 1)
        for at_row, values in ((3, first_row(k)), (4, q * TURNED), (5, first_row(q))):
            full = jnp.where(row == at_row, values, full)
        list_ref[:, n * BLK : (n + 1) * BLK] = full


def first_row(slot):
    return slot // LOCAL * (2 * ROWS) + slot % LOCAL * BLK


def rows(first, count=BLK):
    return pl.ds(pl.multiple_of(first, BLK), count)


class Entry:
    def __init__(self, q_to, k_to, keys, values, queries_t, out_grads_t, causal=False):
        self.q_to, self.k_to, self.keys = q_to, k_to, keys
        self.score = [nn(k, q) * (SCALE * LOG2E) for k, q in zip(keys, queries_t)]
        self.dprob = [nn(v, o) for v, o in zip(values, out_grads_t)]
        if causal:
            down = lax.broadcasted_iota(jnp.int32, (BLK, BLK), 0)
            live = down <= lax.broadcasted_iota(jnp.int32, (BLK, BLK), 1)
            self.score = [jnp.where(live, score, NEG) for score in self.score]


def met(q_to, k_to, k_row, turned_row, qt_ref, kg_ref, causal=False):
    keys, values = [[kg_ref[rows(k_row + n * ROWS), tile] for tile in TILES] for n in range(2)]
    turned = [[qt_ref[rows(turned_row + n * WIDE + tile.start), :] for tile in TILES] for n in range(2)]
    return Entry(q_to, k_to, keys, values, *turned, causal)


ITSELF = tuple((n, n) for n in range(LOCAL))
BEFORE = ((1, 0), (3, 2))


def listed_entries(list_ref, qt_ref, kg_ref, finish):
    def batch(first, count):
        entries = []
        for at in [first + u for u in range(count)]:
            q_to, k_to, _, k_row, turned_row, q_row = [list_ref[m, at] for m in range(6)]
            e = met(q_to, k_to, k_row, turned_row, qt_ref, kg_ref)
            e.q_row = q_row
            entries.append(e)
        finish(entries)
        return 0

    full = lax.div(list_ref[2, 0], MANY)
    rest = list_ref[2, 0] - full * MANY
    some = lax.div(rest + (SOME - FEW - 1), SOME)
    left_over = rest - some * SOME
    lax.fori_loop(0, full, lambda n, _: batch(n * MANY, MANY), 0)
    lax.fori_loop(0, some, lambda n, _: batch(full * MANY + n * SOME, SOME), 0)

    @pl.when(left_over > 0)
    def _():
        batch(full * MANY + some * SOME, FEW)


def stats_place(q_slot):
    return lax.div(q_slot, LOCAL), pl.ds(lax.rem(q_slot, LOCAL) * HEADS, HEADS)


def add_stats(part_ref, entries):
    found = []
    for e in entries:
        tops = [jnp.max(score, axis=0, keepdims=True) for score in e.score]
        probs = [jnp.exp2(score - top) for score, top in zip(e.score, tops)]
        sums = [jnp.sum(prob, axis=0, keepdims=True) for prob in probs]
        dots = [jnp.sum(p * d, axis=0, keepdims=True) for p, d in zip(probs, e.dprob)]
        found.append([jnp.concatenate(lines, axis=0) for lines in (tops, sums, dots)])
    for e, (top, total, dot) in zip(entries, found):
        holder, lines = stats_place(e.q_to)
        old_top = part_ref[holder, 0, lines, :]
        new_top = jnp.maximum(old_top, top)
        was, now = jnp.exp2(old_top - new_top), jnp.exp2(top - new_top)
        part_ref[holder, 0, lines, :] = new_top
        part_ref[holder, 1, lines, :] = part_ref[holder, 1, lines, :] * was + total * now
        part_ref[holder, 2, lines, :] = part_ref[holder, 2, lines, :] * was + dot * now


def add_grads(dq_ref, dk_ref, dv_ref, full_ref, stats_slot, queries, out_grads, entries):
    found = []
    for e in entries:
        holder, lines = stats_place(stats_slot(e))
        lse, delta = full_ref[holder, 0, lines, :], full_ref[holder, 1, lines, :]
        dq, dk, dv = [], [], []
        for i in range(HEADS):
            prob = jnp.exp2(e.score[i] - lse[i : i + 1])
            dscore = (prob * (e.dprob[i] - delta[i : i + 1])).astype(BF16)
            dk.append(nn(dscore, queries(e, i)))
            dv.append(nn(prob.astype(BF16), out_grads(e, i)))
            dq.append(tn(dscore, e.keys[i]))
        found.append([jnp.concatenate(terms, axis=1) for terms in (dq, dk, dv)])
    for e, (dq, dk, dv) in zip(entries, found):
        dq_ref[e.q_to] += dq.astype(dq_ref.dtype)
        dk_ref[e.k_to] += dk.astype(dk_ref.dtype)
        dv_ref[e.k_to] += dv.astype(dv_ref.dtype)


def clear(ref, count):
    def body(n, _):
        ref[n] = jnp.zeros(ref.shape[1:], ref.dtype)
        return 0

    lax.fori_loop(0, count, body, 0)


N_GATHER = 40


def gather_kernel(
    q_ref, o_ref, k_ref, v_ref, links_ref,
    qg_ref, kg_ref, qt_ref, list_ref, part_ref, dq_ref, dk_ref, dv_ref,
    table_ref, named_ref, send_sem, recv_sem, own_sem,
):
    copies = Copies(send_sem, recv_sem)
    go = copies.start
    own = []
    table = pltpu.make_async_copy(links_ref, table_ref, own_sem.at[8])
    table.start()

    def columns(ref, s):
        return ref.at[:, s * WIDE : (s + 1) * WIDE]

    def part(ref, at, n):
        return ref.at[rows((at * 2 + n) * ROWS, ROWS)]

    def keep(src, dst):
        copy = pltpu.make_async_copy(src, dst, own_sem.at[len(own)])
        copy.start()
        own.append(copy)

    def turn(g, a):
        def body(lb, _):
            for tile in TILES:
                turned = (g * LOCAL + lb) * TURNED + a * WIDE + tile.start
                qt_ref[rows(turned), :] = qg_ref[rows((g * 2 + a) * ROWS + lb * BLK), tile].T
            return 0

        lax.fori_loop(0, LOCAL, body, 0)

    def work(s):
        at = Half(s)
        ka, qa = at.k_at, at.q_at
        q, o, k, v = [columns(ref, s) for ref in (q_ref, o_ref, k_ref, v_ref)]
        keep(q, part(qg_ref, qa, 0))
        keep(o, part(qg_ref, qa, 1))
        keep(k, part(kg_ref, ka, 0))
        keep(v, part(kg_ref, ka, 1))
        if s == 0:
            barrier_with([at.right, at.left, at.upper, at.lower, at.twin])
        yield
        kr0 = go(k, part(kg_ref, ka, 0), at.right)
        kl1 = go(v, part(kg_ref, ka, 1), at.left)
        yield
        qu0 = go(q, part(qg_ref, qa, 0), at.upper)
        ql1 = go(o, part(qg_ref, qa, 1), at.lower)
        yield
        kr1 = go(v, part(kg_ref, ka, 1), at.right)
        kl0 = go(k, part(kg_ref, ka, 0), at.left)
        twins = [go(k, part(kg_ref, ka, 0), at.twin), go(v, part(kg_ref, ka, 1), at.twin)]
        yield
        qu1 = go(o, part(qg_ref, qa, 1), at.upper)
        ql0 = go(q, part(qg_ref, qa, 0), at.lower)
        yield
        if s == 0:
            table.wait()
            write_list(table_ref, named_ref, list_ref)
            part_ref[:, 0] = jnp.full((HOLDERS + 1, LINES, BLK), NEG, F32)
            part_ref[:, 1:3] = jnp.zeros((HOLDERS + 1, 2, LINES, BLK), F32)
        for copy in own[4 * s : 4 * s + 4]:
            copy.wait()
        turn(qa, 0)
        turn(qa, 1)
        yield
        for pairs in (ITSELF, BEFORE):
            entries = []
            for m, n in pairs:
                q_slot, k_slot = qa * LOCAL + m, ka * LOCAL + n
                k_row, turned_row = ka * (2 * ROWS) + n * BLK, q_slot * TURNED
                entries.append(met(q_slot, k_slot, k_row, turned_row, qt_ref, kg_ref, pairs is ITSELF))
            add_stats(part_ref, entries)
        if s == 0:
            clear(dk_ref, NK + 1)
        else:
            clear(dq_ref, NQ + 1)
            clear(dv_ref, NK + 1)
        yield

        def on(ref, holder, n, device):
            slot = part(ref, holder, n)
            return go(slot, slot, device)

        def keys(a):
            return s * NG + a * 2 + at.c

        def queries(b):
            return s * SIDE + b

        kr0.wait_recv()
        kr2 = on(kg_ref, keys(at.a_down), 0, at.right)
        twins.append(on(kg_ref, keys(at.a_down), 0, at.twin))
        kl1.wait_recv()
        kl2 = on(kg_ref, keys(at.a_up), 1, at.left)
        twins.append(on(kg_ref, keys(at.a_up), 1, at.twin))
        yield
        qu0.wait_recv()
        qu2 = on(qg_ref, queries(at.b_down), 0, at.upper)
        ql1.wait_recv()
        ql2 = on(qg_ref, queries(at.b_up), 1, at.lower)
        yield
        turn(queries(at.b_down), 0)
        turn(queries(at.b_up), 1)
        yield
        kr1.wait_recv()
        twins.append(on(kg_ref, keys(at.a_down), 1, at.twin))
        kl0.wait_recv()
        twins.append(on(kg_ref, keys(at.a_up), 0, at.twin))
        yield
        qu1.wait_recv()
        turn(queries(at.b_down), 1)
        ql0.wait_recv()
        turn(queries(at.b_up), 0)
        yield
        kr2.wait_recv()
        twins.append(on(kg_ref, keys(at.a_far), 0, at.twin))
        kl2.wait_recv()
        twins.append(on(kg_ref, keys(at.a_far), 1, at.twin))
        yield
        qu2.wait_recv()
        turn(queries(at.b_far), 0)
        ql2.wait_recv()
        turn(queries(at.b_far), 1)
        for copy in twins:
            copy.wait_recv()

    in_turn(work(0), work(1))
    copies.finish_sends()


def gathered(query, out_grad, key, value, links):
    return pl.pallas_call(
        gather_kernel,
        out_shape=(
            VMEM((2 * SIDE * 2 * ROWS, WIDE), BF16),
            VMEM((2 * NG * 2 * ROWS, WIDE), BF16),
            VMEM((NQ * TURNED, BLK), BF16),
            VMEM((8, LIST), jnp.int32),
            VMEM((HOLDERS + 1, 3, LINES, BLK), F32),
            VMEM((NQ + 1, BLK, WIDE), BF16),
            VMEM((NK + 1, BLK, WIDE), BF16),
            VMEM((NK + 1, BLK, WIDE), BF16),
        ),
        in_specs=[whole(pltpu.HBM)] * 5,
        out_specs=(whole(VMEM),) * 8,
        scratch_shapes=[
            VMEM((LINKS, BLK), jnp.int32),
            VMEM((8, BLK), jnp.int32),
            pltpu.SemaphoreType.DMA((N_GATHER,)),
            pltpu.SemaphoreType.DMA((N_GATHER,)),
            pltpu.SemaphoreType.DMA((9,)),
        ],
        compiler_params=pltpu.CompilerParams(
            collective_id=0, has_side_effects=True, vmem_limit_bytes=8 * MIB
        ),
        name="gather",
    )(query, out_grad, key, value, pltpu.with_memory_space_constraint(links, pltpu.HBM))


def stats_kernel(list_ref, qt_ref, kg_ref, first_ref, part_ref):
    del first_ref
    listed_entries(list_ref, qt_ref, kg_ref, functools.partial(add_stats, part_ref))


def partial_stats(entries, qt, kg, part):
    return pl.pallas_call(
        stats_kernel,
        out_shape=VMEM((HOLDERS + 1, 3, LINES, BLK), F32),
        in_specs=[whole(pltpu.SMEM)] + [whole(VMEM)] * 3,
        out_specs=whole(VMEM),
        input_output_aliases={3: 0},
        compiler_params=pltpu.CompilerParams(vmem_limit_bytes=8 * MIB),
        name="partial_stats",
    )(entries, *pinned(qt, kg, part))


def merged(parts):
    tops = [part[0] for part in parts]
    top = functools.reduce(jnp.maximum, tops)
    weights = [jnp.exp2(t - top) for t in tops]
    total = sum(part[1] * w for part, w in zip(parts, weights))
    dot = sum(part[2] * w for part, w in zip(parts, weights))
    return top, total, dot


def join_kernel(part_ref, full_ref, got_ref, send_sem, recv_sem):
    halves = [Half(0), Half(1)]

    def around(at):
        return [(b, at.at(at.a, b, at.c)) for b in (at.b_far, at.b_up, at.b_down)]

    barrier_with([device for at in halves for _, device in around(at)])
    copies = Copies(send_sem, recv_sem)
    first = [[], []]
    for n in range(SIDE - 1):
        for at in halves:
            b, device = around(at)[n]
            first[at.s].append(copies.start(part_ref.at[at.s * SIDE + b], got_ref.at[at.s, n], device))
    later = []
    for at in halves:
        for copy in first[at.s]:
            copy.wait_recv()
        top, total, dot = merged([part_ref[at.q_at]] + [got_ref[at.s, n] for n in range(SIDE - 1)])
        full_ref[at.q_at, 0] = top + jnp.log(total) * LOG2E
        full_ref[at.q_at, 1] = dot / total
        for _, device in around(at):
            later.append(copies.start(full_ref.at[at.q_at], full_ref.at[at.q_at], device))
    for copy in later:
        copy.wait_recv()
    copies.finish_sends()


def joined_stats(part):
    return pl.pallas_call(
        join_kernel,
        out_shape=VMEM((HOLDERS, 2, LINES, BLK), F32),
        in_specs=[whole(VMEM)],
        out_specs=whole(VMEM),
        scratch_shapes=[
            VMEM((2, SIDE - 1, 3, LINES, BLK), F32),
            pltpu.SemaphoreType.DMA((12,)),
            pltpu.SemaphoreType.DMA((12,)),
        ],
        compiler_params=pltpu.CompilerParams(
            collective_id=1, has_side_effects=True, vmem_limit_bytes=8 * MIB
        ),
        name="join_stats",
    )(*pinned(part))


def grads_kernel(
    list_ref, qg_ref, qt_ref, kg_ref, full_ref, zero_q, zero_k, zero_v, dq_ref, dk_ref, dv_ref
):
    del zero_q, zero_k, zero_v

    def tiles(n):
        return lambda e, i: qg_ref[rows(e.q_row + n * ROWS), TILES[i]]

    finish = functools.partial(
        add_grads, dq_ref, dk_ref, dv_ref, full_ref, lambda e: jnp.bitwise_and(e.q_to, NQ - 1), tiles(0), tiles(1)
    )
    listed_entries(list_ref, qt_ref, kg_ref, finish)


def partial_grads(entries, qg, qt, kg, full, dq, dk, dv):
    return pl.pallas_call(
        grads_kernel,
        out_shape=(
            VMEM((NQ + 1, BLK, WIDE), BF16),
            VMEM((NK + 1, BLK, WIDE), BF16),
            VMEM((NK + 1, BLK, WIDE), BF16),
        ),
        in_specs=[whole(pltpu.SMEM)] + [whole(VMEM)] * 7,
        out_specs=(whole(VMEM),) * 3,
        input_output_aliases={5: 0, 6: 1, 7: 2},
        compiler_params=pltpu.CompilerParams(vmem_limit_bytes=8 * MIB),
        name="partial_grads",
    )(entries, *pinned(qg, qt, kg, full, dq, dk, dv))


N_SUM = 40


def add(dst, first, last, *terms):
    def body(n, _):
        total = terms[0][n].astype(F32)
        for term in terms[1:]:
            total = total + term[n].astype(F32)
        dst[n] = total.astype(BF16)
        return 0

    lax.fori_loop(first, last, body, 0)


def sum_kernel(
    dq_ref, dk_ref, dv_ref, full_ref, q_ref, o_ref, k_ref, v_ref,
    q_in, k_in, v_in, k_own, own_q, own_k, own_v,
    own_ref, twin_buf, k_all, q_far, k_far, send_sem, recv_sem, own_sem,
):
    copies = Copies(send_sem, recv_sem)
    go = copies.start
    low, high = pl.ds(0, 2), pl.ds(2, 2)
    kept = [
        pltpu.make_async_copy(ref, own_ref.at[n], own_sem.at[n])
        for n, ref in enumerate((q_ref, o_ref, k_ref, v_ref))
    ]
    for copy in kept:
        copy.start()

    def own_grads(at, pairs):
        def block(n, lb):
            return [
                own_ref[n, lb * BLK : (lb + 1) * BLK, (at.s * HEADS + i) * HEAD_DIM : (at.s * HEADS + i + 1) * HEAD_DIM]
                for i in range(HEADS)
            ]

        def turned(n, lb):
            return [tile.T for tile in block(n, lb)]

        base = at.s * LOCAL
        entries = []
        for m, n in pairs:
            e = Entry(base + m, base + n, block(2, n), block(3, n), turned(0, m), turned(1, m), pairs is ITSELF)
            e.local = m
            entries.append(e)

        def stats_slot(e):
            return at.q_at * LOCAL + e.local

        add_grads(
            own_q, own_k, own_v, full_ref, stats_slot,
            lambda e, i: block(0, e.local)[i], lambda e, i: block(1, e.local)[i], entries,
        )


    def work(s):
        at = Half(s)
        if s == 0:
            barrier_with([at.right, at.left, at.upper, at.lower, at.twin])
        yield

        def mine(ref):
            return ref.at[pl.ds(s * LOCAL, LOCAL)]

        def keys(ref, a, c):
            return ref.at[pl.ds((s * NG + a * 2 + c) * LOCAL, LOCAL)]

        def queries(b):
            return dq_ref.at[pl.ds((s * SIDE + b) * LOCAL, LOCAL)]

        order = (at.a_far, at.a_up, at.a_down, at.a)
        pairs = [
            [go(keys(ref, a, 1 - at.c), twin_buf.at[s, n, t], at.twin) for t, ref in enumerate((dk_ref, dv_ref))]
            for n, a in enumerate(order)
        ]
        qu0 = go(queries(at.b_far).at[low], q_far.at[s, 0, low], at.upper)
        ql0 = go(queries(at.b_far).at[high], q_far.at[s, 0, high], at.lower)
        yield
        qu1 = go(queries(at.b_up).at[high], q_in.at[s, 0, high], at.upper)
        ql1 = go(queries(at.b_down).at[low], q_in.at[s, 1, low], at.lower)
        yield

        def take(n, t):
            pairs[n][t].wait_recv()
            ref = (dk_ref, dv_ref)[t]
            add(k_all.at[s, n, t], 0, LOCAL, keys(ref, order[n], at.c), twin_buf.at[s, n, t])
            return k_all.at[s, n, t]

        kr0 = go(take(0, 0), k_far.at[s, 0], at.right)
        kl0 = go(take(0, 1), k_far.at[s, 1], at.left)
        yield
        kr1 = go(take(1, 1), v_in.at[s, 0], at.right)
        kl1 = go(take(2, 0), k_in.at[s, 1], at.left)
        yield
        qu0.wait_recv()
        add(q_far.at[s, 1], 0, 2, queries(at.b_up), q_far.at[s, 0])
        qu2 = go(q_far.at[s, 1, low], q_in.at[s, 0, low], at.upper)
        ql0.wait_recv()
        add(q_far.at[s, 1], 2, LOCAL, queries(at.b_down), q_far.at[s, 0])
        ql2 = go(q_far.at[s, 1, high], q_in.at[s, 1, high], at.lower)
        yield
        for n, t in ((1, 0), (2, 1)):
            take(n, t)
        for t, ref in enumerate((dk_ref, dv_ref)):
            pairs[3][t].wait_recv()
            add(k_own.at[s, t], 0, LOCAL, keys(ref, at.a, at.c), twin_buf.at[s, 3, t])
        for ref in (own_q, own_k, own_v):
            clear(mine(ref), LOCAL)
        if s == 0:
            for copy in kept:
                copy.wait()
        own_grads(at, ITSELF)
        own_grads(at, BEFORE)
        yield
        kr0.wait_recv()
        add(k_far.at[s, 2], 0, LOCAL, k_all.at[s, 1, 0], k_far.at[s, 0])
        kr2 = go(k_far.at[s, 2], k_in.at[s, 0], at.right)
        kl0.wait_recv()
        add(k_far.at[s, 3], 0, LOCAL, k_all.at[s, 2, 1], k_far.at[s, 1])
        kl2 = go(k_far.at[s, 3], v_in.at[s, 1], at.left)
        yield
        for copy in (qu1, ql1, qu2, ql2, kr1, kl1, kr2, kl2):
            copy.wait_recv()

    in_turn(work(0), work(1))
    copies.finish_sends()


def summed(dq, dk, dv, full, *args):
    block = (LOCAL, BLK, WIDE)
    own = VMEM((2 * LOCAL, BLK, WIDE), F32)
    came = VMEM((2, 2, *block), BF16)
    return pl.pallas_call(
        sum_kernel,
        out_shape=(came, came, came, came, own, own, own),
        in_specs=[whole(VMEM)] * 4 + [whole(pltpu.HBM)] * 4,
        out_specs=(whole(VMEM),) * 7,
        scratch_shapes=[
            VMEM((4, ROWS, COLS), BF16),
            VMEM((2, SIDE, 2, *block), BF16),
            VMEM((2, SIDE - 1, 2, *block), BF16),
            VMEM((2, 2, *block), BF16),
            VMEM((2, 4, *block), BF16),
            pltpu.SemaphoreType.DMA((N_SUM,)),
            pltpu.SemaphoreType.DMA((N_SUM,)),
            pltpu.SemaphoreType.DMA((4,)),
        ],
        compiler_params=pltpu.CompilerParams(
            collective_id=2, has_side_effects=True, vmem_limit_bytes=18 * MIB
        ),
        name="sum_grads",
    )(*pinned(dq, dk, dv, full), *args)


def leave(dst, s, scale, *terms):
    for n in range(LOCAL):
        total = terms[0][n].astype(F32)
        for term in terms[1:]:
            total = total + term[n].astype(F32)
        dst[n * BLK : (n + 1) * BLK, s * WIDE : (s + 1) * WIDE] = (total * scale).astype(BF16)


def leave_kernel(
    dq_ref, q_in, k_in, v_in, k_own, own_q, own_k, own_v, gq_out, gk_out, gv_out, gq_ref, gk_ref, gv_ref, sem
):
    halves = [Half(0), Half(1)]

    def mine(ref, s):
        return ref.at[pl.ds(s * LOCAL, LOCAL)]

    copies = []

    def hand_out(src, dst):
        copies.append(pltpu.make_async_copy(src, dst, sem.at[len(copies)]))
        copies[-1].start()

    for at in halves:
        queries = dq_ref.at[pl.ds(at.q_at * LOCAL, LOCAL)]
        leave(gq_ref, at.s, SCALE, mine(own_q, at.s), queries, q_in.at[at.s, 0], q_in.at[at.s, 1])
    hand_out(gq_ref, gq_out)
    for s in range(2):
        leave(gv_ref, s, 1.0, mine(own_v, s), k_own.at[s, 1], v_in.at[s, 0], v_in.at[s, 1])
    hand_out(gv_ref, gv_out)
    for s in range(2):
        leave(gk_ref, s, SCALE, mine(own_k, s), k_own.at[s, 0], k_in.at[s, 0], k_in.at[s, 1])
    hand_out(gk_ref, gk_out)
    for copy in copies:
        copy.wait()


def left(*sums):
    return pl.pallas_call(
        leave_kernel,
        out_shape=(pltpu.HBM((ROWS, COLS), BF16),) * 3,
        in_specs=[whole(VMEM)] * 8,
        out_specs=(whole(pltpu.HBM),) * 3,
        scratch_shapes=[VMEM((ROWS, COLS), BF16)] * 3 + [pltpu.SemaphoreType.DMA((3,))],
        compiler_params=pltpu.CompilerParams(vmem_limit_bytes=4 * MIB),
        name="leave",
    )(*pinned(*sums))


def per_device(query, key, value, out_grad, links):
    args = [pltpu.with_memory_space_constraint(v, pltpu.HBM) for v in (query, out_grad, key, value)]
    qg, kg, qt, entries, part, dq, dk, dv = gathered(*args, links.T)
    full = joined_stats(partial_stats(entries, qt, kg, part))
    dq, dk, dv = partial_grads(entries, qg, qt, kg, full, dq, dk, dv)
    return left(dq, *summed(dq, dk, dv, full, *args))


def solution(mesh):
    spec = P("ctx", "head")
    return jax.shard_map(
        per_device,
        mesh=mesh,
        in_specs=(spec, spec, spec, spec, P()),
        out_specs=(spec, spec, spec),
        check_vma=False,
    )
```

```python
import functools

import jax
import jax.numpy as jnp
from jax import lax
from jax.experimental import pallas as pl
from jax.experimental.pallas import tpu as pltpu
from jax.sharding import PartitionSpec as P

HEAD_DIM = 128
BLK = 128
LINKS = 6
HEADS = 2
SIDE = 4
NG = 8
LOCAL = 4
ROWS = 512
COLS = 512
WIDE = HEADS * HEAD_DIM
NQ = 2 * SIDE * LOCAL
NK = 2 * NG * LOCAL
TURNED = 2 * WIDE
HOLDERS = 2 * SIDE
LINES = LOCAL * HEADS
LAST = 63
TILES = (slice(0, HEAD_DIM), slice(HEAD_DIM, WIDE))
MANY, SOME, FEW = 16, 8, 4
LIST = 256
NEG = -1e30
SCALE = HEAD_DIM**-0.5
LOG2E = 1.4426950408889634
MESH = pl.DeviceIdType.MESH
BF16 = jnp.bfloat16
F32 = jnp.float32
VMEM = pltpu.VMEM
MIB = 1 << 20


def whole(space):
    return pl.BlockSpec(memory_space=space)


def pinned(*arrays):
    return [pltpu.with_memory_space_constraint(array, VMEM) for array in arrays]


def place():
    me = lax.axis_index("ctx")
    return me // 8, (me // 2) % 4, me % 2


class Half:
    def __init__(self, s):
        x, y, c = place()
        self.s, self.c = s, c
        self.a, self.b = (x, y) if s == 0 else (y, x)
        self.q_at, self.k_at = s * SIDE + self.b, s * NG + self.a * 2 + c
        self.a_up, self.a_down, self.a_far = [(self.a + n) % SIDE for n in (1, 3, 2)]
        self.b_up, self.b_down, self.b_far = [(self.b + n) % SIDE for n in (1, 3, 2)]
        self.right, self.left = self.at(self.a_up, self.b, c), self.at(self.a_down, self.b, c)
        self.upper, self.lower = self.at(self.a, self.b_up, c), self.at(self.a, self.b_down, c)
        self.twin = self.at(self.a, self.b, 1 - c)

    def at(self, a, b, c):
        x, y = (a, b) if self.s == 0 else (b, a)
        return ((x * SIDE + y) * 2 + c, lax.axis_index("head"))


def barrier_with(partners):
    sem = pltpu.get_barrier_semaphore()
    for partner in partners:
        pl.semaphore_signal(sem, inc=1, device_id=partner, device_id_type=MESH)
    pl.semaphore_wait(sem, len(partners))


class Copies:
    def __init__(self, send_sem, recv_sem):
        self.send_sem, self.recv_sem, self.made = send_sem, recv_sem, []

    def start(self, src, dst, device):
        n = len(self.made)
        copy = pltpu.make_async_remote_copy(
            src_ref=src,
            dst_ref=dst,
            send_sem=self.send_sem.at[n],
            recv_sem=self.recv_sem.at[n],
            device_id=device,
            device_id_type=MESH,
        )
        copy.start()
        self.made.append(copy)
        return copy

    def finish_sends(self):
        for copy in self.made:
            copy.wait_send()


def nt(a, b):
    return lax.dot_general(a, b, (((1,), (1,)), ((), ())), preferred_element_type=F32)


def nn(a, b):
    return lax.dot_general(a, b, (((1,), (0,)), ((), ())), preferred_element_type=F32)


def tn(a, b):
    return lax.dot_general(a, b, (((0,), (0,)), ((), ())), preferred_element_type=F32)


def in_turn(*works):
    works = list(works)
    while works:
        for work in list(works):
            if next(work, works) is works:
                works.remove(work)


def index_of_holder(block):
    stretch = block // 2
    late = stretch > LAST // 2
    return jnp.where(late, LAST - stretch, stretch), block % 2 + jnp.where(late, 2, 0)


def write_list(links_ref, named_ref, list_ref):
    shape = (8, BLK)
    block = lax.broadcasted_iota(jnp.int32, shape, 1)
    row = lax.broadcasted_iota(jnp.int32, shape, 0)
    named_ref[...] = block - 1
    named_ref[0:LINKS, :] = links_ref[...]
    named = named_ref[...]
    q_dev, q_local = index_of_holder(block)
    k_dev, k_local = index_of_holder(jnp.maximum(named, 0))
    within = jnp.logical_or(row > LINKS, jnp.logical_and(row == LINKS, block % 2 == 1))
    used = jnp.logical_and(named >= 0, jnp.logical_not(within))
    keys = lax.broadcasted_iota(jnp.int32, (BLK, BLK), 0)
    lanes = lax.broadcasted_iota(jnp.int32, (BLK, BLK), 1)
    before = jnp.where(keys < lanes, 1.0, 0.0).astype(BF16)
    out = [jnp.zeros(shape, F32) for _ in range(LIST // BLK)]
    base = jnp.zeros((1, 1), F32)
    for s in range(2):
        half = Half(s)
        q_x, q_y, k_x, k_y = q_dev // 8, (q_dev // 2) % 4, k_dev // 8, (k_dev // 2) % 4
        q_a, q_b = (q_x, q_y) if s == 0 else (q_y, q_x)
        k_a, k_b = (k_x, k_y) if s == 0 else (k_y, k_x)
        meets = jnp.logical_and(q_a * 2 + q_dev % 2 == half.a * 2 + half.c, k_b == half.b)
        here = jnp.where(jnp.logical_and(used, meets), 1.0, 0.0)
        q_slot = (s * SIDE + q_b) * LOCAL + q_local
        k_slot = (s * NG + k_a * 2 + k_dev % 2) * LOCAL + k_local
        at = base + jnp.sum(nn(here.astype(BF16), before), axis=0, keepdims=True)
        for t in range(LINKS + 1):
            flag = here[t : t + 1, :]
            values = jnp.where(row == 0, q_slot[t : t + 1, :], k_slot[t : t + 1, :]).astype(F32)
            for n in range(LIST // BLK):
                spot = keys.astype(F32) + float(n * BLK)
                hot = jnp.where(spot == at, flag, 0.0).astype(BF16)
                out[n] = out[n] + nt(values.astype(BF16), hot)
            at = at + flag
        base = base + jnp.sum(jnp.sum(here, axis=1, keepdims=True), axis=0, keepdims=True)
    for n in range(LIST // BLK):
        spot = block.astype(F32) + float(n * BLK)
        spare = jnp.where(row == 0, float(NQ), float(NK))
        full = jnp.where(row == 2, base, jnp.where(spot < base, out[n], spare)).astype(jnp.int32)
        q, k = jnp.bitwise_and(full[0:1, :], NQ - 1), jnp.bitwise_and(full[1:2, :], NK - 1)
        for at_row, values in ((3, first_row(k)), (4, q * TURNED), (5, first_row(q))):
            full = jnp.where(row == at_row, values, full)
        list_ref[:, n * BLK : (n + 1) * BLK] = full


def first_row(slot):
    return slot // LOCAL * (2 * ROWS) + slot % LOCAL * BLK


def rows(first, count=BLK):
    return pl.ds(pl.multiple_of(first, BLK), count)


class Entry:
    def __init__(self, q_to, k_to, keys, values, queries_t, out_grads_t, causal=False):
        self.q_to, self.k_to, self.keys = q_to, k_to, keys
        self.score = [nn(k, q) * (SCALE * LOG2E) for k, q in zip(keys, queries_t)]
        self.dprob = [nn(v, o) for v, o in zip(values, out_grads_t)]
        if causal:
            down = lax.broadcasted_iota(jnp.int32, (BLK, BLK), 0)
            live = down <= lax.broadcasted_iota(jnp.int32, (BLK, BLK), 1)
            self.score = [jnp.where(live, score, NEG) for score in self.score]


def met(q_to, k_to, k_row, turned_row, qt_ref, kg_ref, causal=False):
    keys, values = [[kg_ref[rows(k_row + n * ROWS), tile] for tile in TILES] for n in range(2)]
    turned = [[qt_ref[rows(turned_row + n * WIDE + tile.start), :] for tile in TILES] for n in range(2)]
    return Entry(q_to, k_to, keys, values, *turned, causal)


ITSELF = tuple((n, n) for n in range(LOCAL))
BEFORE = ((1, 0), (3, 2))


def listed_entries(list_ref, qt_ref, kg_ref, finish):
    def batch(first, count):
        entries = []
        for at in [first + u for u in range(count)]:
            q_to, k_to, _, k_row, turned_row, q_row = [list_ref[m, at] for m in range(6)]
            e = met(q_to, k_to, k_row, turned_row, qt_ref, kg_ref)
            e.q_row = q_row
            entries.append(e)
        finish(entries)
        return 0

    full = lax.div(list_ref[2, 0], MANY)
    rest = list_ref[2, 0] - full * MANY
    some = lax.div(rest + (SOME - FEW - 1), SOME)
    left_over = rest - some * SOME
    lax.fori_loop(0, full, lambda n, _: batch(n * MANY, MANY), 0)
    lax.fori_loop(0, some, lambda n, _: batch(full * MANY + n * SOME, SOME), 0)

    @pl.when(left_over > 0)
    def _():
        batch(full * MANY + some * SOME, FEW)


def stats_place(q_slot):
    return lax.div(q_slot, LOCAL), pl.ds(lax.rem(q_slot, LOCAL) * HEADS, HEADS)


def add_stats(part_ref, entries):
    found = []
    for e in entries:
        tops = [jnp.max(score, axis=0, keepdims=True) for score in e.score]
        probs = [jnp.exp2(score - top) for score, top in zip(e.score, tops)]
        sums = [jnp.sum(prob, axis=0, keepdims=True) for prob in probs]
        dots = [jnp.sum(p * d, axis=0, keepdims=True) for p, d in zip(probs, e.dprob)]
        found.append([jnp.concatenate(lines, axis=0) for lines in (tops, sums, dots)])
    for e, (top, total, dot) in zip(entries, found):
        holder, lines = stats_place(e.q_to)
        old_top = part_ref[holder, 0, lines, :]
        new_top = jnp.maximum(old_top, top)
        was, now = jnp.exp2(old_top - new_top), jnp.exp2(top - new_top)
        part_ref[holder, 0, lines, :] = new_top
        part_ref[holder, 1, lines, :] = part_ref[holder, 1, lines, :] * was + total * now
        part_ref[holder, 2, lines, :] = part_ref[holder, 2, lines, :] * was + dot * now


def add_grads(dq_ref, dk_ref, dv_ref, full_ref, stats_slot, queries, out_grads, entries):
    found = []
    for e in entries:
        holder, lines = stats_place(stats_slot(e))
        lse, delta = full_ref[holder, 0, lines, :], full_ref[holder, 1, lines, :]
        dq, dk, dv = [], [], []
        for i in range(HEADS):
            prob = jnp.exp2(e.score[i] - lse[i : i + 1])
            dscore = (prob * (e.dprob[i] - delta[i : i + 1])).astype(BF16)
            dk.append(nn(dscore, queries(e, i)))
            dv.append(nn(prob.astype(BF16), out_grads(e, i)))
            dq.append(tn(dscore, e.keys[i]))
        found.append([jnp.concatenate(terms, axis=1) for terms in (dq, dk, dv)])
    for e, (dq, dk, dv) in zip(entries, found):
        dq_ref[e.q_to] += dq.astype(dq_ref.dtype)
        dk_ref[e.k_to] += dk.astype(dk_ref.dtype)
        dv_ref[e.k_to] += dv.astype(dv_ref.dtype)


def clear(ref, count):
    def body(n, _):
        ref[n] = jnp.zeros(ref.shape[1:], ref.dtype)
        return 0

    lax.fori_loop(0, count, body, 0)


N_GATHER = 44


def gather_kernel(
    q_ref, o_ref, k_ref, v_ref, links_ref,
    qg_ref, kg_ref, qt_ref, list_ref, part_ref, dq_ref, dk_ref, dv_ref,
    table_ref, named_ref, send_sem, recv_sem, own_sem,
):
    copies = Copies(send_sem, recv_sem)
    go = copies.start
    own = []
    table = pltpu.make_async_copy(links_ref, table_ref, own_sem.at[8])
    table.start()

    def columns(ref, s):
        return ref.at[:, s * WIDE : (s + 1) * WIDE]

    def part(ref, at, n):
        return ref.at[rows((at * 2 + n) * ROWS, ROWS)]

    def keep(src, dst):
        copy = pltpu.make_async_copy(src, dst, own_sem.at[len(own)])
        copy.start()
        own.append(copy)

    def turn(g, a, first=0, last=LOCAL):
        def body(lb, _):
            for tile in TILES:
                turned = (g * LOCAL + lb) * TURNED + a * WIDE + tile.start
                qt_ref[rows(turned), :] = qg_ref[rows((g * 2 + a) * ROWS + lb * BLK), tile].T
            return 0

        lax.fori_loop(first, last, body, 0)

    def work(s):
        at = Half(s)
        ka, qa = at.k_at, at.q_at
        q, o, k, v = [columns(ref, s) for ref in (q_ref, o_ref, k_ref, v_ref)]
        keep(q, part(qg_ref, qa, 0))
        keep(o, part(qg_ref, qa, 1))
        keep(k, part(kg_ref, ka, 0))
        keep(v, part(kg_ref, ka, 1))
        if s == 0:
            barrier_with([at.right, at.left, at.upper, at.lower, at.twin])
        yield
        kr0 = go(k, part(kg_ref, ka, 0), at.right)
        kl1 = go(v, part(kg_ref, ka, 1), at.left)
        yield
        qu0 = go(q, part(qg_ref, qa, 0), at.upper)
        ql1 = go(o, part(qg_ref, qa, 1), at.lower)
        yield
        kr1 = go(v, part(kg_ref, ka, 1), at.right)
        kl0 = go(k, part(kg_ref, ka, 0), at.left)
        twins = [go(k, part(kg_ref, ka, 0), at.twin), go(v, part(kg_ref, ka, 1), at.twin)]
        yield
        qu1 = go(o, part(qg_ref, qa, 1), at.upper)
        ql0 = go(q, part(qg_ref, qa, 0), at.lower)
        yield
        if s == 0:
            table.wait()
            write_list(table_ref, named_ref, list_ref)
            part_ref[:, 0] = jnp.full((HOLDERS + 1, LINES, BLK), NEG, F32)
            part_ref[:, 1:3] = jnp.zeros((HOLDERS + 1, 2, LINES, BLK), F32)
        for copy in own[4 * s : 4 * s + 4]:
            copy.wait()
        turn(qa, 0)
        turn(qa, 1)
        yield
        for pairs in (ITSELF, BEFORE):
            entries = []
            for m, n in pairs:
                q_slot, k_slot = qa * LOCAL + m, ka * LOCAL + n
                k_row, turned_row = ka * (2 * ROWS) + n * BLK, q_slot * TURNED
                entries.append(met(q_slot, k_slot, k_row, turned_row, qt_ref, kg_ref, pairs is ITSELF))
            add_stats(part_ref, entries)
        if s == 0:
            clear(dk_ref, NK + 1)
        else:
            clear(dq_ref, NQ + 1)
            clear(dv_ref, NK + 1)
        yield

        def on(ref, holder, n, device, piece=None):
            slot = part(ref, holder, n)
            if piece is not None:
                slot = ref.at[rows((holder * 2 + n) * ROWS + piece * (ROWS // 2), ROWS // 2)]
            return go(slot, slot, device)

        def keys(a):
            return s * NG + a * 2 + at.c

        def queries(b):
            return s * SIDE + b

        kr0.wait_recv()
        kr2 = on(kg_ref, keys(at.a_down), 0, at.right)
        twins.append(on(kg_ref, keys(at.a_down), 0, at.twin))
        kl1.wait_recv()
        kl2 = on(kg_ref, keys(at.a_up), 1, at.left)
        twins.append(on(kg_ref, keys(at.a_up), 1, at.twin))
        yield
        qu0.wait_recv()
        qu2 = [on(qg_ref, queries(at.b_down), 0, at.upper, n) for n in range(2)]
        ql1.wait_recv()
        ql2 = [on(qg_ref, queries(at.b_up), 1, at.lower, n) for n in range(2)]
        yield
        turn(queries(at.b_down), 0)
        turn(queries(at.b_up), 1)
        yield
        kr1.wait_recv()
        twins.append(on(kg_ref, keys(at.a_down), 1, at.twin))
        kl0.wait_recv()
        twins.append(on(kg_ref, keys(at.a_up), 0, at.twin))
        yield
        qu1.wait_recv()
        turn(queries(at.b_down), 1)
        ql0.wait_recv()
        turn(queries(at.b_up), 0)
        yield
        kr2.wait_recv()
        twins.append(on(kg_ref, keys(at.a_far), 0, at.twin))
        kl2.wait_recv()
        twins.append(on(kg_ref, keys(at.a_far), 1, at.twin))
        yield
        for n in range(2):
            if n == 1:
                yield
            qu2[n].wait_recv()
            turn(queries(at.b_far), 0, 2 * n, 2 * n + 2)
            ql2[n].wait_recv()
            turn(queries(at.b_far), 1, 2 * n, 2 * n + 2)
        for copy in twins:
            copy.wait_recv()

    in_turn(work(0), work(1))
    copies.finish_sends()


def gathered(query, out_grad, key, value, links):
    return pl.pallas_call(
        gather_kernel,
        out_shape=(
            VMEM((2 * SIDE * 2 * ROWS, WIDE), BF16),
            VMEM((2 * NG * 2 * ROWS, WIDE), BF16),
            VMEM((NQ * TURNED, BLK), BF16),
            VMEM((8, LIST), jnp.int32),
            VMEM((HOLDERS + 1, 3, LINES, BLK), F32),
            VMEM((NQ + 1, BLK, WIDE), BF16),
            VMEM((NK + 1, BLK, WIDE), BF16),
            VMEM((NK + 1, BLK, WIDE), BF16),
        ),
        in_specs=[whole(pltpu.HBM)] * 5,
        out_specs=(whole(VMEM),) * 8,
        scratch_shapes=[
            VMEM((LINKS, BLK), jnp.int32),
            VMEM((8, BLK), jnp.int32),
            pltpu.SemaphoreType.DMA((N_GATHER,)),
            pltpu.SemaphoreType.DMA((N_GATHER,)),
            pltpu.SemaphoreType.DMA((9,)),
        ],
        compiler_params=pltpu.CompilerParams(
            collective_id=0, has_side_effects=True, vmem_limit_bytes=8 * MIB
        ),
        name="gather",
    )(query, out_grad, key, value, pltpu.with_memory_space_constraint(links, pltpu.HBM))


def stats_kernel(list_ref, qt_ref, kg_ref, first_ref, part_ref):
    del first_ref
    listed_entries(list_ref, qt_ref, kg_ref, functools.partial(add_stats, part_ref))


def partial_stats(entries, qt, kg, part):
    return pl.pallas_call(
        stats_kernel,
        out_shape=VMEM((HOLDERS + 1, 3, LINES, BLK), F32),
        in_specs=[whole(pltpu.SMEM)] + [whole(VMEM)] * 3,
        out_specs=whole(VMEM),
        input_output_aliases={3: 0},
        compiler_params=pltpu.CompilerParams(vmem_limit_bytes=8 * MIB),
        name="partial_stats",
    )(entries, *pinned(qt, kg, part))


def merged(parts):
    tops = [part[0] for part in parts]
    top = functools.reduce(jnp.maximum, tops)
    weights = [jnp.exp2(t - top) for t in tops]
    total = sum(part[1] * w for part, w in zip(parts, weights))
    dot = sum(part[2] * w for part, w in zip(parts, weights))
    return top, total, dot


def join_kernel(part_ref, full_ref, got_ref, send_sem, recv_sem):
    halves = [Half(0), Half(1)]

    def around(at):
        return [(b, at.at(at.a, b, at.c)) for b in (at.b_far, at.b_up, at.b_down)]

    barrier_with([device for at in halves for _, device in around(at)])
    copies = Copies(send_sem, recv_sem)
    first = [[], []]
    for n in range(SIDE - 1):
        for at in halves:
            b, device = around(at)[n]
            first[at.s].append(copies.start(part_ref.at[at.s * SIDE + b], got_ref.at[at.s, n], device))
    later = []
    for at in halves:
        for copy in first[at.s]:
            copy.wait_recv()
        top, total, dot = merged([part_ref[at.q_at]] + [got_ref[at.s, n] for n in range(SIDE - 1)])
        full_ref[at.q_at, 0] = top + jnp.log(total) * LOG2E
        full_ref[at.q_at, 1] = dot / total
        for _, device in around(at):
            later.append(copies.start(full_ref.at[at.q_at], full_ref.at[at.q_at], device))
    for copy in later:
        copy.wait_recv()
    copies.finish_sends()


def joined_stats(part):
    return pl.pallas_call(
        join_kernel,
        out_shape=VMEM((HOLDERS, 2, LINES, BLK), F32),
        in_specs=[whole(VMEM)],
        out_specs=whole(VMEM),
        scratch_shapes=[
            VMEM((2, SIDE - 1, 3, LINES, BLK), F32),
            pltpu.SemaphoreType.DMA((12,)),
            pltpu.SemaphoreType.DMA((12,)),
        ],
        compiler_params=pltpu.CompilerParams(
            collective_id=1, has_side_effects=True, vmem_limit_bytes=8 * MIB
        ),
        name="join_stats",
    )(*pinned(part))


def grads_kernel(
    list_ref, qg_ref, qt_ref, kg_ref, full_ref, zero_q, zero_k, zero_v, dq_ref, dk_ref, dv_ref
):
    del zero_q, zero_k, zero_v

    def tiles(n):
        return lambda e, i: qg_ref[rows(e.q_row + n * ROWS), TILES[i]]

    finish = functools.partial(
        add_grads, dq_ref, dk_ref, dv_ref, full_ref, lambda e: jnp.bitwise_and(e.q_to, NQ - 1), tiles(0), tiles(1)
    )
    listed_entries(list_ref, qt_ref, kg_ref, finish)


def partial_grads(entries, qg, qt, kg, full, dq, dk, dv):
    return pl.pallas_call(
        grads_kernel,
        out_shape=(
            VMEM((NQ + 1, BLK, WIDE), BF16),
            VMEM((NK + 1, BLK, WIDE), BF16),
            VMEM((NK + 1, BLK, WIDE), BF16),
        ),
        in_specs=[whole(pltpu.SMEM)] + [whole(VMEM)] * 7,
        out_specs=(whole(VMEM),) * 3,
        input_output_aliases={5: 0, 6: 1, 7: 2},
        compiler_params=pltpu.CompilerParams(vmem_limit_bytes=8 * MIB),
        name="partial_grads",
    )(entries, *pinned(qg, qt, kg, full, dq, dk, dv))


N_SUM = 40


def add(dst, first, last, *terms):
    def body(n, _):
        total = terms[0][n].astype(F32)
        for term in terms[1:]:
            total = total + term[n].astype(F32)
        dst[n] = total.astype(BF16)
        return 0

    lax.fori_loop(first, last, body, 0)


def sum_kernel(
    dq_ref, dk_ref, dv_ref, full_ref, q_ref, o_ref, k_ref, v_ref,
    q_in, k_in, v_in, k_own, own_q, own_k, own_v,
    own_ref, twin_buf, k_all, q_far, k_far, send_sem, recv_sem, own_sem,
):
    copies = Copies(send_sem, recv_sem)
    go = copies.start
    low, high = pl.ds(0, 2), pl.ds(2, 2)
    kept = [
        pltpu.make_async_copy(ref, own_ref.at[n], own_sem.at[n])
        for n, ref in enumerate((q_ref, o_ref, k_ref, v_ref))
    ]
    for copy in kept:
        copy.start()

    def own_grads(at, pairs):
        def block(n, lb):
            return [
                own_ref[n, lb * BLK : (lb + 1) * BLK, (at.s * HEADS + i) * HEAD_DIM : (at.s * HEADS + i + 1) * HEAD_DIM]
                for i in range(HEADS)
            ]

        def turned(n, lb):
            return [tile.T for tile in block(n, lb)]

        base = at.s * LOCAL
        entries = []
        for m, n in pairs:
            e = Entry(base + m, base + n, block(2, n), block(3, n), turned(0, m), turned(1, m), pairs is ITSELF)
            e.local = m
            entries.append(e)

        def stats_slot(e):
            return at.q_at * LOCAL + e.local

        add_grads(
            own_q, own_k, own_v, full_ref, stats_slot,
            lambda e, i: block(0, e.local)[i], lambda e, i: block(1, e.local)[i], entries,
        )


    def work(s):
        at = Half(s)
        if s == 0:
            barrier_with([at.right, at.left, at.upper, at.lower, at.twin])
        yield

        def mine(ref):
            return ref.at[pl.ds(s * LOCAL, LOCAL)]

        def keys(ref, a, c):
            return ref.at[pl.ds((s * NG + a * 2 + c) * LOCAL, LOCAL)]

        def queries(b):
            return dq_ref.at[pl.ds((s * SIDE + b) * LOCAL, LOCAL)]

        order = (at.a_far, at.a_up, at.a_down, at.a)
        pairs = [
            [go(keys(ref, a, 1 - at.c), twin_buf.at[s, n, t], at.twin) for t, ref in enumerate((dk_ref, dv_ref))]
            for n, a in enumerate(order)
        ]
        qu0 = go(queries(at.b_far).at[low], q_far.at[s, 0, low], at.upper)
        ql0 = go(queries(at.b_far).at[high], q_far.at[s, 0, high], at.lower)
        yield
        qu1 = go(queries(at.b_up).at[high], q_in.at[s, 0, high], at.upper)
        ql1 = go(queries(at.b_down).at[low], q_in.at[s, 1, low], at.lower)
        yield

        def take(n, t):
            pairs[n][t].wait_recv()
            ref = (dk_ref, dv_ref)[t]
            add(k_all.at[s, n, t], 0, LOCAL, keys(ref, order[n], at.c), twin_buf.at[s, n, t])
            return k_all.at[s, n, t]

        kr0 = go(take(0, 0), k_far.at[s, 0], at.right)
        kl0 = go(take(0, 1), k_far.at[s, 1], at.left)
        yield
        kr1 = go(take(1, 1), v_in.at[s, 0], at.right)
        kl1 = go(take(2, 0), k_in.at[s, 1], at.left)
        yield
        qu0.wait_recv()
        add(q_far.at[s, 1], 0, 2, queries(at.b_up), q_far.at[s, 0])
        qu2 = go(q_far.at[s, 1, low], q_in.at[s, 0, low], at.upper)
        ql0.wait_recv()
        add(q_far.at[s, 1], 2, LOCAL, queries(at.b_down), q_far.at[s, 0])
        ql2 = go(q_far.at[s, 1, high], q_in.at[s, 1, high], at.lower)
        yield
        for n, t in ((1, 0), (2, 1)):
            take(n, t)
        for t, ref in enumerate((dk_ref, dv_ref)):
            pairs[3][t].wait_recv()
            add(k_own.at[s, t], 0, LOCAL, keys(ref, at.a, at.c), twin_buf.at[s, 3, t])
        for ref in (own_q, own_k, own_v):
            clear(mine(ref), LOCAL)
        if s == 0:
            for copy in kept:
                copy.wait()
        own_grads(at, ITSELF)
        own_grads(at, BEFORE)
        yield
        kr0.wait_recv()
        add(k_far.at[s, 2], 0, LOCAL, k_all.at[s, 1, 0], k_far.at[s, 0])
        kr2 = go(k_far.at[s, 2], k_in.at[s, 0], at.right)
        kl0.wait_recv()
        add(k_far.at[s, 3], 0, LOCAL, k_all.at[s, 2, 1], k_far.at[s, 1])
        kl2 = go(k_far.at[s, 3], v_in.at[s, 1], at.left)
        yield
        for copy in (qu1, ql1, qu2, ql2, kr1, kl1, kr2, kl2):
            copy.wait_recv()

    in_turn(work(0), work(1))
    copies.finish_sends()


def summed(dq, dk, dv, full, *args):
    block = (LOCAL, BLK, WIDE)
    own = VMEM((2 * LOCAL, BLK, WIDE), F32)
    came = VMEM((2, 2, *block), BF16)
    return pl.pallas_call(
        sum_kernel,
        out_shape=(came, came, came, came, own, own, own),
        in_specs=[whole(VMEM)] * 4 + [whole(pltpu.HBM)] * 4,
        out_specs=(whole(VMEM),) * 7,
        scratch_shapes=[
            VMEM((4, ROWS, COLS), BF16),
            VMEM((2, SIDE, 2, *block), BF16),
            VMEM((2, SIDE - 1, 2, *block), BF16),
            VMEM((2, 2, *block), BF16),
            VMEM((2, 4, *block), BF16),
            pltpu.SemaphoreType.DMA((N_SUM,)),
            pltpu.SemaphoreType.DMA((N_SUM,)),
            pltpu.SemaphoreType.DMA((4,)),
        ],
        compiler_params=pltpu.CompilerParams(
            collective_id=2, has_side_effects=True, vmem_limit_bytes=18 * MIB
        ),
        name="sum_grads",
    )(*pinned(dq, dk, dv, full), *args)


def leave(dst, s, scale, *terms):
    for n in range(LOCAL):
        total = terms[0][n].astype(F32)
        for term in terms[1:]:
            total = total + term[n].astype(F32)
        dst[n * BLK : (n + 1) * BLK, s * WIDE : (s + 1) * WIDE] = (total * scale).astype(BF16)


def leave_kernel(
    dq_ref, q_in, k_in, v_in, k_own, own_q, own_k, own_v, gq_out, gk_out, gv_out, gq_ref, gk_ref, gv_ref, sem
):
    halves = [Half(0), Half(1)]

    def mine(ref, s):
        return ref.at[pl.ds(s * LOCAL, LOCAL)]

    copies = []

    def hand_out(src, dst):
        copies.append(pltpu.make_async_copy(src, dst, sem.at[len(copies)]))
        copies[-1].start()

    for at in halves:
        queries = dq_ref.at[pl.ds(at.q_at * LOCAL, LOCAL)]
        leave(gq_ref, at.s, SCALE, mine(own_q, at.s), queries, q_in.at[at.s, 0], q_in.at[at.s, 1])
    hand_out(gq_ref, gq_out)
    for s in range(2):
        leave(gv_ref, s, 1.0, mine(own_v, s), k_own.at[s, 1], v_in.at[s, 0], v_in.at[s, 1])
    hand_out(gv_ref, gv_out)
    for s in range(2):
        leave(gk_ref, s, SCALE, mine(own_k, s), k_own.at[s, 0], k_in.at[s, 0], k_in.at[s, 1])
    hand_out(gk_ref, gk_out)
    for copy in copies:
        copy.wait()


def left(*sums):
    return pl.pallas_call(
        leave_kernel,
        out_shape=(pltpu.HBM((ROWS, COLS), BF16),) * 3,
        in_specs=[whole(VMEM)] * 8,
        out_specs=(whole(pltpu.HBM),) * 3,
        scratch_shapes=[VMEM((ROWS, COLS), BF16)] * 3 + [pltpu.SemaphoreType.DMA((3,))],
        compiler_params=pltpu.CompilerParams(vmem_limit_bytes=4 * MIB),
        name="leave",
    )(*pinned(*sums))


def per_device(query, key, value, out_grad, links):
    args = [pltpu.with_memory_space_constraint(v, pltpu.HBM) for v in (query, out_grad, key, value)]
    qg, kg, qt, entries, part, dq, dk, dv = gathered(*args, links.T)
    full = joined_stats(partial_stats(entries, qt, kg, part))
    dq, dk, dv = partial_grads(entries, qg, qt, kg, full, dq, dk, dv)
    return left(dq, *summed(dq, dk, dv, full, *args))


def solution(mesh):
    spec = P("ctx", "head")
    return jax.shard_map(
        per_device,
        mesh=mesh,
        in_specs=(spec, spec, spec, spec, P()),
        out_specs=(spec, spec, spec),
        check_vma=False,
    )
```

```python
import functools

import jax
import jax.numpy as jnp
from jax import lax
from jax.experimental import pallas as pl
from jax.experimental.pallas import tpu as pltpu
from jax.sharding import PartitionSpec as P

HEAD_DIM = 128
BLK = 128
LINKS = 6
HEADS = 2
SIDE = 4
NG = 8
LOCAL = 4
ROWS = 512
COLS = 512
WIDE = HEADS * HEAD_DIM
NQ = 2 * SIDE * LOCAL
NK = 2 * NG * LOCAL
TURNED = 2 * WIDE
HOLDERS = 2 * SIDE
LINES = LOCAL * HEADS
LAST = 63
TILES = (slice(0, HEAD_DIM), slice(HEAD_DIM, WIDE))
MANY, SOME, FEW = 16, 8, 4
LIST = 256
NEG = -1e30
SCALE = HEAD_DIM**-0.5
LOG2E = 1.4426950408889634
MESH = pl.DeviceIdType.MESH
BF16 = jnp.bfloat16
F32 = jnp.float32
VMEM = pltpu.VMEM
MIB = 1 << 20


def whole(space):
    return pl.BlockSpec(memory_space=space)


def pinned(*arrays):
    return [pltpu.with_memory_space_constraint(array, VMEM) for array in arrays]


def place():
    me = lax.axis_index("ctx")
    return me // 8, (me // 2) % 4, me % 2


class Half:
    def __init__(self, s):
        x, y, c = place()
        self.s, self.c = s, c
        self.a, self.b = (x, y) if s == 0 else (y, x)
        self.q_at, self.k_at = s * SIDE + self.b, s * NG + self.a * 2 + c
        self.a_up, self.a_down, self.a_far = [(self.a + n) % SIDE for n in (1, 3, 2)]
        self.b_up, self.b_down, self.b_far = [(self.b + n) % SIDE for n in (1, 3, 2)]
        self.right, self.left = self.at(self.a_up, self.b, c), self.at(self.a_down, self.b, c)
        self.upper, self.lower = self.at(self.a, self.b_up, c), self.at(self.a, self.b_down, c)
        self.twin = self.at(self.a, self.b, 1 - c)

    def at(self, a, b, c):
        x, y = (a, b) if self.s == 0 else (b, a)
        return ((x * SIDE + y) * 2 + c, lax.axis_index("head"))


def barrier_with(partners):
    sem = pltpu.get_barrier_semaphore()
    for partner in partners:
        pl.semaphore_signal(sem, inc=1, device_id=partner, device_id_type=MESH)
    pl.semaphore_wait(sem, len(partners))


class Copies:
    def __init__(self, send_sem, recv_sem):
        self.send_sem, self.recv_sem, self.made = send_sem, recv_sem, []

    def start(self, src, dst, device):
        n = len(self.made)
        copy = pltpu.make_async_remote_copy(
            src_ref=src,
            dst_ref=dst,
            send_sem=self.send_sem.at[n],
            recv_sem=self.recv_sem.at[n],
            device_id=device,
            device_id_type=MESH,
        )
        copy.start()
        self.made.append(copy)
        return copy

    def finish_sends(self):
        for copy in self.made:
            copy.wait_send()


def nt(a, b):
    return lax.dot_general(a, b, (((1,), (1,)), ((), ())), preferred_element_type=F32)


def nn(a, b):
    return lax.dot_general(a, b, (((1,), (0,)), ((), ())), preferred_element_type=F32)


def tn(a, b):
    return lax.dot_general(a, b, (((0,), (0,)), ((), ())), preferred_element_type=F32)


def in_turn(*works):
    works = list(works)
    while works:
        for work in list(works):
            if next(work, works) is works:
                works.remove(work)


def index_of_holder(block):
    stretch = block // 2
    late = stretch > LAST // 2
    return jnp.where(late, LAST - stretch, stretch), block % 2 + jnp.where(late, 2, 0)


def write_list(links_ref, named_ref, list_ref):
    shape = (8, BLK)
    block = lax.broadcasted_iota(jnp.int32, shape, 1)
    row = lax.broadcasted_iota(jnp.int32, shape, 0)
    named_ref[...] = block - 1
    named_ref[0:LINKS, :] = links_ref[...]
    named = named_ref[...]
    q_dev, q_local = index_of_holder(block)
    k_dev, k_local = index_of_holder(jnp.maximum(named, 0))
    within = jnp.logical_or(row > LINKS, jnp.logical_and(row == LINKS, block % 2 == 1))
    used = jnp.logical_and(named >= 0, jnp.logical_not(within))
    keys = lax.broadcasted_iota(jnp.int32, (BLK, BLK), 0)
    lanes = lax.broadcasted_iota(jnp.int32, (BLK, BLK), 1)
    before = jnp.where(keys < lanes, 1.0, 0.0).astype(BF16)
    out = [jnp.zeros(shape, F32) for _ in range(LIST // BLK)]
    base = jnp.zeros((1, 1), F32)
    for s in range(2):
        half = Half(s)
        q_x, q_y, k_x, k_y = q_dev // 8, (q_dev // 2) % 4, k_dev // 8, (k_dev // 2) % 4
        q_a, q_b = (q_x, q_y) if s == 0 else (q_y, q_x)
        k_a, k_b = (k_x, k_y) if s == 0 else (k_y, k_x)
        meets = jnp.logical_and(q_a * 2 + q_dev % 2 == half.a * 2 + half.c, k_b == half.b)
        here = jnp.where(jnp.logical_and(used, meets), 1.0, 0.0)
        q_slot = (s * SIDE + q_b) * LOCAL + q_local
        k_slot = (s * NG + k_a * 2 + k_dev % 2) * LOCAL + k_local
        at = base + jnp.sum(nn(here.astype(BF16), before), axis=0, keepdims=True)
        for t in range(LINKS + 1):
            flag = here[t : t + 1, :]
            values = jnp.where(row == 0, q_slot[t : t + 1, :], k_slot[t : t + 1, :]).astype(F32)
            for n in range(LIST // BLK):
                spot = keys.astype(F32) + float(n * BLK)
                hot = jnp.where(spot == at, flag, 0.0).astype(BF16)
                out[n] = out[n] + nt(values.astype(BF16), hot)
            at = at + flag
        base = base + jnp.sum(jnp.sum(here, axis=1, keepdims=True), axis=0, keepdims=True)
    for n in range(LIST // BLK):
        spot = block.astype(F32) + float(n * BLK)
        spare = jnp.where(row == 0, float(NQ), float(NK))
        full = jnp.where(row == 2, base, jnp.where(spot < base, out[n], spare)).astype(jnp.int32)
        q, k = jnp.bitwise_and(full[0:1, :], NQ - 1), jnp.bitwise_and(full[1:2, :], NK - 1)
        for at_row, values in ((3, first_row(k)), (4, q * TURNED), (5, first_row(q))):
            full = jnp.where(row == at_row, values, full)
        list_ref[:, n * BLK : (n + 1) * BLK] = full


def first_row(slot):
    return slot // LOCAL * (2 * ROWS) + slot % LOCAL * BLK


def rows(first, count=BLK):
    return pl.ds(pl.multiple_of(first, BLK), count)


class Entry:
    def __init__(self, q_to, k_to, keys, values, queries_t, out_grads_t, causal=False):
        self.q_to, self.k_to, self.keys = q_to, k_to, keys
        self.score = [nn(k, q) * (SCALE * LOG2E) for k, q in zip(keys, queries_t)]
        self.dprob = [nn(v, o) for v, o in zip(values, out_grads_t)]
        if causal:
            down = lax.broadcasted_iota(jnp.int32, (BLK, BLK), 0)
            live = down <= lax.broadcasted_iota(jnp.int32, (BLK, BLK), 1)
            self.score = [jnp.where(live, score, NEG) for score in self.score]


def met(q_to, k_to, k_row, turned_row, qt_ref, kg_ref, causal=False):
    keys, values = [[kg_ref[rows(k_row + n * ROWS), tile] for tile in TILES] for n in range(2)]
    turned = [[qt_ref[rows(turned_row + n * WIDE + tile.start), :] for tile in TILES] for n in range(2)]
    return Entry(q_to, k_to, keys, values, *turned, causal)


ITSELF = tuple((n, n) for n in range(LOCAL))
BEFORE = ((1, 0), (3, 2))


def listed_entries(list_ref, qt_ref, kg_ref, finish):
    def batch(first, count):
        entries = []
        for at in [first + u for u in range(count)]:
            q_to, k_to, _, k_row, turned_row, q_row = [list_ref[m, at] for m in range(6)]
            e = met(q_to, k_to, k_row, turned_row, qt_ref, kg_ref)
            e.q_row = q_row
            entries.append(e)
        finish(entries)
        return 0

    full = lax.div(list_ref[2, 0], MANY)
    rest = list_ref[2, 0] - full * MANY
    some = lax.div(rest + (SOME - FEW - 1), SOME)
    left_over = rest - some * SOME
    lax.fori_loop(0, full, lambda n, _: batch(n * MANY, MANY), 0)
    lax.fori_loop(0, some, lambda n, _: batch(full * MANY + n * SOME, SOME), 0)

    @pl.when(left_over > 0)
    def _():
        batch(full * MANY + some * SOME, FEW)


def stats_place(q_slot):
    return lax.div(q_slot, LOCAL), pl.ds(lax.rem(q_slot, LOCAL) * HEADS, HEADS)


def add_stats(part_ref, entries):
    found = []
    for e in entries:
        tops = [jnp.max(score, axis=0, keepdims=True) for score in e.score]
        probs = [jnp.exp2(score - top) for score, top in zip(e.score, tops)]
        sums = [jnp.sum(prob, axis=0, keepdims=True) for prob in probs]
        dots = [jnp.sum(p * d, axis=0, keepdims=True) for p, d in zip(probs, e.dprob)]
        found.append([jnp.concatenate(lines, axis=0) for lines in (tops, sums, dots)])
    for e, (top, total, dot) in zip(entries, found):
        holder, lines = stats_place(e.q_to)
        old_top = part_ref[holder, 0, lines, :]
        new_top = jnp.maximum(old_top, top)
        was, now = jnp.exp2(old_top - new_top), jnp.exp2(top - new_top)
        part_ref[holder, 0, lines, :] = new_top
        part_ref[holder, 1, lines, :] = part_ref[holder, 1, lines, :] * was + total * now
        part_ref[holder, 2, lines, :] = part_ref[holder, 2, lines, :] * was + dot * now


def add_grads(dq_ref, dk_ref, dv_ref, full_ref, stats_slot, queries, out_grads, entries):
    found = []
    for e in entries:
        holder, lines = stats_place(stats_slot(e))
        lse, delta = full_ref[holder, 0, lines, :], full_ref[holder, 1, lines, :]
        dq, dk, dv = [], [], []
        for i in range(HEADS):
            prob = jnp.exp2(e.score[i] - lse[i : i + 1])
            dscore = (prob * (e.dprob[i] - delta[i : i + 1])).astype(BF16)
            dk.append(nn(dscore, queries(e, i)))
            dv.append(nn(prob.astype(BF16), out_grads(e, i)))
            dq.append(tn(dscore, e.keys[i]))
        found.append([jnp.concatenate(terms, axis=1) for terms in (dq, dk, dv)])
    for e, (dq, dk, dv) in zip(entries, found):
        dq_ref[e.q_to] += dq.astype(dq_ref.dtype)
        dk_ref[e.k_to] += dk.astype(dk_ref.dtype)
        dv_ref[e.k_to] += dv.astype(dv_ref.dtype)


def clear(ref, count):
    def body(n, _):
        ref[n] = jnp.zeros(ref.shape[1:], ref.dtype)
        return 0

    lax.fori_loop(0, count, body, 0)


N_GATHER = 52


def gather_kernel(
    q_ref, o_ref, k_ref, v_ref, links_ref,
    qg_ref, kg_ref, qt_ref, list_ref, part_ref, dq_ref, dk_ref, dv_ref,
    table_ref, named_ref, send_sem, recv_sem, own_sem,
):
    copies = Copies(send_sem, recv_sem)
    go = copies.start
    own = []
    table = pltpu.make_async_copy(links_ref, table_ref, own_sem.at[8])
    table.start()

    def columns(ref, s):
        return ref.at[:, s * WIDE : (s + 1) * WIDE]

    def part(ref, at, n):
        return ref.at[rows((at * 2 + n) * ROWS, ROWS)]

    def keep(src, dst):
        copy = pltpu.make_async_copy(src, dst, own_sem.at[len(own)])
        copy.start()
        own.append(copy)

    def turn(g, a, first=0, last=LOCAL):
        def body(lb, _):
            for tile in TILES:
                turned = (g * LOCAL + lb) * TURNED + a * WIDE + tile.start
                qt_ref[rows(turned), :] = qg_ref[rows((g * 2 + a) * ROWS + lb * BLK), tile].T
            return 0

        lax.fori_loop(first, last, body, 0)

    def work(s):
        at = Half(s)
        ka, qa = at.k_at, at.q_at
        q, o, k, v = [columns(ref, s) for ref in (q_ref, o_ref, k_ref, v_ref)]
        keep(q, part(qg_ref, qa, 0))
        keep(o, part(qg_ref, qa, 1))
        keep(k, part(kg_ref, ka, 0))
        keep(v, part(kg_ref, ka, 1))
        if s == 0:
            barrier_with([at.right, at.left, at.upper, at.lower, at.twin])
        yield
        kr0 = go(k, part(kg_ref, ka, 0), at.right)
        kl1 = go(v, part(kg_ref, ka, 1), at.left)
        yield
        qu0 = go(q, part(qg_ref, qa, 0), at.upper)
        ql1 = go(o, part(qg_ref, qa, 1), at.lower)
        yield
        kr1 = go(v, part(kg_ref, ka, 1), at.right)
        kl0 = go(k, part(kg_ref, ka, 0), at.left)
        twins = [go(k, part(kg_ref, ka, 0), at.twin), go(v, part(kg_ref, ka, 1), at.twin)]
        yield
        qu1 = go(o, part(qg_ref, qa, 1), at.upper)
        ql0 = go(q, part(qg_ref, qa, 0), at.lower)
        yield
        if s == 0:
            table.wait()
            write_list(table_ref, named_ref, list_ref)
            part_ref[:, 0] = jnp.full((HOLDERS + 1, LINES, BLK), NEG, F32)
            part_ref[:, 1:3] = jnp.zeros((HOLDERS + 1, 2, LINES, BLK), F32)
        for copy in own[4 * s : 4 * s + 4]:
            copy.wait()
        turn(qa, 0)
        turn(qa, 1)
        yield
        for pairs in (ITSELF, BEFORE):
            entries = []
            for m, n in pairs:
                q_slot, k_slot = qa * LOCAL + m, ka * LOCAL + n
                k_row, turned_row = ka * (2 * ROWS) + n * BLK, q_slot * TURNED
                entries.append(met(q_slot, k_slot, k_row, turned_row, qt_ref, kg_ref, pairs is ITSELF))
            add_stats(part_ref, entries)
        if s == 0:
            clear(dk_ref, NK + 1)
        else:
            clear(dq_ref, NQ + 1)
            clear(dv_ref, NK + 1)
        yield

        def on(ref, holder, n, device, piece=None):
            slot = part(ref, holder, n)
            if piece is not None:
                slot = ref.at[rows((holder * 2 + n) * ROWS + piece * BLK)]
            return go(slot, slot, device)

        def keys(a):
            return s * NG + a * 2 + at.c

        def queries(b):
            return s * SIDE + b

        kr0.wait_recv()
        kr2 = on(kg_ref, keys(at.a_down), 0, at.right)
        twins.append(on(kg_ref, keys(at.a_down), 0, at.twin))
        kl1.wait_recv()
        kl2 = on(kg_ref, keys(at.a_up), 1, at.left)
        twins.append(on(kg_ref, keys(at.a_up), 1, at.twin))
        yield
        qu0.wait_recv()
        qu2 = [on(qg_ref, queries(at.b_down), 0, at.upper, n) for n in range(LOCAL)]
        ql1.wait_recv()
        ql2 = [on(qg_ref, queries(at.b_up), 1, at.lower, n) for n in range(LOCAL)]
        yield
        turn(queries(at.b_down), 0)
        turn(queries(at.b_up), 1)
        yield
        kr1.wait_recv()
        twins.append(on(kg_ref, keys(at.a_down), 1, at.twin))
        kl0.wait_recv()
        twins.append(on(kg_ref, keys(at.a_up), 0, at.twin))
        yield
        qu1.wait_recv()
        turn(queries(at.b_down), 1)
        ql0.wait_recv()
        turn(queries(at.b_up), 0)
        yield
        kr2.wait_recv()
        twins.append(on(kg_ref, keys(at.a_far), 0, at.twin))
        kl2.wait_recv()
        twins.append(on(kg_ref, keys(at.a_far), 1, at.twin))
        yield
        for n in range(LOCAL):
            if n > 0:
                yield
            qu2[n].wait_recv()
            turn(queries(at.b_far), 0, n, n + 1)
            ql2[n].wait_recv()
            turn(queries(at.b_far), 1, n, n + 1)
        for copy in twins:
            copy.wait_recv()

    in_turn(work(0), work(1))
    copies.finish_sends()


def gathered(query, out_grad, key, value, links):
    return pl.pallas_call(
        gather_kernel,
        out_shape=(
            VMEM((2 * SIDE * 2 * ROWS, WIDE), BF16),
            VMEM((2 * NG * 2 * ROWS, WIDE), BF16),
            VMEM((NQ * TURNED, BLK), BF16),
            VMEM((8, LIST), jnp.int32),
            VMEM((HOLDERS + 1, 3, LINES, BLK), F32),
            VMEM((NQ + 1, BLK, WIDE), BF16),
            VMEM((NK + 1, BLK, WIDE), BF16),
            VMEM((NK + 1, BLK, WIDE), BF16),
        ),
        in_specs=[whole(pltpu.HBM)] * 5,
        out_specs=(whole(VMEM),) * 8,
        scratch_shapes=[
            VMEM((LINKS, BLK), jnp.int32),
            VMEM((8, BLK), jnp.int32),
            pltpu.SemaphoreType.DMA((N_GATHER,)),
            pltpu.SemaphoreType.DMA((N_GATHER,)),
            pltpu.SemaphoreType.DMA((9,)),
        ],
        compiler_params=pltpu.CompilerParams(
            collective_id=0, has_side_effects=True, vmem_limit_bytes=8 * MIB
        ),
        name="gather",
    )(query, out_grad, key, value, pltpu.with_memory_space_constraint(links, pltpu.HBM))


def stats_kernel(list_ref, qt_ref, kg_ref, first_ref, part_ref):
    del first_ref
    listed_entries(list_ref, qt_ref, kg_ref, functools.partial(add_stats, part_ref))


def partial_stats(entries, qt, kg, part):
    return pl.pallas_call(
        stats_kernel,
        out_shape=VMEM((HOLDERS + 1, 3, LINES, BLK), F32),
        in_specs=[whole(pltpu.SMEM)] + [whole(VMEM)] * 3,
        out_specs=whole(VMEM),
        input_output_aliases={3: 0},
        compiler_params=pltpu.CompilerParams(vmem_limit_bytes=8 * MIB),
        name="partial_stats",
    )(entries, *pinned(qt, kg, part))


def merged(parts):
    tops = [part[0] for part in parts]
    top = functools.reduce(jnp.maximum, tops)
    weights = [jnp.exp2(t - top) for t in tops]
    total = sum(part[1] * w for part, w in zip(parts, weights))
    dot = sum(part[2] * w for part, w in zip(parts, weights))
    return top, total, dot


def join_kernel(part_ref, full_ref, got_ref, send_sem, recv_sem):
    halves = [Half(0), Half(1)]

    def around(at):
        return [(b, at.at(at.a, b, at.c)) for b in (at.b_far, at.b_up, at.b_down)]

    barrier_with([device for at in halves for _, device in around(at)])
    copies = Copies(send_sem, recv_sem)
    first = [[], []]
    for n in range(SIDE - 1):
        for at in halves:
            b, device = around(at)[n]
            first[at.s].append(copies.start(part_ref.at[at.s * SIDE + b], got_ref.at[at.s, n], device))
    later = []
    for at in halves:
        for copy in first[at.s]:
            copy.wait_recv()
        top, total, dot = merged([part_ref[at.q_at]] + [got_ref[at.s, n] for n in range(SIDE - 1)])
        full_ref[at.q_at, 0] = top + jnp.log(total) * LOG2E
        full_ref[at.q_at, 1] = dot / total
        for _, device in around(at):
            later.append(copies.start(full_ref.at[at.q_at], full_ref.at[at.q_at], device))
    for copy in later:
        copy.wait_recv()
    copies.finish_sends()


def joined_stats(part):
    return pl.pallas_call(
        join_kernel,
        out_shape=VMEM((HOLDERS, 2, LINES, BLK), F32),
        in_specs=[whole(VMEM)],
        out_specs=whole(VMEM),
        scratch_shapes=[
            VMEM((2, SIDE - 1, 3, LINES, BLK), F32),
            pltpu.SemaphoreType.DMA((12,)),
            pltpu.SemaphoreType.DMA((12,)),
        ],
        compiler_params=pltpu.CompilerParams(
            collective_id=1, has_side_effects=True, vmem_limit_bytes=8 * MIB
        ),
        name="join_stats",
    )(*pinned(part))


def grads_kernel(
    list_ref, qg_ref, qt_ref, kg_ref, full_ref, zero_q, zero_k, zero_v, dq_ref, dk_ref, dv_ref
):
    del zero_q, zero_k, zero_v

    def tiles(n):
        return lambda e, i: qg_ref[rows(e.q_row + n * ROWS), TILES[i]]

    finish = functools.partial(
        add_grads, dq_ref, dk_ref, dv_ref, full_ref, lambda e: jnp.bitwise_and(e.q_to, NQ - 1), tiles(0), tiles(1)
    )
    listed_entries(list_ref, qt_ref, kg_ref, finish)


def partial_grads(entries, qg, qt, kg, full, dq, dk, dv):
    return pl.pallas_call(
        grads_kernel,
        out_shape=(
            VMEM((NQ + 1, BLK, WIDE), BF16),
            VMEM((NK + 1, BLK, WIDE), BF16),
            VMEM((NK + 1, BLK, WIDE), BF16),
        ),
        in_specs=[whole(pltpu.SMEM)] + [whole(VMEM)] * 7,
        out_specs=(whole(VMEM),) * 3,
        input_output_aliases={5: 0, 6: 1, 7: 2},
        compiler_params=pltpu.CompilerParams(vmem_limit_bytes=8 * MIB),
        name="partial_grads",
    )(entries, *pinned(qg, qt, kg, full, dq, dk, dv))


N_SUM = 40


def add(dst, first, last, *terms):
    def body(n, _):
        total = terms[0][n].astype(F32)
        for term in terms[1:]:
            total = total + term[n].astype(F32)
        dst[n] = total.astype(BF16)
        return 0

    lax.fori_loop(first, last, body, 0)


def sum_kernel(
    dq_ref, dk_ref, dv_ref, full_ref, q_ref, o_ref, k_ref, v_ref,
    q_in, k_in, v_in, k_own, own_q, own_k, own_v,
    own_ref, twin_buf, k_all, q_far, k_far, send_sem, recv_sem, own_sem,
):
    copies = Copies(send_sem, recv_sem)
    go = copies.start
    low, high = pl.ds(0, 2), pl.ds(2, 2)
    kept = [
        pltpu.make_async_copy(ref, own_ref.at[n], own_sem.at[n])
        for n, ref in enumerate((q_ref, o_ref, k_ref, v_ref))
    ]
    for copy in kept:
        copy.start()

    def own_grads(at, pairs):
        def block(n, lb):
            return [
                own_ref[n, lb * BLK : (lb + 1) * BLK, (at.s * HEADS + i) * HEAD_DIM : (at.s * HEADS + i + 1) * HEAD_DIM]
                for i in range(HEADS)
            ]

        def turned(n, lb):
            return [tile.T for tile in block(n, lb)]

        base = at.s * LOCAL
        entries = []
        for m, n in pairs:
            e = Entry(base + m, base + n, block(2, n), block(3, n), turned(0, m), turned(1, m), pairs is ITSELF)
            e.local = m
            entries.append(e)

        def stats_slot(e):
            return at.q_at * LOCAL + e.local

        add_grads(
            own_q, own_k, own_v, full_ref, stats_slot,
            lambda e, i: block(0, e.local)[i], lambda e, i: block(1, e.local)[i], entries,
        )


    def work(s):
        at = Half(s)
        if s == 0:
            barrier_with([at.right, at.left, at.upper, at.lower, at.twin])
        yield

        def mine(ref):
            return ref.at[pl.ds(s * LOCAL, LOCAL)]

        def keys(ref, a, c):
            return ref.at[pl.ds((s * NG + a * 2 + c) * LOCAL, LOCAL)]

        def queries(b):
            return dq_ref.at[pl.ds((s * SIDE + b) * LOCAL, LOCAL)]

        order = (at.a_far, at.a_up, at.a_down, at.a)
        pairs = [
            [go(keys(ref, a, 1 - at.c), twin_buf.at[s, n, t], at.twin) for t, ref in enumerate((dk_ref, dv_ref))]
            for n, a in enumerate(order)
        ]
        qu0 = go(queries(at.b_far).at[low], q_far.at[s, 0, low], at.upper)
        ql0 = go(queries(at.b_far).at[high], q_far.at[s, 0, high], at.lower)
        yield
        qu1 = go(queries(at.b_up).at[high], q_in.at[s, 0, high], at.upper)
        ql1 = go(queries(at.b_down).at[low], q_in.at[s, 1, low], at.lower)
        yield

        def take(n, t):
            pairs[n][t].wait_recv()
            ref = (dk_ref, dv_ref)[t]
            add(k_all.at[s, n, t], 0, LOCAL, keys(ref, order[n], at.c), twin_buf.at[s, n, t])
            return k_all.at[s, n, t]

        kr0 = go(take(0, 0), k_far.at[s, 0], at.right)
        kl0 = go(take(0, 1), k_far.at[s, 1], at.left)
        yield
        kr1 = go(take(1, 1), v_in.at[s, 0], at.right)
        kl1 = go(take(2, 0), k_in.at[s, 1], at.left)
        yield
        qu0.wait_recv()
        add(q_far.at[s, 1], 0, 2, queries(at.b_up), q_far.at[s, 0])
        qu2 = go(q_far.at[s, 1, low], q_in.at[s, 0, low], at.upper)
        ql0.wait_recv()
        add(q_far.at[s, 1], 2, LOCAL, queries(at.b_down), q_far.at[s, 0])
        ql2 = go(q_far.at[s, 1, high], q_in.at[s, 1, high], at.lower)
        yield
        for n, t in ((1, 0), (2, 1)):
            take(n, t)
        for t, ref in enumerate((dk_ref, dv_ref)):
            pairs[3][t].wait_recv()
            add(k_own.at[s, t], 0, LOCAL, keys(ref, at.a, at.c), twin_buf.at[s, 3, t])
        for ref in (own_q, own_k, own_v):
            clear(mine(ref), LOCAL)
        if s == 0:
            for copy in kept:
                copy.wait()
        own_grads(at, ITSELF)
        own_grads(at, BEFORE)
        yield
        kr0.wait_recv()
        add(k_far.at[s, 2], 0, LOCAL, k_all.at[s, 1, 0], k_far.at[s, 0])
        kr2 = go(k_far.at[s, 2], k_in.at[s, 0], at.right)
        kl0.wait_recv()
        add(k_far.at[s, 3], 0, LOCAL, k_all.at[s, 2, 1], k_far.at[s, 1])
        kl2 = go(k_far.at[s, 3], v_in.at[s, 1], at.left)
        yield
        for copy in (qu1, ql1, qu2, ql2, kr1, kl1, kr2, kl2):
            copy.wait_recv()

    in_turn(work(0), work(1))
    copies.finish_sends()


def summed(dq, dk, dv, full, *args):
    block = (LOCAL, BLK, WIDE)
    own = VMEM((2 * LOCAL, BLK, WIDE), F32)
    came = VMEM((2, 2, *block), BF16)
    return pl.pallas_call(
        sum_kernel,
        out_shape=(came, came, came, came, own, own, own),
        in_specs=[whole(VMEM)] * 4 + [whole(pltpu.HBM)] * 4,
        out_specs=(whole(VMEM),) * 7,
        scratch_shapes=[
            VMEM((4, ROWS, COLS), BF16),
            VMEM((2, SIDE, 2, *block), BF16),
            VMEM((2, SIDE - 1, 2, *block), BF16),
            VMEM((2, 2, *block), BF16),
            VMEM((2, 4, *block), BF16),
            pltpu.SemaphoreType.DMA((N_SUM,)),
            pltpu.SemaphoreType.DMA((N_SUM,)),
            pltpu.SemaphoreType.DMA((4,)),
        ],
        compiler_params=pltpu.CompilerParams(
            collective_id=2, has_side_effects=True, vmem_limit_bytes=18 * MIB
        ),
        name="sum_grads",
    )(*pinned(dq, dk, dv, full), *args)


def leave(dst, s, scale, *terms):
    for n in range(LOCAL):
        total = terms[0][n].astype(F32)
        for term in terms[1:]:
            total = total + term[n].astype(F32)
        dst[n * BLK : (n + 1) * BLK, s * WIDE : (s + 1) * WIDE] = (total * scale).astype(BF16)


def leave_kernel(
    dq_ref, q_in, k_in, v_in, k_own, own_q, own_k, own_v, gq_out, gk_out, gv_out, gq_ref, gk_ref, gv_ref, sem
):
    halves = [Half(0), Half(1)]

    def mine(ref, s):
        return ref.at[pl.ds(s * LOCAL, LOCAL)]

    copies = []

    def hand_out(src, dst):
        copies.append(pltpu.make_async_copy(src, dst, sem.at[len(copies)]))
        copies[-1].start()

    for at in halves:
        queries = dq_ref.at[pl.ds(at.q_at * LOCAL, LOCAL)]
        leave(gq_ref, at.s, SCALE, mine(own_q, at.s), queries, q_in.at[at.s, 0], q_in.at[at.s, 1])
    hand_out(gq_ref, gq_out)
    for s in range(2):
        leave(gv_ref, s, 1.0, mine(own_v, s), k_own.at[s, 1], v_in.at[s, 0], v_in.at[s, 1])
    hand_out(gv_ref, gv_out)
    for s in range(2):
        leave(gk_ref, s, SCALE, mine(own_k, s), k_own.at[s, 0], k_in.at[s, 0], k_in.at[s, 1])
    hand_out(gk_ref, gk_out)
    for copy in copies:
        copy.wait()


def left(*sums):
    return pl.pallas_call(
        leave_kernel,
        out_shape=(pltpu.HBM((ROWS, COLS), BF16),) * 3,
        in_specs=[whole(VMEM)] * 8,
        out_specs=(whole(pltpu.HBM),) * 3,
        scratch_shapes=[VMEM((ROWS, COLS), BF16)] * 3 + [pltpu.SemaphoreType.DMA((3,))],
        compiler_params=pltpu.CompilerParams(vmem_limit_bytes=4 * MIB),
        name="leave",
    )(*pinned(*sums))


def per_device(query, key, value, out_grad, links):
    args = [pltpu.with_memory_space_constraint(v, pltpu.HBM) for v in (query, out_grad, key, value)]
    qg, kg, qt, entries, part, dq, dk, dv = gathered(*args, links.T)
    full = joined_stats(partial_stats(entries, qt, kg, part))
    dq, dk, dv = partial_grads(entries, qg, qt, kg, full, dq, dk, dv)
    return left(dq, *summed(dq, dk, dv, full, *args))


def solution(mesh):
    spec = P("ctx", "head")
    return jax.shard_map(
        per_device,
        mesh=mesh,
        in_specs=(spec, spec, spec, spec, P()),
        out_specs=(spec, spec, spec),
        check_vma=False,
    )
```

```python
import functools

import jax
import jax.numpy as jnp
from jax import lax
from jax.experimental import pallas as pl
from jax.experimental.pallas import tpu as pltpu
from jax.sharding import PartitionSpec as P

HEAD_DIM = 128
BLK = 128
LINKS = 6
HEADS = 2
SIDE = 4
NG = 8
LOCAL = 4
ROWS = 512
COLS = 512
WIDE = HEADS * HEAD_DIM
NQ = 2 * SIDE * LOCAL
NK = 2 * NG * LOCAL
TURNED = 2 * WIDE
HOLDERS = 2 * SIDE
LINES = LOCAL * HEADS
LAST = 63
TILES = (slice(0, HEAD_DIM), slice(HEAD_DIM, WIDE))
MANY, SOME, FEW = 16, 8, 4
LIST = 256
NEG = -1e30
SCALE = HEAD_DIM**-0.5
LOG2E = 1.4426950408889634
MESH = pl.DeviceIdType.MESH
BF16 = jnp.bfloat16
F32 = jnp.float32
VMEM = pltpu.VMEM
MIB = 1 << 20


def whole(space):
    return pl.BlockSpec(memory_space=space)


def pinned(*arrays):
    return [pltpu.with_memory_space_constraint(array, VMEM) for array in arrays]


def place():
    me = lax.axis_index("ctx")
    return me // 8, (me // 2) % 4, me % 2


class Half:
    def __init__(self, s):
        x, y, c = place()
        self.s, self.c = s, c
        self.a, self.b = (x, y) if s == 0 else (y, x)
        self.q_at, self.k_at = s * SIDE + self.b, s * NG + self.a * 2 + c
        self.a_up, self.a_down, self.a_far = [(self.a + n) % SIDE for n in (1, 3, 2)]
        self.b_up, self.b_down, self.b_far = [(self.b + n) % SIDE for n in (1, 3, 2)]
        self.right, self.left = self.at(self.a_up, self.b, c), self.at(self.a_down, self.b, c)
        self.upper, self.lower = self.at(self.a, self.b_up, c), self.at(self.a, self.b_down, c)
        self.twin = self.at(self.a, self.b, 1 - c)

    def at(self, a, b, c):
        x, y = (a, b) if self.s == 0 else (b, a)
        return ((x * SIDE + y) * 2 + c, lax.axis_index("head"))


def barrier_with(partners):
    sem = pltpu.get_barrier_semaphore()
    for partner in partners:
        pl.semaphore_signal(sem, inc=1, device_id=partner, device_id_type=MESH)
    pl.semaphore_wait(sem, len(partners))


class Copies:
    def __init__(self, send_sem, recv_sem):
        self.send_sem, self.recv_sem, self.made = send_sem, recv_sem, []

    def start(self, src, dst, device):
        n = len(self.made)
        copy = pltpu.make_async_remote_copy(
            src_ref=src,
            dst_ref=dst,
            send_sem=self.send_sem.at[n],
            recv_sem=self.recv_sem.at[n],
            device_id=device,
            device_id_type=MESH,
        )
        copy.start()
        self.made.append(copy)
        return copy

    def finish_sends(self):
        for copy in self.made:
            copy.wait_send()


def nt(a, b):
    return lax.dot_general(a, b, (((1,), (1,)), ((), ())), preferred_element_type=F32)


def nn(a, b):
    return lax.dot_general(a, b, (((1,), (0,)), ((), ())), preferred_element_type=F32)


def tn(a, b):
    return lax.dot_general(a, b, (((0,), (0,)), ((), ())), preferred_element_type=F32)


def in_turn(*works):
    works = list(works)
    while works:
        for work in list(works):
            if next(work, works) is works:
                works.remove(work)


def index_of_holder(block):
    stretch = block // 2
    late = stretch > LAST // 2
    return jnp.where(late, LAST - stretch, stretch), block % 2 + jnp.where(late, 2, 0)


def write_list(links_ref, named_ref, list_ref):
    shape = (8, BLK)
    block = lax.broadcasted_iota(jnp.int32, shape, 1)
    row = lax.broadcasted_iota(jnp.int32, shape, 0)
    named_ref[...] = block - 1
    named_ref[0:LINKS, :] = links_ref[...]
    named = named_ref[...]
    q_dev, q_local = index_of_holder(block)
    k_dev, k_local = index_of_holder(jnp.maximum(named, 0))
    within = jnp.logical_or(row > LINKS, jnp.logical_and(row == LINKS, block % 2 == 1))
    used = jnp.logical_and(named >= 0, jnp.logical_not(within))
    keys = lax.broadcasted_iota(jnp.int32, (BLK, BLK), 0)
    lanes = lax.broadcasted_iota(jnp.int32, (BLK, BLK), 1)
    before = jnp.where(keys < lanes, 1.0, 0.0).astype(BF16)
    out = [jnp.zeros(shape, F32) for _ in range(LIST // BLK)]
    base = jnp.zeros((1, 1), F32)
    for s in range(2):
        half = Half(s)
        q_x, q_y, k_x, k_y = q_dev // 8, (q_dev // 2) % 4, k_dev // 8, (k_dev // 2) % 4
        q_a, q_b = (q_x, q_y) if s == 0 else (q_y, q_x)
        k_a, k_b = (k_x, k_y) if s == 0 else (k_y, k_x)
        meets = jnp.logical_and(q_a * 2 + q_dev % 2 == half.a * 2 + half.c, k_b == half.b)
        here = jnp.where(jnp.logical_and(used, meets), 1.0, 0.0)
        q_slot = (s * SIDE + q_b) * LOCAL + q_local
        k_slot = (s * NG + k_a * 2 + k_dev % 2) * LOCAL + k_local
        at = base + jnp.sum(nn(here.astype(BF16), before), axis=0, keepdims=True)
        for t in range(LINKS + 1):
            flag = here[t : t + 1, :]
            values = jnp.where(row == 0, q_slot[t : t + 1, :], k_slot[t : t + 1, :]).astype(F32)
            for n in range(LIST // BLK):
                spot = keys.astype(F32) + float(n * BLK)
                hot = jnp.where(spot == at, flag, 0.0).astype(BF16)
                out[n] = out[n] + nt(values.astype(BF16), hot)
            at = at + flag
        base = base + jnp.sum(jnp.sum(here, axis=1, keepdims=True), axis=0, keepdims=True)
    for n in range(LIST // BLK):
        spot = block.astype(F32) + float(n * BLK)
        spare = jnp.where(row == 0, float(NQ), float(NK))
        full = jnp.where(row == 2, base, jnp.where(spot < base, out[n], spare)).astype(jnp.int32)
        q, k = jnp.bitwise_and(full[0:1, :], NQ - 1), jnp.bitwise_and(full[1:2, :], NK - 1)
        for at_row, values in ((3, first_row(k)), (4, q * TURNED), (5, first_row(q))):
            full = jnp.where(row == at_row, values, full)
        list_ref[:, n * BLK : (n + 1) * BLK] = full


def first_row(slot):
    return slot // LOCAL * (2 * ROWS) + slot % LOCAL * BLK


def rows(first, count=BLK):
    return pl.ds(pl.multiple_of(first, BLK), count)


class Entry:
    def __init__(self, q_to, k_to, keys, values, queries_t, out_grads_t, causal=False):
        self.q_to, self.k_to, self.keys = q_to, k_to, keys
        self.score = [nn(k, q) * (SCALE * LOG2E) for k, q in zip(keys, queries_t)]
        self.dprob = [nn(v, o) for v, o in zip(values, out_grads_t)]
        if causal:
            down = lax.broadcasted_iota(jnp.int32, (BLK, BLK), 0)
            live = down <= lax.broadcasted_iota(jnp.int32, (BLK, BLK), 1)
            self.score = [jnp.where(live, score, NEG) for score in self.score]


def met(q_to, k_to, k_row, turned_row, qt_ref, kg_ref, causal=False):
    keys, values = [[kg_ref[rows(k_row + n * ROWS), tile] for tile in TILES] for n in range(2)]
    turned = [[qt_ref[rows(turned_row + n * WIDE + tile.start), :] for tile in TILES] for n in range(2)]
    return Entry(q_to, k_to, keys, values, *turned, causal)


ITSELF = tuple((n, n) for n in range(LOCAL))
BEFORE = ((1, 0), (3, 2))


def listed_entries(list_ref, qt_ref, kg_ref, finish):
    def batch(first, count):
        entries = []
        for at in [first + u for u in range(count)]:
            q_to, k_to, _, k_row, turned_row, q_row = [list_ref[m, at] for m in range(6)]
            e = met(q_to, k_to, k_row, turned_row, qt_ref, kg_ref)
            e.q_row = q_row
            entries.append(e)
        finish(entries)
        return 0

    full = lax.div(list_ref[2, 0], MANY)
    rest = list_ref[2, 0] - full * MANY
    some = lax.div(rest + (SOME - FEW - 1), SOME)
    left_over = rest - some * SOME
    lax.fori_loop(0, full, lambda n, _: batch(n * MANY, MANY), 0)
    lax.fori_loop(0, some, lambda n, _: batch(full * MANY + n * SOME, SOME), 0)

    @pl.when(left_over > 0)
    def _():
        batch(full * MANY + some * SOME, FEW)


def stats_place(q_slot):
    return lax.div(q_slot, LOCAL), pl.ds(lax.rem(q_slot, LOCAL) * HEADS, HEADS)


def add_stats(part_ref, entries):
    found = []
    for e in entries:
        tops = [jnp.max(score, axis=0, keepdims=True) for score in e.score]
        probs = [jnp.exp2(score - top) for score, top in zip(e.score, tops)]
        sums = [jnp.sum(prob, axis=0, keepdims=True) for prob in probs]
        dots = [jnp.sum(p * d, axis=0, keepdims=True) for p, d in zip(probs, e.dprob)]
        found.append([jnp.concatenate(lines, axis=0) for lines in (tops, sums, dots)])
    for e, (top, total, dot) in zip(entries, found):
        holder, lines = stats_place(e.q_to)
        old_top = part_ref[holder, 0, lines, :]
        new_top = jnp.maximum(old_top, top)
        was, now = jnp.exp2(old_top - new_top), jnp.exp2(top - new_top)
        part_ref[holder, 0, lines, :] = new_top
        part_ref[holder, 1, lines, :] = part_ref[holder, 1, lines, :] * was + total * now
        part_ref[holder, 2, lines, :] = part_ref[holder, 2, lines, :] * was + dot * now


def add_grads(dq_ref, dk_ref, dv_ref, full_ref, stats_slot, queries, out_grads, entries):
    found = []
    for e in entries:
        holder, lines = stats_place(stats_slot(e))
        lse, delta = full_ref[holder, 0, lines, :], full_ref[holder, 1, lines, :]
        dq, dk, dv = [], [], []
        for i in range(HEADS):
            prob = jnp.exp2(e.score[i] - lse[i : i + 1])
            dscore = (prob * (e.dprob[i] - delta[i : i + 1])).astype(BF16)
            dk.append(nn(dscore, queries(e, i)))
            dv.append(nn(prob.astype(BF16), out_grads(e, i)))
            dq.append(tn(dscore, e.keys[i]))
        found.append([jnp.concatenate(terms, axis=1) for terms in (dq, dk, dv)])
    for e, (dq, dk, dv) in zip(entries, found):
        dq_ref[e.q_to] += dq.astype(dq_ref.dtype)
        dk_ref[e.k_to] += dk.astype(dk_ref.dtype)
        dv_ref[e.k_to] += dv.astype(dv_ref.dtype)


def clear(ref, count):
    def body(n, _):
        ref[n] = jnp.zeros(ref.shape[1:], ref.dtype)
        return 0

    lax.fori_loop(0, count, body, 0)


N_GATHER = 52


def gather_kernel(
    q_ref, o_ref, k_ref, v_ref, links_ref,
    qg_ref, kg_ref, qt_ref, list_ref, part_ref, dq_ref, dk_ref, dv_ref,
    table_ref, named_ref, send_sem, recv_sem, own_sem,
):
    copies = Copies(send_sem, recv_sem)
    go = copies.start
    own = []
    table = pltpu.make_async_copy(links_ref, table_ref, own_sem.at[8])
    table.start()

    def columns(ref, s):
        return ref.at[:, s * WIDE : (s + 1) * WIDE]

    def part(ref, at, n):
        return ref.at[rows((at * 2 + n) * ROWS, ROWS)]

    def keep(src, dst):
        copy = pltpu.make_async_copy(src, dst, own_sem.at[len(own)])
        copy.start()
        own.append(copy)

    def turn(g, a, first=0, last=LOCAL):
        def body(lb, _):
            for tile in TILES:
                turned = (g * LOCAL + lb) * TURNED + a * WIDE + tile.start
                qt_ref[rows(turned), :] = qg_ref[rows((g * 2 + a) * ROWS + lb * BLK), tile].T
            return 0

        lax.fori_loop(first, last, body, 0)

    def work(s):
        at = Half(s)
        ka, qa = at.k_at, at.q_at
        q, o, k, v = [columns(ref, s) for ref in (q_ref, o_ref, k_ref, v_ref)]
        keep(q, part(qg_ref, qa, 0))
        keep(o, part(qg_ref, qa, 1))
        keep(k, part(kg_ref, ka, 0))
        keep(v, part(kg_ref, ka, 1))
        if s == 0:
            barrier_with([at.right, at.left, at.upper, at.lower, at.twin])
        yield
        qu0 = go(q, part(qg_ref, qa, 0), at.upper)
        ql1 = go(o, part(qg_ref, qa, 1), at.lower)
        yield
        kr0 = go(k, part(kg_ref, ka, 0), at.right)
        kl1 = go(v, part(kg_ref, ka, 1), at.left)
        yield
        kr1 = go(v, part(kg_ref, ka, 1), at.right)
        kl0 = go(k, part(kg_ref, ka, 0), at.left)
        twins = [go(k, part(kg_ref, ka, 0), at.twin), go(v, part(kg_ref, ka, 1), at.twin)]
        yield
        qu1 = go(o, part(qg_ref, qa, 1), at.upper)
        ql0 = go(q, part(qg_ref, qa, 0), at.lower)
        yield
        if s == 0:
            table.wait()
            write_list(table_ref, named_ref, list_ref)
            part_ref[:, 0] = jnp.full((HOLDERS + 1, LINES, BLK), NEG, F32)
            part_ref[:, 1:3] = jnp.zeros((HOLDERS + 1, 2, LINES, BLK), F32)
        for copy in own[4 * s : 4 * s + 4]:
            copy.wait()
        turn(qa, 0)
        turn(qa, 1)
        yield
        for pairs in (ITSELF, BEFORE):
            entries = []
            for m, n in pairs:
                q_slot, k_slot = qa * LOCAL + m, ka * LOCAL + n
                k_row, turned_row = ka * (2 * ROWS) + n * BLK, q_slot * TURNED
                entries.append(met(q_slot, k_slot, k_row, turned_row, qt_ref, kg_ref, pairs is ITSELF))
            add_stats(part_ref, entries)
        if s == 0:
            clear(dk_ref, NK + 1)
        else:
            clear(dq_ref, NQ + 1)
            clear(dv_ref, NK + 1)
        yield

        def on(ref, holder, n, device, piece=None):
            slot = part(ref, holder, n)
            if piece is not None:
                slot = ref.at[rows((holder * 2 + n) * ROWS + piece * BLK)]
            return go(slot, slot, device)

        def keys(a):
            return s * NG + a * 2 + at.c

        def queries(b):
            return s * SIDE + b

        kr0.wait_recv()
        kr2 = on(kg_ref, keys(at.a_down), 0, at.right)
        twins.append(on(kg_ref, keys(at.a_down), 0, at.twin))
        kl1.wait_recv()
        kl2 = on(kg_ref, keys(at.a_up), 1, at.left)
        twins.append(on(kg_ref, keys(at.a_up), 1, at.twin))
        yield
        qu0.wait_recv()
        qu2 = [on(qg_ref, queries(at.b_down), 0, at.upper, n) for n in range(LOCAL)]
        ql1.wait_recv()
        ql2 = [on(qg_ref, queries(at.b_up), 1, at.lower, n) for n in range(LOCAL)]
        yield
        turn(queries(at.b_down), 0)
        turn(queries(at.b_up), 1)
        yield
        kr1.wait_recv()
        twins.append(on(kg_ref, keys(at.a_down), 1, at.twin))
        kl0.wait_recv()
        twins.append(on(kg_ref, keys(at.a_up), 0, at.twin))
        yield
        qu1.wait_recv()
        turn(queries(at.b_down), 1)
        ql0.wait_recv()
        turn(queries(at.b_up), 0)
        yield
        kr2.wait_recv()
        twins.append(on(kg_ref, keys(at.a_far), 0, at.twin))
        kl2.wait_recv()
        twins.append(on(kg_ref, keys(at.a_far), 1, at.twin))
        yield
        for n in range(LOCAL):
            if n > 0:
                yield
            qu2[n].wait_recv()
            turn(queries(at.b_far), 0, n, n + 1)
            ql2[n].wait_recv()
            turn(queries(at.b_far), 1, n, n + 1)
        for copy in twins:
            copy.wait_recv()

    in_turn(work(0), work(1))
    copies.finish_sends()


def gathered(query, out_grad, key, value, links):
    return pl.pallas_call(
        gather_kernel,
        out_shape=(
            VMEM((2 * SIDE * 2 * ROWS, WIDE), BF16),
            VMEM((2 * NG * 2 * ROWS, WIDE), BF16),
            VMEM((NQ * TURNED, BLK), BF16),
            VMEM((8, LIST), jnp.int32),
            VMEM((HOLDERS + 1, 3, LINES, BLK), F32),
            VMEM((NQ + 1, BLK, WIDE), BF16),
            VMEM((NK + 1, BLK, WIDE), BF16),
            VMEM((NK + 1, BLK, WIDE), BF16),
        ),
        in_specs=[whole(pltpu.HBM)] * 5,
        out_specs=(whole(VMEM),) * 8,
        scratch_shapes=[
            VMEM((LINKS, BLK), jnp.int32),
            VMEM((8, BLK), jnp.int32),
            pltpu.SemaphoreType.DMA((N_GATHER,)),
            pltpu.SemaphoreType.DMA((N_GATHER,)),
            pltpu.SemaphoreType.DMA((9,)),
        ],
        compiler_params=pltpu.CompilerParams(
            collective_id=0, has_side_effects=True, vmem_limit_bytes=8 * MIB
        ),
        name="gather",
    )(query, out_grad, key, value, pltpu.with_memory_space_constraint(links, pltpu.HBM))


def stats_kernel(list_ref, qt_ref, kg_ref, first_ref, part_ref):
    del first_ref
    listed_entries(list_ref, qt_ref, kg_ref, functools.partial(add_stats, part_ref))


def partial_stats(entries, qt, kg, part):
    return pl.pallas_call(
        stats_kernel,
        out_shape=VMEM((HOLDERS + 1, 3, LINES, BLK), F32),
        in_specs=[whole(pltpu.SMEM)] + [whole(VMEM)] * 3,
        out_specs=whole(VMEM),
        input_output_aliases={3: 0},
        compiler_params=pltpu.CompilerParams(vmem_limit_bytes=8 * MIB),
        name="partial_stats",
    )(entries, *pinned(qt, kg, part))


def merged(parts):
    tops = [part[0] for part in parts]
    top = functools.reduce(jnp.maximum, tops)
    weights = [jnp.exp2(t - top) for t in tops]
    total = sum(part[1] * w for part, w in zip(parts, weights))
    dot = sum(part[2] * w for part, w in zip(parts, weights))
    return top, total, dot


def join_kernel(part_ref, full_ref, got_ref, send_sem, recv_sem):
    halves = [Half(0), Half(1)]

    def around(at):
        return [(b, at.at(at.a, b, at.c)) for b in (at.b_far, at.b_up, at.b_down)]

    barrier_with([device for at in halves for _, device in around(at)])
    copies = Copies(send_sem, recv_sem)
    first = [[], []]
    for n in range(SIDE - 1):
        for at in halves:
            b, device = around(at)[n]
            first[at.s].append(copies.start(part_ref.at[at.s * SIDE + b], got_ref.at[at.s, n], device))
    later = []
    for at in halves:
        for copy in first[at.s]:
            copy.wait_recv()
        top, total, dot = merged([part_ref[at.q_at]] + [got_ref[at.s, n] for n in range(SIDE - 1)])
        full_ref[at.q_at, 0] = top + jnp.log(total) * LOG2E
        full_ref[at.q_at, 1] = dot / total
        for _, device in around(at):
            later.append(copies.start(full_ref.at[at.q_at], full_ref.at[at.q_at], device))
    for copy in later:
        copy.wait_recv()
    copies.finish_sends()


def joined_stats(part):
    return pl.pallas_call(
        join_kernel,
        out_shape=VMEM((HOLDERS, 2, LINES, BLK), F32),
        in_specs=[whole(VMEM)],
        out_specs=whole(VMEM),
        scratch_shapes=[
            VMEM((2, SIDE - 1, 3, LINES, BLK), F32),
            pltpu.SemaphoreType.DMA((12,)),
            pltpu.SemaphoreType.DMA((12,)),
        ],
        compiler_params=pltpu.CompilerParams(
            collective_id=1, has_side_effects=True, vmem_limit_bytes=8 * MIB
        ),
        name="join_stats",
    )(*pinned(part))


def grads_kernel(
    list_ref, qg_ref, qt_ref, kg_ref, full_ref, zero_q, zero_k, zero_v, dq_ref, dk_ref, dv_ref
):
    del zero_q, zero_k, zero_v

    def tiles(n):
        return lambda e, i: qg_ref[rows(e.q_row + n * ROWS), TILES[i]]

    finish = functools.partial(
        add_grads, dq_ref, dk_ref, dv_ref, full_ref, lambda e: jnp.bitwise_and(e.q_to, NQ - 1), tiles(0), tiles(1)
    )
    listed_entries(list_ref, qt_ref, kg_ref, finish)


def partial_grads(entries, qg, qt, kg, full, dq, dk, dv):
    return pl.pallas_call(
        grads_kernel,
        out_shape=(
            VMEM((NQ + 1, BLK, WIDE), BF16),
            VMEM((NK + 1, BLK, WIDE), BF16),
            VMEM((NK + 1, BLK, WIDE), BF16),
        ),
        in_specs=[whole(pltpu.SMEM)] + [whole(VMEM)] * 7,
        out_specs=(whole(VMEM),) * 3,
        input_output_aliases={5: 0, 6: 1, 7: 2},
        compiler_params=pltpu.CompilerParams(vmem_limit_bytes=8 * MIB),
        name="partial_grads",
    )(entries, *pinned(qg, qt, kg, full, dq, dk, dv))


N_SUM = 40


def add(dst, first, last, *terms):
    def body(n, _):
        total = terms[0][n].astype(F32)
        for term in terms[1:]:
            total = total + term[n].astype(F32)
        dst[n] = total.astype(BF16)
        return 0

    lax.fori_loop(first, last, body, 0)


def sum_kernel(
    dq_ref, dk_ref, dv_ref, full_ref, q_ref, o_ref, k_ref, v_ref,
    q_in, k_in, v_in, k_own, own_q, own_k, own_v,
    own_ref, twin_buf, k_all, q_far, k_far, send_sem, recv_sem, own_sem,
):
    copies = Copies(send_sem, recv_sem)
    go = copies.start
    low, high = pl.ds(0, 2), pl.ds(2, 2)
    kept = [
        pltpu.make_async_copy(ref, own_ref.at[n], own_sem.at[n])
        for n, ref in enumerate((q_ref, o_ref, k_ref, v_ref))
    ]
    for copy in kept:
        copy.start()

    def own_grads(at, pairs):
        def block(n, lb):
            return [
                own_ref[n, lb * BLK : (lb + 1) * BLK, (at.s * HEADS + i) * HEAD_DIM : (at.s * HEADS + i + 1) * HEAD_DIM]
                for i in range(HEADS)
            ]

        def turned(n, lb):
            return [tile.T for tile in block(n, lb)]

        base = at.s * LOCAL
        entries = []
        for m, n in pairs:
            e = Entry(base + m, base + n, block(2, n), block(3, n), turned(0, m), turned(1, m), pairs is ITSELF)
            e.local = m
            entries.append(e)

        def stats_slot(e):
            return at.q_at * LOCAL + e.local

        add_grads(
            own_q, own_k, own_v, full_ref, stats_slot,
            lambda e, i: block(0, e.local)[i], lambda e, i: block(1, e.local)[i], entries,
        )


    def work(s):
        at = Half(s)
        if s == 0:
            barrier_with([at.right, at.left, at.upper, at.lower, at.twin])
        yield

        def mine(ref):
            return ref.at[pl.ds(s * LOCAL, LOCAL)]

        def keys(ref, a, c):
            return ref.at[pl.ds((s * NG + a * 2 + c) * LOCAL, LOCAL)]

        def queries(b):
            return dq_ref.at[pl.ds((s * SIDE + b) * LOCAL, LOCAL)]

        order = (at.a_far, at.a_up, at.a_down, at.a)
        pairs = [
            [go(keys(ref, a, 1 - at.c), twin_buf.at[s, n, t], at.twin) for t, ref in enumerate((dk_ref, dv_ref))]
            for n, a in enumerate(order)
        ]
        qu0 = go(queries(at.b_far).at[low], q_far.at[s, 0, low], at.upper)
        ql0 = go(queries(at.b_far).at[high], q_far.at[s, 0, high], at.lower)
        yield
        qu1 = go(queries(at.b_up).at[high], q_in.at[s, 0, high], at.upper)
        ql1 = go(queries(at.b_down).at[low], q_in.at[s, 1, low], at.lower)
        yield

        def take(n, t):
            pairs[n][t].wait_recv()
            ref = (dk_ref, dv_ref)[t]
            add(k_all.at[s, n, t], 0, LOCAL, keys(ref, order[n], at.c), twin_buf.at[s, n, t])
            return k_all.at[s, n, t]

        kr0 = go(take(0, 0), k_far.at[s, 0], at.right)
        kl0 = go(take(0, 1), k_far.at[s, 1], at.left)
        yield
        kr1 = go(take(1, 1), v_in.at[s, 0], at.right)
        kl1 = go(take(2, 0), k_in.at[s, 1], at.left)
        yield
        qu0.wait_recv()
        add(q_far.at[s, 1], 0, 2, queries(at.b_up), q_far.at[s, 0])
        qu2 = go(q_far.at[s, 1, low], q_in.at[s, 0, low], at.upper)
        ql0.wait_recv()
        add(q_far.at[s, 1], 2, LOCAL, queries(at.b_down), q_far.at[s, 0])
        ql2 = go(q_far.at[s, 1, high], q_in.at[s, 1, high], at.lower)
        yield
        for n, t in ((1, 0), (2, 1)):
            take(n, t)
        for t, ref in enumerate((dk_ref, dv_ref)):
            pairs[3][t].wait_recv()
            add(k_own.at[s, t], 0, LOCAL, keys(ref, at.a, at.c), twin_buf.at[s, 3, t])
        for ref in (own_q, own_k, own_v):
            clear(mine(ref), LOCAL)
        if s == 0:
            for copy in kept:
                copy.wait()
        own_grads(at, ITSELF)
        own_grads(at, BEFORE)
        yield
        kr0.wait_recv()
        add(k_far.at[s, 2], 0, LOCAL, k_all.at[s, 1, 0], k_far.at[s, 0])
        kr2 = go(k_far.at[s, 2], k_in.at[s, 0], at.right)
        kl0.wait_recv()
        add(k_far.at[s, 3], 0, LOCAL, k_all.at[s, 2, 1], k_far.at[s, 1])
        kl2 = go(k_far.at[s, 3], v_in.at[s, 1], at.left)
        yield
        for copy in (qu1, ql1, qu2, ql2, kr1, kl1, kr2, kl2):
            copy.wait_recv()

    in_turn(work(0), work(1))
    copies.finish_sends()


def summed(dq, dk, dv, full, *args):
    block = (LOCAL, BLK, WIDE)
    own = VMEM((2 * LOCAL, BLK, WIDE), F32)
    came = VMEM((2, 2, *block), BF16)
    return pl.pallas_call(
        sum_kernel,
        out_shape=(came, came, came, came, own, own, own),
        in_specs=[whole(VMEM)] * 4 + [whole(pltpu.HBM)] * 4,
        out_specs=(whole(VMEM),) * 7,
        scratch_shapes=[
            VMEM((4, ROWS, COLS), BF16),
            VMEM((2, SIDE, 2, *block), BF16),
            VMEM((2, SIDE - 1, 2, *block), BF16),
            VMEM((2, 2, *block), BF16),
            VMEM((2, 4, *block), BF16),
            pltpu.SemaphoreType.DMA((N_SUM,)),
            pltpu.SemaphoreType.DMA((N_SUM,)),
            pltpu.SemaphoreType.DMA((4,)),
        ],
        compiler_params=pltpu.CompilerParams(
            collective_id=2, has_side_effects=True, vmem_limit_bytes=18 * MIB
        ),
        name="sum_grads",
    )(*pinned(dq, dk, dv, full), *args)


def leave(dst, s, scale, *terms):
    for n in range(LOCAL):
        total = terms[0][n].astype(F32)
        for term in terms[1:]:
            total = total + term[n].astype(F32)
        dst[n * BLK : (n + 1) * BLK, s * WIDE : (s + 1) * WIDE] = (total * scale).astype(BF16)


def leave_kernel(
    dq_ref, q_in, k_in, v_in, k_own, own_q, own_k, own_v, gq_out, gk_out, gv_out, gq_ref, gk_ref, gv_ref, sem
):
    halves = [Half(0), Half(1)]

    def mine(ref, s):
        return ref.at[pl.ds(s * LOCAL, LOCAL)]

    copies = []

    def hand_out(src, dst):
        copies.append(pltpu.make_async_copy(src, dst, sem.at[len(copies)]))
        copies[-1].start()

    for at in halves:
        queries = dq_ref.at[pl.ds(at.q_at * LOCAL, LOCAL)]
        leave(gq_ref, at.s, SCALE, mine(own_q, at.s), queries, q_in.at[at.s, 0], q_in.at[at.s, 1])
    hand_out(gq_ref, gq_out)
    for s in range(2):
        leave(gv_ref, s, 1.0, mine(own_v, s), k_own.at[s, 1], v_in.at[s, 0], v_in.at[s, 1])
    hand_out(gv_ref, gv_out)
    for s in range(2):
        leave(gk_ref, s, SCALE, mine(own_k, s), k_own.at[s, 0], k_in.at[s, 0], k_in.at[s, 1])
    hand_out(gk_ref, gk_out)
    for copy in copies:
        copy.wait()


def left(*sums):
    return pl.pallas_call(
        leave_kernel,
        out_shape=(pltpu.HBM((ROWS, COLS), BF16),) * 3,
        in_specs=[whole(VMEM)] * 8,
        out_specs=(whole(pltpu.HBM),) * 3,
        scratch_shapes=[VMEM((ROWS, COLS), BF16)] * 3 + [pltpu.SemaphoreType.DMA((3,))],
        compiler_params=pltpu.CompilerParams(vmem_limit_bytes=4 * MIB),
        name="leave",
    )(*pinned(*sums))


def per_device(query, key, value, out_grad, links):
    args = [pltpu.with_memory_space_constraint(v, pltpu.HBM) for v in (query, out_grad, key, value)]
    qg, kg, qt, entries, part, dq, dk, dv = gathered(*args, links.T)
    full = joined_stats(partial_stats(entries, qt, kg, part))
    dq, dk, dv = partial_grads(entries, qg, qt, kg, full, dq, dk, dv)
    return left(dq, *summed(dq, dk, dv, full, *args))


def solution(mesh):
    spec = P("ctx", "head")
    return jax.shard_map(
        per_device,
        mesh=mesh,
        in_specs=(spec, spec, spec, spec, P()),
        out_specs=(spec, spec, spec),
        check_vma=False,
    )
```
